128 devices in a mesh: segment: 8 (over z_hi, y), patch: 16 (over x, z_lo, core).
Axes of the slice: x: 4, y: 4, z: 4 (z_hi: 2, z_lo: 2; z = z_hi * 2 + z_lo), core: 2. Of those that a mesh axis runs over, the one named last changes fastest.
Arguments:
- features: bfloat16 [8, 2, 320, 64, 128], P('segment', None, None, 'patch'), may hold values from -48 to 48, as said below
- latent: float32 [2, 4, 64, 128], P(None, None, 'patch'), may hold values from -48 to 48
- plan_pos: int32 [2], replicated, may hold values from 0 to 9
- blocks_used: int32 [8], P('segment'), may hold values from 1 to 2, as said below
- conv1_w: bfloat16 [8, 2, 9, 320, 320], P('segment'), may hold values from -0.109375 to 0.109375
- conv2_w: bfloat16 [8, 2, 9, 320, 320], P('segment'), may hold values from -0.109375 to 0.109375
- norm_gain: float32 [8, 2, 2, 320], P('segment'), may hold values from 0.25 to 1.75
- norm_shift: float32 [8, 2, 2, 320], P('segment'), may hold values from -3 to 3
- in_w: bfloat16 [9, 320, 4], replicated, may hold values from -1 to 1
- head_w: bfloat16 [9, 4, 320], replicated, may hold values from -0.109375 to 0.109375
- head_gain: float32 [320], replicated, may hold values from 0.25 to 1.75
- head_shift: float32 [320], replicated, may hold values from -3 to 3
Outputs:
- latent_out: float32 [2, 4, 64, 128], P(None, None, 'patch', 'segment')
- features_out: bfloat16 [8, 2, 320, 64, 128], P('segment', None, None, 'patch')
The draws below stay inside these ranges and needn't reach their ends.
Inputs may be any that keep to these rules, and one draw needn't show every extreme that they name: `features`: every entry lies within the range; row magnitudes vary over the rows. `blocks_used`: each section holds 1 or 2 blocks; both counts occur.
All inputs are finite; a program needn't handle non-finite values.
Results may differ from the reference program's by a relative error of at most 0.0075.
Values may be sent and summed in bfloat16 or wider, within the bound.
A program may use at most 64 MiB of HBM per device.

```python
import jax
import jax.numpy as jnp
from jax import lax

C = 320
GROUPS = 32
LAT = 4
BLOCKS = 2
STEPS = 2
SCHED = 12
COLS = 128
MB = 2
SEGMENTS = 8
NR = 64


def ramp_field(key, lead_shape, chan_count):
    full_shape = lead_shape + (chan_count, NR, COLS)
    row_pos = jnp.arange(NR, dtype=jnp.float32) / max(NR - 1, 1)
    row_scale = 0.3 * jnp.exp(jnp.log(10.0) * row_pos)
    chan_scale = jnp.exp(jax.random.uniform(jax.random.fold_in(key, 1), lead_shape + (chan_count, 1, 1), minval=-0.69, maxval=0.69))
    col_scale = jnp.exp(jax.random.uniform(jax.random.fold_in(key, 2), (COLS,), minval=-0.69, maxval=0.69))
    base_draw = jnp.clip(jax.random.normal(jax.random.fold_in(key, 3), full_shape), -4.0, 4.0)
    return base_draw * chan_scale * row_scale[:, None] * col_scale


def draw_features(key, part):
    return ramp_field(key, (SEGMENTS, MB), C).astype(jnp.bfloat16)


def draw_latent(key, part):
    return ramp_field(key, (MB,), LAT).astype(jnp.float32)


def draw_blocks_used(key, part):
    counts_run = jax.random.randint(jax.random.fold_in(key, 11), (SEGMENTS,), 1, 3)
    first_pos = jax.random.randint(jax.random.fold_in(key, 12), (), 0, SEGMENTS)
    second_pos = (first_pos + 1 + jax.random.randint(jax.random.fold_in(key, 13), (), 0, SEGMENTS - 1)) % SEGMENTS
    counts_run = counts_run.at[first_pos].set(2)
    counts_run = counts_run.at[second_pos].set(1)
    return counts_run.astype(jnp.int32)


def levels(rng, dims, split, low, largest):
    level = 1.0
    for dim, blocks in split:
        draws = jax.random.uniform(jax.random.fold_in(jax.random.fold_in(rng, 6), dim), (blocks,), jnp.float32, low / len(split), largest / len(split))
        level = level * jnp.repeat(jnp.exp(draws), dims[dim] // blocks).reshape((-1,) + (1,) * (len(dims) - 1 - dim))
    return level


def normal_values(rng, dims, width, limit, split=(), kind=jnp.bfloat16):
    result = width * jax.random.normal(rng, dims, jnp.float32)
    if split:
        result = result * levels(rng, dims, split, -0.22, 0.18)
    return jnp.clip(result, -limit, limit).astype(kind)


def setup_inputs(seed: int = 0) -> dict:
    streams_of = jax.random.split(jax.random.key(seed), 13)
    return {
        "features": draw_features(jax.random.fold_in(streams_of[12], 71), 0),
        "latent": draw_latent(jax.random.fold_in(streams_of[12], 71), 0),
        "plan_pos": jax.random.randint(streams_of[2], (MB,), 0, SCHED - 2).astype(jnp.int32),
        "blocks_used": draw_blocks_used(jax.random.fold_in(streams_of[12], 71), 0),
        "conv1_w": normal_values(streams_of[4], (SEGMENTS, BLOCKS, 9, C, C), (9 * C) ** -0.5, 0.109375, ((0, 8),)),
        "conv2_w": normal_values(streams_of[5], (SEGMENTS, BLOCKS, 9, C, C), (9 * C) ** -0.5, 0.109375, ((0, 8),)),
        "norm_gain": jnp.clip(1.0 + 0.15 * jax.random.normal(streams_of[6], (SEGMENTS, BLOCKS, 2, C), jnp.float32), 0.25, 1.75),
        "norm_shift": normal_values(streams_of[7], (SEGMENTS, BLOCKS, 2, C), 0.5, 3.0, ((0, 8),), jnp.float32),
        "in_w": normal_values(streams_of[8], (9, C, LAT), (9 * LAT) ** -0.5, 1.0),
        "head_w": normal_values(streams_of[9], (9, LAT, C), (9 * C) ** -0.5, 0.109375),
        "head_gain": jnp.clip(1.0 + 0.15 * jax.random.normal(streams_of[10], (C,), jnp.float32), 0.25, 1.75),
        "head_shift": normal_values(streams_of[11], (C,), 0.5, 3.0, (), jnp.float32),
    }


epsilon = 1e-05
sigma_top = 3.0
sigma_low = 0.1
rho_power = 7.0

def sigma_at(position):
    fraction = position.astype(jnp.float32) / (SCHED - 1)
    top_root = sigma_top ** (1.0 / rho_power)
    low_root = sigma_low ** (1.0 / rho_power)
    return (top_root + fraction * (low_root - top_root)) ** rho_power

def group_norm_silu(values, gain, shift):
    batch_size, chan_count, height, col_count = values.shape
    grouped = values.reshape(batch_size, GROUPS, chan_count // GROUPS, height, col_count)
    center = lax.optimization_barrier(jnp.mean(grouped, axis=(2, 3, 4), keepdims=True))
    spread = lax.optimization_barrier(jnp.mean(jnp.square(grouped - center), axis=(2, 3, 4), keepdims=True))
    normed = ((grouped - center) / jnp.sqrt(spread + epsilon)).reshape(values.shape)
    normed = normed * gain[None, :, None, None] + shift[None, :, None, None]
    return jax.nn.silu(normed).astype(jnp.bfloat16)

def conv_same(inputs, kernel):
    padded = jnp.pad(inputs.astype(jnp.float32), ((0, 0), (0, 0), (1, 1), (1, 1)))
    kernel_wide = kernel.astype(jnp.float32)
    height, col_count = (inputs.shape[2], inputs.shape[3])
    accum = jnp.zeros((inputs.shape[0], kernel.shape[1], height, col_count), jnp.float32)
    for tap_no in range(9):
        row_off, col_off = (tap_no // 3, tap_no % 3)
        window = padded[:, :, row_off:row_off + height, col_off:col_off + col_count]
        accum = accum + jnp.einsum('oi,bihw->bohw', kernel_wide[tap_no], window)
    return accum

def resnet_unit(hidden, kern_one, kern_two, gain_pair, shift_pair):
    first_act = group_norm_silu(hidden.astype(jnp.float32), gain_pair[0], shift_pair[0])
    middle = conv_same(first_act, kern_one)
    second = group_norm_silu(middle, gain_pair[1], shift_pair[1])
    return (hidden.astype(jnp.float32) + conv_same(second, kern_two)).astype(jnp.bfloat16)

def reference(features, latent, plan_pos, blocks_used, conv1_w, conv2_w, norm_gain, norm_shift, in_w, head_w, head_gain, head_shift):
    for step_no in range(STEPS):
        head_input = group_norm_silu(features[SEGMENTS - 1].astype(jnp.float32), head_gain, head_shift)
        noise_pred = conv_same(head_input, head_w)
        position = (plan_pos + step_no).astype(jnp.int32)
        sigma_now = sigma_at(position)
        sigma_next = sigma_at(position + 1)
        latent = latent + (sigma_next - sigma_now)[:, None, None, None] * noise_pred
        scaled = (latent / jnp.sqrt(sigma_next * sigma_next + 1.0)[:, None, None, None]).astype(jnp.bfloat16)
        entry_rows = conv_same(scaled, in_w).astype(jnp.bfloat16)
        outputs = []
        for segment_no in range(SEGMENTS):
            source = entry_rows if segment_no == 0 else features[segment_no - 1]
            after_one = resnet_unit(source, conv1_w[segment_no, 0], conv2_w[segment_no, 0], norm_gain[segment_no, 0], norm_shift[segment_no, 0])
            after_two = resnet_unit(after_one, conv1_w[segment_no, 1], conv2_w[segment_no, 1], norm_gain[segment_no, 1], norm_shift[segment_no, 1])
            outputs.append(jnp.where(blocks_used[segment_no] >= 2, after_two, after_one))
        features = jnp.stack(outputs)
    return (latent, features)
```

```python
import jax
import jax.numpy as jnp
from jax import lax
from jax.sharding import PartitionSpec as P
from jax.experimental import pallas as pl
from jax.experimental.pallas import tpu as pltpu

GROUPS = 32
STEPS = 2
SCHED = 12


epsilon = 1e-05
sigma_top = 3.0
sigma_low = 0.1
rho_power = 7.0


def with_halo(block, sides, width):
    for axis, dim in sides:
        count = lax.axis_size(axis)
        forward = [(i, i + 1) for i in range(count - 1)]
        backward = [(target, source) for source, target in forward]
        low = lax.ppermute(
            lax.slice_in_dim(block, block.shape[dim] - width, None, axis=dim), axis, forward
        )
        high = lax.ppermute(lax.slice_in_dim(block, 0, width, axis=dim), axis, backward)
        block = jnp.concatenate([low, block, high], axis=dim)
    return block


def from_behind(shard, axis, by):
    devices = lax.axis_size(axis)
    pairs = [(i, i + by) for i in range(devices) if 0 <= i + by < devices]
    return lax.ppermute(shard, axis, pairs)


def broadcast(shard, axis, root):
    mine = lax.axis_index(axis) == root
    return lax.psum(jnp.where(mine, shard, jnp.zeros_like(shard)), axis)


def sigma_at(position):
    fraction = position.astype(jnp.float32) / (SCHED - 1)
    top_root = sigma_top ** (1.0 / rho_power)
    low_root = sigma_low ** (1.0 / rho_power)
    return (top_root + fraction * (low_root - top_root)) ** rho_power


def gather_kernel(peers, x_ref, o_ref, send_sem, recv_sem):
    me = lax.axis_index("patch")
    seg = lax.axis_index("segment")
    barrier = pltpu.get_barrier_semaphore()
    for dist in range(1, peers):
        pl.semaphore_signal(
            barrier,
            1,
            device_id=(seg, lax.rem(me + dist, peers)),
            device_id_type=pl.DeviceIdType.MESH,
        )
    pl.semaphore_wait(barrier, peers - 1)
    copies = []
    for dist in range(1, peers):
        copy = pltpu.make_async_remote_copy(
            src_ref=x_ref,
            dst_ref=o_ref.at[me],
            send_sem=send_sem.at[dist],
            recv_sem=recv_sem.at[dist],
            device_id=(seg, lax.rem(me + dist, peers)),
            device_id_type=pl.DeviceIdType.MESH,
        )
        copy.start()
        copies.append(copy)
    o_ref[me] = x_ref[...]
    for copy in copies:
        copy.wait()


def gather_patch(packed):
    peers = lax.axis_size("patch")
    return pl.pallas_call(
        lambda *refs: gather_kernel(peers, *refs),
        out_shape=jax.ShapeDtypeStruct((peers,) + packed.shape, packed.dtype),
        in_specs=[pl.BlockSpec(memory_space=pltpu.VMEM)],
        out_specs=pl.BlockSpec(memory_space=pltpu.VMEM),
        scratch_shapes=[pltpu.SemaphoreType.DMA((peers,)), pltpu.SemaphoreType.DMA((peers,))],
        compiler_params=pltpu.CompilerParams(collective_id=0, has_side_effects=True),
        name="gather_patch_stats",
    )(packed)


def group_moments(values):
    batch_size, chan_count, height, col_count = values.shape
    grouped = values.reshape(batch_size, GROUPS, chan_count // GROUPS, height, col_count)
    local_count = chan_count // GROUPS * height * col_count
    peers = lax.axis_size("patch")
    local_sum = jnp.sum(grouped, axis=(2, 3, 4))
    local_center = local_sum / local_count
    local_dev = jnp.sum(
        jnp.square(grouped - local_center[:, :, None, None, None]), axis=(2, 3, 4)
    )
    flat = jnp.concatenate([local_sum.reshape(-1), local_dev.reshape(-1)])
    width = 128 * ((flat.shape[0] + 127) // 128)
    packed = jnp.zeros((8, width), jnp.float32).at[0, : flat.shape[0]].set(flat)
    every = gather_patch(packed)[:, 0, :]
    half = batch_size * GROUPS
    sums = every[:, :half].reshape(peers, batch_size, GROUPS)
    devs = every[:, half : 2 * half].reshape(peers, batch_size, GROUPS)
    cell_count = local_count * peers
    center = jnp.sum(sums, axis=0) / cell_count
    between = jnp.sum(jnp.square(sums / local_count - center[None]), axis=0) * local_count
    spread = (jnp.sum(devs, axis=0) + between) / cell_count
    return (center, jnp.sqrt(spread + epsilon))


def norm_silu(values, moments, gain, shift):
    center, root_spread = moments
    batch_size, chan_count, height, col_count = values.shape
    grouped = values.reshape(batch_size, GROUPS, chan_count // GROUPS, height, col_count)
    normed = (
        (grouped - center[:, :, None, None, None]) / root_spread[:, :, None, None, None]
    ).reshape(values.shape)
    normed = normed * gain[None, :, None, None] + shift[None, :, None, None]
    return jax.nn.silu(normed)


def conv_valid(rows_in, kernel):
    padded = jnp.pad(rows_in, ((0, 0), (0, 0), (0, 0), (1, 1)))
    height = rows_in.shape[2] - 2
    col_count = rows_in.shape[3]
    accum = jnp.zeros((rows_in.shape[0], kernel.shape[1], height, col_count), jnp.float32)
    for tap_no in range(9):
        row_off, col_off = (tap_no // 3, tap_no % 3)
        window = padded[:, :, row_off : row_off + height, col_off : col_off + col_count]
        accum = accum + jnp.einsum(
            "oi,bihw->bohw", kernel[tap_no], window, preferred_element_type=jnp.float32
        )
    return accum


def with_rows(values):
    return with_halo(values, (("patch", 2),), 1)


def resnet_unit(hidden, kern_one, kern_two, gain_pair, shift_pair):
    hidden_wide = hidden.astype(jnp.float32)
    first_act = norm_silu(
        hidden_wide, group_moments(hidden_wide), gain_pair[0], shift_pair[0]
    ).astype(jnp.bfloat16)
    middle = conv_valid(with_rows(first_act), kern_one)
    second = norm_silu(middle, group_moments(middle), gain_pair[1], shift_pair[1]).astype(
        jnp.bfloat16
    )
    result = conv_valid(with_rows(second), kern_two)
    return (hidden_wide + result).astype(jnp.bfloat16)


def head_noise(source, head_w, head_gain, head_shift):
    source_wide = source.astype(jnp.float32)
    head_input = norm_silu(source_wide, group_moments(source_wide), head_gain, head_shift).astype(
        jnp.bfloat16
    )
    return conv_valid(with_rows(head_input), head_w)


def per_device(
    features,
    latent,
    plan_pos,
    blocks_used,
    conv1_w,
    conv2_w,
    norm_gain,
    norm_shift,
    in_w,
    head_w,
    head_gain,
    head_shift,
):
    segment_count = lax.axis_size("segment")
    segment_pos = lax.axis_index("segment")
    last = segment_count - 1
    current = features[0]
    for step_no in range(STEPS):
        arrived = from_behind(current, "segment", 1)
        noise_local = head_noise(current, head_w, head_gain, head_shift)
        position = plan_pos + step_no
        sigma_now = sigma_at(position)
        sigma_next = sigma_at(position + 1)
        latent = latent + (sigma_next - sigma_now)[:, None, None, None] * noise_local
        scaled = (latent / jnp.sqrt(sigma_next * sigma_next + 1.0)[:, None, None, None]).astype(
            jnp.bfloat16
        )
        scaled_first = lax.ppermute(scaled, "segment", [(last, 0)])
        entry_rows = conv_valid(with_rows(scaled_first), in_w).astype(jnp.bfloat16)
        source = jnp.where(segment_pos == 0, entry_rows, arrived)
        after_one = resnet_unit(
            source, conv1_w[0, 0], conv2_w[0, 0], norm_gain[0, 0], norm_shift[0, 0]
        )
        current = lax.cond(
            blocks_used[0] >= 2,
            lambda hidden: resnet_unit(
                hidden, conv1_w[0, 1], conv2_w[0, 1], norm_gain[0, 1], norm_shift[0, 1]
            ),
            lambda hidden: hidden,
            after_one,
        )
    col_share = latent.shape[3] // segment_count
    latent_part = lax.dynamic_slice_in_dim(latent, segment_pos * col_share, col_share, 3)
    for target in range(last):
        piece = lax.slice_in_dim(latent, target * col_share, (target + 1) * col_share, axis=3)
        moved = lax.ppermute(piece, "segment", [(last, target)])
        latent_part = jnp.where(segment_pos == target, moved, latent_part)
    return (latent_part, current[None])


def solution(mesh):
    placed = (
        P("segment", None, None, "patch", None),
        P(None, None, "patch", None),
        P(),
        P("segment"),
        P("segment", None, None, None, None),
        P("segment", None, None, None, None),
        P("segment", None, None, None),
        P("segment", None, None, None),
        P(),
        P(),
        P(),
        P(),
    )
    return jax.shard_map(
        per_device,
        mesh=mesh,
        in_specs=placed,
        out_specs=(P(None, None, "patch", "segment"), P("segment", None, None, "patch", None)),
        check_vma=False,
    )
```

```python
import jax
import jax.numpy as jnp
from jax import lax
from jax.sharding import PartitionSpec as P
from jax.experimental import pallas as pl
from jax.experimental.pallas import tpu as pltpu

GROUPS = 32
STEPS = 2
SCHED = 12


epsilon = 1e-05
sigma_top = 3.0
sigma_low = 0.1
rho_power = 7.0


def with_halo(block, sides, width):
    for axis, dim in sides:
        count = lax.axis_size(axis)
        forward = [(i, i + 1) for i in range(count - 1)]
        backward = [(target, source) for source, target in forward]
        low = lax.ppermute(
            lax.slice_in_dim(block, block.shape[dim] - width, None, axis=dim), axis, forward
        )
        high = lax.ppermute(lax.slice_in_dim(block, 0, width, axis=dim), axis, backward)
        block = jnp.concatenate([low, block, high], axis=dim)
    return block


def from_behind(shard, axis, by):
    devices = lax.axis_size(axis)
    pairs = [(i, i + by) for i in range(devices) if 0 <= i + by < devices]
    return lax.ppermute(shard, axis, pairs)


def broadcast(shard, axis, root):
    mine = lax.axis_index(axis) == root
    return lax.psum(jnp.where(mine, shard, jnp.zeros_like(shard)), axis)


def sigma_at(position):
    fraction = position.astype(jnp.float32) / (SCHED - 1)
    top_root = sigma_top ** (1.0 / rho_power)
    low_root = sigma_low ** (1.0 / rho_power)
    return (top_root + fraction * (low_root - top_root)) ** rho_power


def gather_kernel(peers, x_ref, o_ref, send_sem, recv_sem):
    me = lax.axis_index("patch")
    seg = lax.axis_index("segment")
    barrier = pltpu.get_barrier_semaphore()
    for dist in range(1, peers):
        pl.semaphore_signal(
            barrier,
            1,
            device_id=(seg, lax.rem(me + dist, peers)),
            device_id_type=pl.DeviceIdType.MESH,
        )
    pl.semaphore_wait(barrier, peers - 1)
    copies = []
    for dist in range(1, peers):
        copy = pltpu.make_async_remote_copy(
            src_ref=x_ref,
            dst_ref=o_ref.at[me],
            send_sem=send_sem.at[dist],
            recv_sem=recv_sem.at[dist],
            device_id=(seg, lax.rem(me + dist, peers)),
            device_id_type=pl.DeviceIdType.MESH,
        )
        copy.start()
        copies.append(copy)
    o_ref[me] = x_ref[...]
    for copy in copies:
        copy.wait()


def gather_patch(packed):
    peers = lax.axis_size("patch")
    return pl.pallas_call(
        lambda *refs: gather_kernel(peers, *refs),
        out_shape=jax.ShapeDtypeStruct((peers,) + packed.shape, packed.dtype),
        in_specs=[pl.BlockSpec(memory_space=pltpu.VMEM)],
        out_specs=pl.BlockSpec(memory_space=pltpu.VMEM),
        scratch_shapes=[pltpu.SemaphoreType.DMA((peers,)), pltpu.SemaphoreType.DMA((peers,))],
        compiler_params=pltpu.CompilerParams(collective_id=0, has_side_effects=True),
        name="gather_patch_stats",
    )(packed)


def group_moments(values):
    batch_size, height, chan_count, col_count = values.shape
    grouped = values.reshape(batch_size, height, GROUPS, chan_count // GROUPS, col_count)
    local_count = chan_count // GROUPS * height * col_count
    peers = lax.axis_size("patch")
    local_sum = jnp.sum(grouped, axis=(1, 3, 4))
    local_center = local_sum / local_count
    local_dev = jnp.sum(
        jnp.square(grouped - local_center[:, None, :, None, None]), axis=(1, 3, 4)
    )
    flat = jnp.concatenate([local_sum.reshape(-1), local_dev.reshape(-1)])
    width = 128 * ((flat.shape[0] + 127) // 128)
    packed = jnp.zeros((8, width), jnp.float32).at[0, : flat.shape[0]].set(flat)
    every = gather_patch(packed)[:, 0, :]
    half = batch_size * GROUPS
    sums = every[:, :half].reshape(peers, batch_size, GROUPS)
    devs = every[:, half : 2 * half].reshape(peers, batch_size, GROUPS)
    cell_count = local_count * peers
    center = jnp.sum(sums, axis=0) / cell_count
    between = jnp.sum(jnp.square(sums / local_count - center[None]), axis=0) * local_count
    spread = (jnp.sum(devs, axis=0) + between) / cell_count
    return (center, jnp.sqrt(spread + epsilon))


def norm_silu(values, moments, gain, shift):
    center, root_spread = moments
    batch_size, height, chan_count, col_count = values.shape
    grouped = values.reshape(batch_size, height, GROUPS, chan_count // GROUPS, col_count)
    normed = (
        (grouped - center[:, None, :, None, None]) / root_spread[:, None, :, None, None]
    ).reshape(values.shape)
    normed = normed * gain[None, None, :, None] + shift[None, None, :, None]
    return jax.nn.silu(normed)


def conv_kernel(x_ref, w_ref, o_ref):
    batch, rows = o_ref.shape[0], o_ref.shape[1]
    for b in range(batch):
        for r in range(rows):
            acc = None
            for tap in range(9):
                part = jnp.dot(
                    w_ref[tap], x_ref[tap % 3, b, r + tap // 3], preferred_element_type=jnp.float32
                )
                acc = part if acc is None else acc + part
            o_ref[b, r] = acc


def conv_wide(rows_in, kernel):
    batch, rows_halo, chans, cols = rows_in.shape
    padded = jnp.pad(rows_in, ((0, 0), (0, 0), (0, 0), (1, 1)))
    shifted = jnp.stack([padded[..., j : j + cols] for j in range(3)])
    flops = 2 * 9 * batch * (rows_halo - 2) * cols * chans * kernel.shape[1]
    return pl.pallas_call(
        conv_kernel,
        out_shape=jax.ShapeDtypeStruct((batch, rows_halo - 2, kernel.shape[1], cols), jnp.float32),
        in_specs=[pl.BlockSpec(memory_space=pltpu.VMEM)] * 2,
        out_specs=pl.BlockSpec(memory_space=pltpu.VMEM),
        cost_estimate=pl.CostEstimate(
            flops=flops,
            transcendentals=0,
            bytes_accessed=shifted.size * 2 + kernel.size * 2 + batch * (rows_halo - 2) * kernel.shape[1] * cols * 4,
        ),
        name="conv3x3_rows",
    )(shifted, kernel)


def conv_valid(rows_in, kernel):
    padded = jnp.pad(rows_in, ((0, 0), (0, 0), (0, 0), (1, 1)))
    height = rows_in.shape[1] - 2
    col_count = rows_in.shape[3]
    accum = jnp.zeros((rows_in.shape[0], height, kernel.shape[1], col_count), jnp.float32)
    for tap_no in range(9):
        row_off, col_off = (tap_no // 3, tap_no % 3)
        window = padded[:, row_off : row_off + height, :, col_off : col_off + col_count]
        accum = accum + jnp.einsum(
            "oi,bhiw->bhow", kernel[tap_no], window, preferred_element_type=jnp.float32
        )
    return accum


def with_rows(values):
    return with_halo(values, (("patch", 1),), 1)


def resnet_unit(hidden, kern_one, kern_two, gain_pair, shift_pair):
    hidden_wide = hidden.astype(jnp.float32)
    first_act = norm_silu(
        hidden_wide, group_moments(hidden_wide), gain_pair[0], shift_pair[0]
    ).astype(jnp.bfloat16)
    middle = conv_wide(with_rows(first_act), kern_one)
    second = norm_silu(middle, group_moments(middle), gain_pair[1], shift_pair[1]).astype(
        jnp.bfloat16
    )
    result = conv_wide(with_rows(second), kern_two)
    return (hidden_wide + result).astype(jnp.bfloat16)


def head_noise(source, head_w, head_gain, head_shift):
    source_wide = source.astype(jnp.float32)
    head_input = norm_silu(source_wide, group_moments(source_wide), head_gain, head_shift).astype(
        jnp.bfloat16
    )
    return jnp.transpose(conv_valid(with_rows(head_input), head_w), (0, 2, 1, 3))


def per_device(
    features,
    latent,
    plan_pos,
    blocks_used,
    conv1_w,
    conv2_w,
    norm_gain,
    norm_shift,
    in_w,
    head_w,
    head_gain,
    head_shift,
):
    segment_count = lax.axis_size("segment")
    segment_pos = lax.axis_index("segment")
    last = segment_count - 1
    current = jnp.transpose(features[0], (0, 2, 1, 3))
    for step_no in range(STEPS):
        arrived = from_behind(current, "segment", 1)
        noise_local = head_noise(current, head_w, head_gain, head_shift)
        position = plan_pos + step_no
        sigma_now = sigma_at(position)
        sigma_next = sigma_at(position + 1)
        latent = latent + (sigma_next - sigma_now)[:, None, None, None] * noise_local
        scaled = (latent / jnp.sqrt(sigma_next * sigma_next + 1.0)[:, None, None, None]).astype(
            jnp.bfloat16
        )
        scaled_first = lax.ppermute(scaled, "segment", [(last, 0)])
        entry_rows = conv_valid(
            with_rows(jnp.transpose(scaled_first, (0, 2, 1, 3))), in_w
        ).astype(jnp.bfloat16)
        source = jnp.where(segment_pos == 0, entry_rows, arrived)
        after_one = resnet_unit(
            source, conv1_w[0, 0], conv2_w[0, 0], norm_gain[0, 0], norm_shift[0, 0]
        )
        current = lax.cond(
            blocks_used[0] >= 2,
            lambda hidden: resnet_unit(
                hidden, conv1_w[0, 1], conv2_w[0, 1], norm_gain[0, 1], norm_shift[0, 1]
            ),
            lambda hidden: hidden,
            after_one,
        )
    col_share = latent.shape[3] // segment_count
    latent_part = lax.dynamic_slice_in_dim(latent, segment_pos * col_share, col_share, 3)
    for target in range(last):
        piece = lax.slice_in_dim(latent, target * col_share, (target + 1) * col_share, axis=3)
        moved = lax.ppermute(piece, "segment", [(last, target)])
        latent_part = jnp.where(segment_pos == target, moved, latent_part)
    return (latent_part, jnp.transpose(current, (0, 2, 1, 3))[None])


def solution(mesh):
    placed = (
        P("segment", None, None, "patch", None),
        P(None, None, "patch", None),
        P(),
        P("segment"),
        P("segment", None, None, None, None),
        P("segment", None, None, None, None),
        P("segment", None, None, None),
        P("segment", None, None, None),
        P(),
        P(),
        P(),
        P(),
    )
    return jax.shard_map(
        per_device,
        mesh=mesh,
        in_specs=placed,
        out_specs=(P(None, None, "patch", "segment"), P("segment", None, None, "patch", None)),
        check_vma=False,
    )
```

```python
import jax
import jax.numpy as jnp
from jax import lax
from jax.sharding import PartitionSpec as P
from jax.experimental import pallas as pl
from jax.experimental.pallas import tpu as pltpu

GROUPS = 32
STEPS = 2
SCHED = 12


epsilon = 1e-05
sigma_top = 3.0
sigma_low = 0.1
rho_power = 7.0


def with_halo(block, sides, width):
    for axis, dim in sides:
        count = lax.axis_size(axis)
        forward = [(i, i + 1) for i in range(count - 1)]
        backward = [(target, source) for source, target in forward]
        low = lax.ppermute(
            lax.slice_in_dim(block, block.shape[dim] - width, None, axis=dim), axis, forward
        )
        high = lax.ppermute(lax.slice_in_dim(block, 0, width, axis=dim), axis, backward)
        block = jnp.concatenate([low, block, high], axis=dim)
    return block


def from_behind(shard, axis, by):
    devices = lax.axis_size(axis)
    pairs = [(i, i + by) for i in range(devices) if 0 <= i + by < devices]
    return lax.ppermute(shard, axis, pairs)


def broadcast(shard, axis, root):
    mine = lax.axis_index(axis) == root
    return lax.psum(jnp.where(mine, shard, jnp.zeros_like(shard)), axis)


def sigma_at(position):
    fraction = position.astype(jnp.float32) / (SCHED - 1)
    top_root = sigma_top ** (1.0 / rho_power)
    low_root = sigma_low ** (1.0 / rho_power)
    return (top_root + fraction * (low_root - top_root)) ** rho_power


def exchange_kernel(
    peers, x_ref, top_ref, bot_ref, o_ref, lo_ref, hi_ref, send_sem, recv_sem, row_send, row_recv
):
    me = lax.axis_index("patch")
    seg = lax.axis_index("segment")
    mesh_ids = pl.DeviceIdType.MESH
    barrier = pltpu.get_barrier_semaphore()
    for dist in range(1, peers):
        pl.semaphore_signal(
            barrier, 1, device_id=(seg, lax.rem(me + dist, peers)), device_id_type=mesh_ids
        )
    pl.semaphore_wait(barrier, peers - 1)
    down = pltpu.make_async_remote_copy(
        src_ref=bot_ref,
        dst_ref=lo_ref,
        send_sem=row_send.at[0],
        recv_sem=row_recv.at[0],
        device_id=(seg, jnp.minimum(me + 1, peers - 1)),
        device_id_type=mesh_ids,
    )
    up = pltpu.make_async_remote_copy(
        src_ref=top_ref,
        dst_ref=hi_ref,
        send_sem=row_send.at[1],
        recv_sem=row_recv.at[1],
        device_id=(seg, jnp.maximum(me - 1, 0)),
        device_id_type=mesh_ids,
    )

    @pl.when(me < peers - 1)
    def _():
        down.start()

    @pl.when(me > 0)
    def _():
        up.start()

    copies = []
    for dist in range(1, peers):
        copy = pltpu.make_async_remote_copy(
            src_ref=x_ref,
            dst_ref=o_ref.at[me],
            send_sem=send_sem.at[dist],
            recv_sem=recv_sem.at[dist],
            device_id=(seg, lax.rem(me + dist, peers)),
            device_id_type=mesh_ids,
        )
        copy.start()
        copies.append(copy)
    o_ref[me] = x_ref[...]

    @pl.when(me == 0)
    def _():
        lo_ref[...] = jnp.zeros(lo_ref.shape, lo_ref.dtype)

    @pl.when(me == peers - 1)
    def _():
        hi_ref[...] = jnp.zeros(hi_ref.shape, hi_ref.dtype)

    for copy in copies:
        copy.wait()

    @pl.when(me < peers - 1)
    def _():
        down.wait_send()
        up.wait_recv()

    @pl.when(me > 0)
    def _():
        up.wait_send()
        down.wait_recv()


def exchange_patch(packed, top, bottom):
    peers = lax.axis_size("patch")
    vmem = pl.BlockSpec(memory_space=pltpu.VMEM)
    return pl.pallas_call(
        lambda *refs: exchange_kernel(peers, *refs),
        out_shape=(
            jax.ShapeDtypeStruct((peers,) + packed.shape, packed.dtype),
            jax.ShapeDtypeStruct(top.shape, top.dtype),
            jax.ShapeDtypeStruct(top.shape, top.dtype),
        ),
        in_specs=[vmem] * 3,
        out_specs=(vmem, vmem, vmem),
        scratch_shapes=[
            pltpu.SemaphoreType.DMA((peers,)),
            pltpu.SemaphoreType.DMA((peers,)),
            pltpu.SemaphoreType.DMA((2,)),
            pltpu.SemaphoreType.DMA((2,)),
        ],
        compiler_params=pltpu.CompilerParams(
            collective_id=0 if top.dtype == jnp.bfloat16 else 1, has_side_effects=True
        ),
        name="exchange_stats_rows",
    )(packed, top, bottom)


def group_moments(values, rows):
    batch_size, height, chan_count, col_count = values.shape
    grouped = values.reshape(batch_size, height, GROUPS, chan_count // GROUPS, col_count)
    local_count = chan_count // GROUPS * height * col_count
    peers = lax.axis_size("patch")
    local_sum = jnp.sum(grouped, axis=(1, 3, 4))
    local_center = local_sum / local_count
    local_dev = jnp.sum(
        jnp.square(grouped - local_center[:, None, :, None, None]), axis=(1, 3, 4)
    )
    flat = jnp.concatenate([local_sum.reshape(-1), local_dev.reshape(-1)])
    width = 128 * ((flat.shape[0] + 127) // 128)
    packed = jnp.zeros((8, width), jnp.float32).at[0, : flat.shape[0]].set(flat)
    every, low, high = exchange_patch(packed, rows[:, 0], rows[:, height - 1])
    every = every[:, 0, :]
    half = batch_size * GROUPS
    sums = every[:, :half].reshape(peers, batch_size, GROUPS)
    devs = every[:, half : 2 * half].reshape(peers, batch_size, GROUPS)
    cell_count = local_count * peers
    center = jnp.sum(sums, axis=0) / cell_count
    between = jnp.sum(jnp.square(sums / local_count - center[None]), axis=0) * local_count
    spread = (jnp.sum(devs, axis=0) + between) / cell_count
    return (center, jnp.sqrt(spread + epsilon)), low, high


def act_with_rows(values, rows, gain, shift):
    moments, low, high = group_moments(values, rows)
    full = jnp.concatenate(
        [low[:, None].astype(jnp.float32), values, high[:, None].astype(jnp.float32)], axis=1
    )
    act = norm_silu(full, moments, gain, shift)
    me = lax.axis_index("patch")
    row = lax.broadcasted_iota(jnp.int32, (1, full.shape[1], 1, 1), 1)
    pad = ((row == 0) & (me == 0)) | ((row == full.shape[1] - 1) & (me == lax.axis_size("patch") - 1))
    return jnp.where(pad, 0.0, act).astype(jnp.bfloat16)


def scatter_kernel(count, x_ref, o_ref, send_sem, recv_sem):
    seg = lax.axis_index("segment")
    me = lax.axis_index("patch")
    last = count - 1
    mesh_ids = pl.DeviceIdType.MESH
    barrier = pltpu.get_barrier_semaphore()

    @pl.when(seg == last)
    def _():
        for target in range(last):
            pl.semaphore_signal(barrier, 1, device_id=(target, me), device_id_type=mesh_ids)
        pl.semaphore_wait(barrier, last)
        copies = []
        for target in range(last):
            copy = pltpu.make_async_remote_copy(
                src_ref=x_ref.at[target],
                dst_ref=o_ref,
                send_sem=send_sem.at[target],
                recv_sem=recv_sem.at[0],
                device_id=(target, me),
                device_id_type=mesh_ids,
            )
            copy.start()
            copies.append(copy)
        o_ref[...] = x_ref[last]
        for copy in copies:
            copy.wait_send()

    @pl.when(seg != last)
    def _():
        pl.semaphore_signal(barrier, 1, device_id=(last, me), device_id_type=mesh_ids)
        pl.semaphore_wait(barrier, 1)
        pltpu.make_async_remote_copy(
            src_ref=x_ref.at[0],
            dst_ref=o_ref,
            send_sem=send_sem.at[0],
            recv_sem=recv_sem.at[0],
            device_id=(last, me),
            device_id_type=mesh_ids,
        ).wait_recv()


def scatter_from_last(pieces):
    count = lax.axis_size("segment")
    vmem = pl.BlockSpec(memory_space=pltpu.VMEM)
    return pl.pallas_call(
        lambda *refs: scatter_kernel(count, *refs),
        out_shape=jax.ShapeDtypeStruct(pieces.shape[1:], pieces.dtype),
        in_specs=[vmem],
        out_specs=vmem,
        scratch_shapes=[pltpu.SemaphoreType.DMA((count,)), pltpu.SemaphoreType.DMA((1,))],
        compiler_params=pltpu.CompilerParams(collective_id=2, has_side_effects=True),
        name="scatter_latent_columns",
    )(pieces)


def norm_silu(values, moments, gain, shift):
    center, root_spread = moments
    batch_size, height, chan_count, col_count = values.shape
    grouped = values.reshape(batch_size, height, GROUPS, chan_count // GROUPS, col_count)
    normed = (
        (grouped - center[:, None, :, None, None]) / root_spread[:, None, :, None, None]
    ).reshape(values.shape)
    normed = normed * gain[None, None, :, None] + shift[None, None, :, None]
    return jax.nn.silu(normed)


def conv_kernel(x_ref, w_ref, o_ref):
    batch, rows = o_ref.shape[0], o_ref.shape[1]
    for b in range(batch):
        for r in range(rows):
            acc = None
            for tap in range(9):
                part = jnp.dot(
                    w_ref[tap], x_ref[tap % 3, b, r + tap // 3], preferred_element_type=jnp.float32
                )
                acc = part if acc is None else acc + part
            o_ref[b, r] = acc


def conv_wide(rows_in, weights, block):
    batch, rows_halo, chans, cols = rows_in.shape
    outs = weights.shape[-2]
    padded = jnp.pad(rows_in, ((0, 0), (0, 0), (0, 0), (1, 1)))
    shifted = jnp.stack([padded[..., j : j + cols] for j in range(3)])
    flops = 2 * 9 * batch * (rows_halo - 2) * cols * chans * outs
    out_shape = (batch, rows_halo - 2, outs, cols)
    return pl.pallas_call(
        conv_kernel,
        grid=(1,),
        out_shape=jax.ShapeDtypeStruct(out_shape, jnp.float32),
        in_specs=[
            pl.BlockSpec(shifted.shape, lambda i: (0, 0, 0, 0, 0)),
            pl.BlockSpec((None, None) + weights.shape[2:], lambda i: (0, block, 0, 0, 0)),
        ],
        out_specs=pl.BlockSpec(out_shape, lambda i: (0, 0, 0, 0)),
        cost_estimate=pl.CostEstimate(
            flops=flops,
            transcendentals=0,
            bytes_accessed=shifted.size * 2 + 9 * chans * outs * 2 + batch * (rows_halo - 2) * outs * cols * 4,
        ),
        name="conv3x3_rows",
    )(shifted, weights)


def conv_valid(rows_in, kernel):
    padded = jnp.pad(rows_in, ((0, 0), (0, 0), (0, 0), (1, 1)))
    height = rows_in.shape[1] - 2
    col_count = rows_in.shape[3]
    accum = jnp.zeros((rows_in.shape[0], height, kernel.shape[1], col_count), jnp.float32)
    for tap_no in range(9):
        row_off, col_off = (tap_no // 3, tap_no % 3)
        window = padded[:, row_off : row_off + height, :, col_off : col_off + col_count]
        accum = accum + jnp.einsum(
            "oi,bhiw->bhow", kernel[tap_no], window, preferred_element_type=jnp.float32
        )
    return accum


def resnet_unit(hidden, conv1_w, conv2_w, block, gain_pair, shift_pair):
    hidden_wide = hidden.astype(jnp.float32)
    first_act = act_with_rows(hidden_wide, hidden, gain_pair[0], shift_pair[0])
    middle = conv_wide(first_act, conv1_w, block)
    second = act_with_rows(middle, middle, gain_pair[1], shift_pair[1])
    result = conv_wide(second, conv2_w, block)
    return (hidden_wide + result).astype(jnp.bfloat16)


def head_noise(source, head_w, head_gain, head_shift):
    head_input = act_with_rows(source.astype(jnp.float32), source, head_gain, head_shift)
    return jnp.transpose(conv_valid(head_input, head_w), (0, 2, 1, 3))


def with_rows(values):
    return with_halo(values, (("patch", 1),), 1)


def per_device(
    features,
    latent,
    plan_pos,
    blocks_used,
    conv1_w,
    conv2_w,
    norm_gain,
    norm_shift,
    in_w,
    head_w,
    head_gain,
    head_shift,
):
    segment_count = lax.axis_size("segment")
    segment_pos = lax.axis_index("segment")
    last = segment_count - 1
    current = jnp.transpose(features[0], (0, 2, 1, 3))
    for step_no in range(STEPS):
        arrived = from_behind(current, "segment", 1)
        noise_local = head_noise(current, head_w, head_gain, head_shift)
        position = plan_pos + step_no
        sigma_now = sigma_at(position)
        sigma_next = sigma_at(position + 1)
        latent = latent + (sigma_next - sigma_now)[:, None, None, None] * noise_local
        scaled = (latent / jnp.sqrt(sigma_next * sigma_next + 1.0)[:, None, None, None]).astype(
            jnp.bfloat16
        )
        scaled_first = lax.ppermute(scaled, "segment", [(last, 0)])
        entry_rows = conv_valid(
            with_rows(jnp.transpose(scaled_first, (0, 2, 1, 3))), in_w
        ).astype(jnp.bfloat16)
        source = jnp.where(segment_pos == 0, entry_rows, arrived)
        after_one = resnet_unit(source, conv1_w, conv2_w, 0, norm_gain[0, 0], norm_shift[0, 0])
        current = lax.cond(
            blocks_used[0] >= 2,
            lambda hidden: resnet_unit(
                hidden, conv1_w, conv2_w, 1, norm_gain[0, 1], norm_shift[0, 1]
            ),
            lambda hidden: hidden,
            after_one,
        )
    batch_size, lat_count, height, col_count = latent.shape
    col_share = col_count // segment_count
    latent, current = lax.optimization_barrier((latent, current))
    pieces = latent.reshape(batch_size, lat_count, height, segment_count, col_share)
    pieces = jnp.transpose(pieces, (3, 0, 1, 2, 4)).reshape(segment_count, -1, 128)
    latent_part = scatter_from_last(pieces).reshape(batch_size, lat_count, height, col_share)
    return (latent_part, jnp.transpose(current, (0, 2, 1, 3))[None])


def solution(mesh):
    placed = (
        P("segment", None, None, "patch", None),
        P(None, None, "patch", None),
        P(),
        P("segment"),
        P("segment", None, None, None, None),
        P("segment", None, None, None, None),
        P("segment", None, None, None),
        P("segment", None, None, None),
        P(),
        P(),
        P(),
        P(),
    )
    return jax.shard_map(
        per_device,
        mesh=mesh,
        in_specs=placed,
        out_specs=(P(None, None, "patch", "segment"), P("segment", None, None, "patch", None)),
        check_vma=False,
    )
```

```python
import jax
import jax.numpy as jnp
from jax import lax
from jax.sharding import PartitionSpec as P
from jax.experimental import pallas as pl
from jax.experimental.pallas import tpu as pltpu

GROUPS = 32
STEPS = 2
SCHED = 12


epsilon = 1e-05
sigma_top = 3.0
sigma_low = 0.1
rho_power = 7.0


def with_halo(block, sides, width):
    for axis, dim in sides:
        count = lax.axis_size(axis)
        forward = [(i, i + 1) for i in range(count - 1)]
        backward = [(target, source) for source, target in forward]
        low = lax.ppermute(
            lax.slice_in_dim(block, block.shape[dim] - width, None, axis=dim), axis, forward
        )
        high = lax.ppermute(lax.slice_in_dim(block, 0, width, axis=dim), axis, backward)
        block = jnp.concatenate([low, block, high], axis=dim)
    return block


def from_behind(shard, axis, by):
    devices = lax.axis_size(axis)
    pairs = [(i, i + by) for i in range(devices) if 0 <= i + by < devices]
    return lax.ppermute(shard, axis, pairs)


def broadcast(shard, axis, root):
    mine = lax.axis_index(axis) == root
    return lax.psum(jnp.where(mine, shard, jnp.zeros_like(shard)), axis)


def sigma_at(position):
    fraction = position.astype(jnp.float32) / (SCHED - 1)
    top_root = sigma_top ** (1.0 / rho_power)
    low_root = sigma_low ** (1.0 / rho_power)
    return (top_root + fraction * (low_root - top_root)) ** rho_power


def exchange_kernel(
    peers, x_ref, top_ref, bot_ref, o_ref, lo_ref, hi_ref, send_sem, recv_sem, row_send, row_recv
):
    me = lax.axis_index("patch")
    seg = lax.axis_index("segment")
    mesh_ids = pl.DeviceIdType.MESH
    barrier = pltpu.get_barrier_semaphore()
    for dist in range(1, peers):
        pl.semaphore_signal(
            barrier, 1, device_id=(seg, lax.rem(me + dist, peers)), device_id_type=mesh_ids
        )
    pl.semaphore_wait(barrier, peers - 1)
    down = pltpu.make_async_remote_copy(
        src_ref=bot_ref,
        dst_ref=lo_ref,
        send_sem=row_send.at[0],
        recv_sem=row_recv.at[0],
        device_id=(seg, jnp.minimum(me + 1, peers - 1)),
        device_id_type=mesh_ids,
    )
    up = pltpu.make_async_remote_copy(
        src_ref=top_ref,
        dst_ref=hi_ref,
        send_sem=row_send.at[1],
        recv_sem=row_recv.at[1],
        device_id=(seg, jnp.maximum(me - 1, 0)),
        device_id_type=mesh_ids,
    )

    @pl.when(me < peers - 1)
    def _():
        down.start()

    @pl.when(me > 0)
    def _():
        up.start()

    copies = []
    for dist in range(1, peers):
        copy = pltpu.make_async_remote_copy(
            src_ref=x_ref,
            dst_ref=o_ref.at[me],
            send_sem=send_sem.at[dist],
            recv_sem=recv_sem.at[dist],
            device_id=(seg, lax.rem(me + dist, peers)),
            device_id_type=mesh_ids,
        )
        copy.start()
        copies.append(copy)
    o_ref[me] = x_ref[...]

    @pl.when(me == 0)
    def _():
        lo_ref[...] = jnp.zeros(lo_ref.shape, lo_ref.dtype)

    @pl.when(me == peers - 1)
    def _():
        hi_ref[...] = jnp.zeros(hi_ref.shape, hi_ref.dtype)

    for copy in copies:
        copy.wait()

    @pl.when(me < peers - 1)
    def _():
        down.wait_send()
        up.wait_recv()

    @pl.when(me > 0)
    def _():
        up.wait_send()
        down.wait_recv()


def exchange_patch(packed, top, bottom):
    peers = lax.axis_size("patch")
    vmem = pl.BlockSpec(memory_space=pltpu.VMEM)
    return pl.pallas_call(
        lambda *refs: exchange_kernel(peers, *refs),
        out_shape=(
            jax.ShapeDtypeStruct((peers,) + packed.shape, packed.dtype),
            jax.ShapeDtypeStruct(top.shape, top.dtype),
            jax.ShapeDtypeStruct(top.shape, top.dtype),
        ),
        in_specs=[vmem] * 3,
        out_specs=(vmem, vmem, vmem),
        scratch_shapes=[
            pltpu.SemaphoreType.DMA((peers,)),
            pltpu.SemaphoreType.DMA((peers,)),
            pltpu.SemaphoreType.DMA((2,)),
            pltpu.SemaphoreType.DMA((2,)),
        ],
        compiler_params=pltpu.CompilerParams(
            collective_id=0 if top.dtype == jnp.bfloat16 else 1, has_side_effects=True
        ),
        name="exchange_stats_rows",
    )(packed, top, bottom)


def group_moments(values, rows):
    batch_size, height, chan_count, col_count = values.shape
    grouped = values.reshape(batch_size, height, GROUPS, chan_count // GROUPS, col_count)
    local_count = chan_count // GROUPS * height * col_count
    peers = lax.axis_size("patch")
    local_sum = jnp.sum(grouped, axis=(1, 3, 4))
    local_center = local_sum / local_count
    local_dev = jnp.sum(
        jnp.square(grouped - local_center[:, None, :, None, None]), axis=(1, 3, 4)
    )
    flat = jnp.concatenate([local_sum.reshape(-1), local_dev.reshape(-1)])
    width = 128 * ((flat.shape[0] + 127) // 128)
    packed = jnp.zeros((8, width), jnp.float32).at[0, : flat.shape[0]].set(flat)
    every, low, high = exchange_patch(packed, rows[:, 0], rows[:, height - 1])
    every = every[:, 0, :]
    half = batch_size * GROUPS
    sums = every[:, :half].reshape(peers, batch_size, GROUPS)
    devs = every[:, half : 2 * half].reshape(peers, batch_size, GROUPS)
    cell_count = local_count * peers
    center = jnp.sum(sums, axis=0) / cell_count
    between = jnp.sum(jnp.square(sums / local_count - center[None]), axis=0) * local_count
    spread = (jnp.sum(devs, axis=0) + between) / cell_count
    return (center, jnp.sqrt(spread + epsilon)), low, high


def act_with_rows(values, rows, gain, shift):
    moments, low, high = group_moments(values, rows)
    full = jnp.concatenate(
        [low[:, None].astype(jnp.float32), values, high[:, None].astype(jnp.float32)], axis=1
    )
    act = norm_silu(full, moments, gain, shift)
    me = lax.axis_index("patch")
    row = lax.broadcasted_iota(jnp.int32, (1, full.shape[1], 1, 1), 1)
    pad = ((row == 0) & (me == 0)) | ((row == full.shape[1] - 1) & (me == lax.axis_size("patch") - 1))
    return jnp.where(pad, 0.0, act).astype(jnp.bfloat16)


def scatter_kernel(count, x_ref, o_ref, send_sem, recv_sem):
    seg = lax.axis_index("segment")
    me = lax.axis_index("patch")
    last = count - 1
    mesh_ids = pl.DeviceIdType.MESH
    barrier = pltpu.get_barrier_semaphore()

    @pl.when(seg == last)
    def _():
        for target in range(last):
            pl.semaphore_signal(barrier, 1, device_id=(target, me), device_id_type=mesh_ids)
        pl.semaphore_wait(barrier, last)
        copies = []
        for target in range(last):
            copy = pltpu.make_async_remote_copy(
                src_ref=x_ref.at[target],
                dst_ref=o_ref,
                send_sem=send_sem.at[target],
                recv_sem=recv_sem.at[0],
                device_id=(target, me),
                device_id_type=mesh_ids,
            )
            copy.start()
            copies.append(copy)
        o_ref[...] = x_ref[last]
        for copy in copies:
            copy.wait_send()

    @pl.when(seg != last)
    def _():
        pl.semaphore_signal(barrier, 1, device_id=(last, me), device_id_type=mesh_ids)
        pl.semaphore_wait(barrier, 1)
        pltpu.make_async_remote_copy(
            src_ref=x_ref.at[0],
            dst_ref=o_ref,
            send_sem=send_sem.at[0],
            recv_sem=recv_sem.at[0],
            device_id=(last, me),
            device_id_type=mesh_ids,
        ).wait_recv()


def scatter_from_last(pieces):
    count = lax.axis_size("segment")
    vmem = pl.BlockSpec(memory_space=pltpu.VMEM)
    return pl.pallas_call(
        lambda *refs: scatter_kernel(count, *refs),
        out_shape=jax.ShapeDtypeStruct(pieces.shape[1:], pieces.dtype),
        in_specs=[vmem],
        out_specs=vmem,
        scratch_shapes=[pltpu.SemaphoreType.DMA((count,)), pltpu.SemaphoreType.DMA((1,))],
        compiler_params=pltpu.CompilerParams(collective_id=2, has_side_effects=True),
        name="scatter_latent_columns",
    )(pieces)


def norm_silu(values, moments, gain, shift):
    center, root_spread = moments
    batch_size, height, chan_count, col_count = values.shape
    grouped = values.reshape(batch_size, height, GROUPS, chan_count // GROUPS, col_count)
    normed = (
        (grouped - center[:, None, :, None, None]) / root_spread[:, None, :, None, None]
    ).reshape(values.shape)
    normed = normed * gain[None, None, :, None] + shift[None, None, :, None]
    return jax.nn.silu(normed)


def conv_kernel(x_ref, w_ref, o_ref):
    rows, chans, cols = o_ref.shape
    for r in range(rows):
        window = x_ref[r : r + 3].reshape(9 * x_ref.shape[2], cols)
        o_ref[r] = jnp.dot(w_ref[...], window, preferred_element_type=jnp.float32)


def flat_taps(weights):
    return jnp.transpose(weights[0], (0, 2, 1, 3)).reshape(
        weights.shape[1], weights.shape[3], 9 * weights.shape[4]
    )


def conv_wide(rows_in, weights, block):
    batch, rows_halo, chans, cols = rows_in.shape
    outs = weights.shape[1]
    padded = jnp.pad(rows_in, ((0, 0), (0, 0), (0, 0), (1, 1)))
    shifted = jnp.stack([padded[..., j : j + cols] for j in range(3)], axis=2)
    flops = 2 * 9 * batch * (rows_halo - 2) * cols * chans * outs
    return pl.pallas_call(
        conv_kernel,
        grid=(batch,),
        out_shape=jax.ShapeDtypeStruct((batch, rows_halo - 2, outs, cols), jnp.float32),
        in_specs=[
            pl.BlockSpec((None,) + shifted.shape[1:], lambda b: (b, 0, 0, 0, 0)),
            pl.BlockSpec((None,) + weights.shape[1:], lambda b: (block, 0, 0)),
        ],
        out_specs=pl.BlockSpec((None, rows_halo - 2, outs, cols), lambda b: (b, 0, 0, 0)),
        cost_estimate=pl.CostEstimate(
            flops=flops,
            transcendentals=0,
            bytes_accessed=shifted.size * 2 + 9 * chans * outs * 2 + batch * (rows_halo - 2) * outs * cols * 4,
        ),
        name="conv3x3_rows",
    )(shifted, weights)


def conv_valid(rows_in, kernel):
    padded = jnp.pad(rows_in, ((0, 0), (0, 0), (0, 0), (1, 1)))
    height = rows_in.shape[1] - 2
    col_count = rows_in.shape[3]
    accum = jnp.zeros((rows_in.shape[0], height, kernel.shape[1], col_count), jnp.float32)
    for tap_no in range(9):
        row_off, col_off = (tap_no // 3, tap_no % 3)
        window = padded[:, row_off : row_off + height, :, col_off : col_off + col_count]
        accum = accum + jnp.einsum(
            "oi,bhiw->bhow", kernel[tap_no], window, preferred_element_type=jnp.float32
        )
    return accum


def resnet_unit(hidden, conv1_w, conv2_w, block, gain_pair, shift_pair):
    hidden_wide = hidden.astype(jnp.float32)
    first_act = act_with_rows(hidden_wide, hidden, gain_pair[0], shift_pair[0])
    middle = conv_wide(first_act, conv1_w, block)
    second = act_with_rows(middle, middle, gain_pair[1], shift_pair[1])
    result = conv_wide(second, conv2_w, block)
    return (hidden_wide + result).astype(jnp.bfloat16)


def head_noise(source, head_w, head_gain, head_shift):
    head_input = act_with_rows(source.astype(jnp.float32), source, head_gain, head_shift)
    return jnp.transpose(conv_valid(head_input, head_w), (0, 2, 1, 3))


def with_rows(values):
    return with_halo(values, (("patch", 1),), 1)


def per_device(
    features,
    latent,
    plan_pos,
    blocks_used,
    conv1_w,
    conv2_w,
    norm_gain,
    norm_shift,
    in_w,
    head_w,
    head_gain,
    head_shift,
):
    segment_count = lax.axis_size("segment")
    segment_pos = lax.axis_index("segment")
    last = segment_count - 1
    current = jnp.transpose(features[0], (0, 2, 1, 3))
    conv1_w = flat_taps(conv1_w)
    conv2_w = flat_taps(conv2_w)
    for step_no in range(STEPS):
        arrived = from_behind(current, "segment", 1)
        noise_local = head_noise(current, head_w, head_gain, head_shift)
        position = plan_pos + step_no
        sigma_now = sigma_at(position)
        sigma_next = sigma_at(position + 1)
        latent = latent + (sigma_next - sigma_now)[:, None, None, None] * noise_local
        scaled = (latent / jnp.sqrt(sigma_next * sigma_next + 1.0)[:, None, None, None]).astype(
            jnp.bfloat16
        )
        scaled_first = lax.ppermute(scaled, "segment", [(last, 0)])
        entry_rows = conv_valid(
            with_rows(jnp.transpose(scaled_first, (0, 2, 1, 3))), in_w
        ).astype(jnp.bfloat16)
        source = jnp.where(segment_pos == 0, entry_rows, arrived)
        after_one = resnet_unit(source, conv1_w, conv2_w, 0, norm_gain[0, 0], norm_shift[0, 0])
        current = lax.cond(
            blocks_used[0] >= 2,
            lambda hidden: resnet_unit(
                hidden, conv1_w, conv2_w, 1, norm_gain[0, 1], norm_shift[0, 1]
            ),
            lambda hidden: hidden,
            after_one,
        )
    batch_size, lat_count, height, col_count = latent.shape
    col_share = col_count // segment_count
    latent, current = lax.optimization_barrier((latent, current))
    pieces = latent.reshape(batch_size, lat_count, height, segment_count, col_share)
    pieces = jnp.transpose(pieces, (3, 0, 1, 2, 4)).reshape(segment_count, -1, 128)
    latent_part = scatter_from_last(pieces).reshape(batch_size, lat_count, height, col_share)
    return (latent_part, jnp.transpose(current, (0, 2, 1, 3))[None])


def solution(mesh):
    placed = (
        P("segment", None, None, "patch", None),
        P(None, None, "patch", None),
        P(),
        P("segment"),
        P("segment", None, None, None, None),
        P("segment", None, None, None, None),
        P("segment", None, None, None),
        P("segment", None, None, None),
        P(),
        P(),
        P(),
        P(),
    )
    return jax.shard_map(
        per_device,
        mesh=mesh,
        in_specs=placed,
        out_specs=(P(None, None, "patch", "segment"), P("segment", None, None, "patch", None)),
        check_vma=False,
    )
```

```python
import jax
import jax.numpy as jnp
from jax import lax
from jax.sharding import PartitionSpec as P
from jax.experimental import pallas as pl
from jax.experimental.pallas import tpu as pltpu

GROUPS = 32
STEPS = 2
SCHED = 12


epsilon = 1e-05
sigma_top = 3.0
sigma_low = 0.1
rho_power = 7.0


def with_halo(block, sides, width):
    for axis, dim in sides:
        count = lax.axis_size(axis)
        forward = [(i, i + 1) for i in range(count - 1)]
        backward = [(target, source) for source, target in forward]
        low = lax.ppermute(
            lax.slice_in_dim(block, block.shape[dim] - width, None, axis=dim), axis, forward
        )
        high = lax.ppermute(lax.slice_in_dim(block, 0, width, axis=dim), axis, backward)
        block = jnp.concatenate([low, block, high], axis=dim)
    return block


def from_behind(shard, axis, by):
    devices = lax.axis_size(axis)
    pairs = [(i, i + by) for i in range(devices) if 0 <= i + by < devices]
    return lax.ppermute(shard, axis, pairs)


def broadcast(shard, axis, root):
    mine = lax.axis_index(axis) == root
    return lax.psum(jnp.where(mine, shard, jnp.zeros_like(shard)), axis)


def sigma_at(position):
    fraction = position.astype(jnp.float32) / (SCHED - 1)
    top_root = sigma_top ** (1.0 / rho_power)
    low_root = sigma_low ** (1.0 / rho_power)
    return (top_root + fraction * (low_root - top_root)) ** rho_power


def exchange_kernel(
    peers, x_ref, top_ref, bot_ref, o_ref, lo_ref, hi_ref, quad_sem, cross_sem, own_sem, row_send, row_recv
):
    me = lax.axis_index("patch")
    seg = lax.axis_index("segment")
    mesh_ids = pl.DeviceIdType.MESH
    quad = 4
    groups = peers // quad
    pos = me % quad
    group = me // quad
    first_in_group = (pos == 0) & (group > 0)
    last_in_group = (pos == quad - 1) & (group < groups - 1)
    quad_peers = [group * quad + (pos + d) % quad for d in range(1, quad)]
    cross_peers = [((group + d) % groups) * quad + pos for d in range(1, groups)]
    barrier = pltpu.get_barrier_semaphore()
    for peer in quad_peers + cross_peers:
        pl.semaphore_signal(barrier, 1, device_id=(seg, peer), device_id_type=mesh_ids)

    @pl.when(first_in_group)
    def _():
        pl.semaphore_signal(barrier, 1, device_id=(seg, me - 1), device_id_type=mesh_ids)

    @pl.when(last_in_group)
    def _():
        pl.semaphore_signal(barrier, 1, device_id=(seg, me + 1), device_id_type=mesh_ids)

    greeted = len(quad_peers) + len(cross_peers)

    @pl.when(first_in_group | last_in_group)
    def _():
        pl.semaphore_wait(barrier, greeted + 1)

    @pl.when(jnp.logical_not(first_in_group | last_in_group))
    def _():
        pl.semaphore_wait(barrier, greeted)

    down = pltpu.make_async_remote_copy(
        src_ref=bot_ref,
        dst_ref=lo_ref,
        send_sem=row_send.at[0],
        recv_sem=row_recv.at[0],
        device_id=(seg, jnp.minimum(me + 1, peers - 1)),
        device_id_type=mesh_ids,
    )
    up = pltpu.make_async_remote_copy(
        src_ref=top_ref,
        dst_ref=hi_ref,
        send_sem=row_send.at[1],
        recv_sem=row_recv.at[1],
        device_id=(seg, jnp.maximum(me - 1, 0)),
        device_id_type=mesh_ids,
    )

    @pl.when(me < peers - 1)
    def _():
        down.start()

    @pl.when(me > 0)
    def _():
        up.start()

    own = pltpu.make_async_copy(x_ref, o_ref.at[me], own_sem.at[0])
    own.start()
    near = []
    for d, peer in enumerate(quad_peers):
        copy = pltpu.make_async_remote_copy(
            src_ref=x_ref,
            dst_ref=o_ref.at[me],
            send_sem=quad_sem.at[0, d],
            recv_sem=quad_sem.at[1, d],
            device_id=(seg, peer),
            device_id_type=mesh_ids,
        )
        copy.start()
        near.append(copy)

    @pl.when(me == 0)
    def _():
        lo_ref[...] = jnp.zeros(lo_ref.shape, lo_ref.dtype)

    @pl.when(me == peers - 1)
    def _():
        hi_ref[...] = jnp.zeros(hi_ref.shape, hi_ref.dtype)

    own.wait()
    for copy in near:
        copy.wait()
    block = o_ref.at[pl.ds(group * quad, quad)]
    far = []
    for d, peer in enumerate(cross_peers):
        copy = pltpu.make_async_remote_copy(
            src_ref=block,
            dst_ref=block,
            send_sem=cross_sem.at[0, d],
            recv_sem=cross_sem.at[1, d],
            device_id=(seg, peer),
            device_id_type=mesh_ids,
        )
        copy.start()
        far.append(copy)
    for copy in far:
        copy.wait()

    @pl.when(me < peers - 1)
    def _():
        down.wait_send()
        up.wait_recv()

    @pl.when(me > 0)
    def _():
        up.wait_send()
        down.wait_recv()


def exchange_patch(packed, top, bottom):
    peers = lax.axis_size("patch")
    vmem = pl.BlockSpec(memory_space=pltpu.VMEM)
    return pl.pallas_call(
        lambda *refs: exchange_kernel(peers, *refs),
        out_shape=(
            jax.ShapeDtypeStruct((peers,) + packed.shape, packed.dtype),
            jax.ShapeDtypeStruct(top.shape, top.dtype),
            jax.ShapeDtypeStruct(top.shape, top.dtype),
        ),
        in_specs=[vmem] * 3,
        out_specs=(vmem, vmem, vmem),
        scratch_shapes=[
            pltpu.SemaphoreType.DMA((2, 3)),
            pltpu.SemaphoreType.DMA((2, peers // 4 - 1)),
            pltpu.SemaphoreType.DMA((1,)),
            pltpu.SemaphoreType.DMA((2,)),
            pltpu.SemaphoreType.DMA((2,)),
        ],
        compiler_params=pltpu.CompilerParams(
            collective_id=0 if top.dtype == jnp.bfloat16 else 1, has_side_effects=True
        ),
        name="exchange_stats_rows",
    )(packed, top, bottom)


def group_moments(values, rows):
    batch_size, height, chan_count, col_count = values.shape
    grouped = values.reshape(batch_size, height, GROUPS, chan_count // GROUPS, col_count)
    local_count = chan_count // GROUPS * height * col_count
    peers = lax.axis_size("patch")
    local_sum = jnp.sum(grouped, axis=(1, 3, 4))
    local_center = local_sum / local_count
    local_dev = jnp.sum(
        jnp.square(grouped - local_center[:, None, :, None, None]), axis=(1, 3, 4)
    )
    flat = jnp.concatenate([local_sum.reshape(-1), local_dev.reshape(-1)])
    width = 128 * ((flat.shape[0] + 127) // 128)
    packed = jnp.zeros((8, width), jnp.float32).at[0, : flat.shape[0]].set(flat)
    every, low, high = exchange_patch(packed, rows[:, 0], rows[:, height - 1])
    every = every[:, 0, :]
    half = batch_size * GROUPS
    sums = every[:, :half].reshape(peers, batch_size, GROUPS)
    devs = every[:, half : 2 * half].reshape(peers, batch_size, GROUPS)
    cell_count = local_count * peers
    center = jnp.sum(sums, axis=0) / cell_count
    between = jnp.sum(jnp.square(sums / local_count - center[None]), axis=0) * local_count
    spread = (jnp.sum(devs, axis=0) + between) / cell_count
    return (center, jnp.sqrt(spread + epsilon)), low, high


def act_with_rows(values, rows, gain, shift):
    moments, low, high = group_moments(values, rows)
    full = jnp.concatenate(
        [low[:, None].astype(jnp.float32), values, high[:, None].astype(jnp.float32)], axis=1
    )
    act = norm_silu(full, moments, gain, shift)
    me = lax.axis_index("patch")
    row = lax.broadcasted_iota(jnp.int32, (1, full.shape[1], 1, 1), 1)
    pad = ((row == 0) & (me == 0)) | ((row == full.shape[1] - 1) & (me == lax.axis_size("patch") - 1))
    return jnp.where(pad, 0.0, act).astype(jnp.bfloat16)


def scatter_kernel(count, x_ref, o_ref, send_sem, recv_sem):
    seg = lax.axis_index("segment")
    me = lax.axis_index("patch")
    last = count - 1
    mesh_ids = pl.DeviceIdType.MESH
    barrier = pltpu.get_barrier_semaphore()

    @pl.when(seg == last)
    def _():
        for target in range(last):
            pl.semaphore_signal(barrier, 1, device_id=(target, me), device_id_type=mesh_ids)
        pl.semaphore_wait(barrier, last)
        copies = []
        for target in range(last):
            copy = pltpu.make_async_remote_copy(
                src_ref=x_ref.at[target],
                dst_ref=o_ref,
                send_sem=send_sem.at[target],
                recv_sem=recv_sem.at[0],
                device_id=(target, me),
                device_id_type=mesh_ids,
            )
            copy.start()
            copies.append(copy)
        o_ref[...] = x_ref[last]
        for copy in copies:
            copy.wait_send()

    @pl.when(seg != last)
    def _():
        pl.semaphore_signal(barrier, 1, device_id=(last, me), device_id_type=mesh_ids)
        pl.semaphore_wait(barrier, 1)
        pltpu.make_async_remote_copy(
            src_ref=x_ref.at[0],
            dst_ref=o_ref,
            send_sem=send_sem.at[0],
            recv_sem=recv_sem.at[0],
            device_id=(last, me),
            device_id_type=mesh_ids,
        ).wait_recv()


def scatter_from_last(pieces):
    count = lax.axis_size("segment")
    vmem = pl.BlockSpec(memory_space=pltpu.VMEM)
    return pl.pallas_call(
        lambda *refs: scatter_kernel(count, *refs),
        out_shape=jax.ShapeDtypeStruct(pieces.shape[1:], pieces.dtype),
        in_specs=[vmem],
        out_specs=vmem,
        scratch_shapes=[pltpu.SemaphoreType.DMA((count,)), pltpu.SemaphoreType.DMA((1,))],
        compiler_params=pltpu.CompilerParams(collective_id=2, has_side_effects=True),
        name="scatter_latent_columns",
    )(pieces)


def norm_silu(values, moments, gain, shift):
    center, root_spread = moments
    batch_size, height, chan_count, col_count = values.shape
    grouped = values.reshape(batch_size, height, GROUPS, chan_count // GROUPS, col_count)
    normed = (
        (grouped - center[:, None, :, None, None]) / root_spread[:, None, :, None, None]
    ).reshape(values.shape)
    normed = normed * gain[None, None, :, None] + shift[None, None, :, None]
    return jax.nn.silu(normed)


def conv_kernel(x_ref, w_ref, o_ref):
    batch, rows = o_ref.shape[0], o_ref.shape[1]
    for b in range(batch):
        for r in range(rows):
            acc = None
            for tap in range(9):
                part = jnp.dot(
                    w_ref[tap], x_ref[tap % 3, b, r + tap // 3], preferred_element_type=jnp.float32
                )
                acc = part if acc is None else acc + part
            o_ref[b, r] = acc


def conv_wide(rows_in, weights, block):
    batch, rows_halo, chans, cols = rows_in.shape
    outs = weights.shape[-2]
    padded = jnp.pad(rows_in, ((0, 0), (0, 0), (0, 0), (1, 1)))
    shifted = jnp.stack([padded[..., j : j + cols] for j in range(3)])
    flops = 2 * 9 * batch * (rows_halo - 2) * cols * chans * outs
    out_shape = (batch, rows_halo - 2, outs, cols)
    return pl.pallas_call(
        conv_kernel,
        grid=(1,),
        out_shape=jax.ShapeDtypeStruct(out_shape, jnp.float32),
        in_specs=[
            pl.BlockSpec(shifted.shape, lambda i: (0, 0, 0, 0, 0)),
            pl.BlockSpec((None, None) + weights.shape[2:], lambda i: (0, block, 0, 0, 0)),
        ],
        out_specs=pl.BlockSpec(out_shape, lambda i: (0, 0, 0, 0)),
        cost_estimate=pl.CostEstimate(
            flops=flops,
            transcendentals=0,
            bytes_accessed=shifted.size * 2 + 9 * chans * outs * 2 + batch * (rows_halo - 2) * outs * cols * 4,
        ),
        name="conv3x3_rows",
    )(shifted, weights)


def conv_valid(rows_in, kernel):
    padded = jnp.pad(rows_in, ((0, 0), (0, 0), (0, 0), (1, 1)))
    height = rows_in.shape[1] - 2
    col_count = rows_in.shape[3]
    accum = jnp.zeros((rows_in.shape[0], height, kernel.shape[1], col_count), jnp.float32)
    for tap_no in range(9):
        row_off, col_off = (tap_no // 3, tap_no % 3)
        window = padded[:, row_off : row_off + height, :, col_off : col_off + col_count]
        accum = accum + jnp.einsum(
            "oi,bhiw->bhow", kernel[tap_no], window, preferred_element_type=jnp.float32
        )
    return accum


def resnet_unit(hidden, conv1_w, conv2_w, block, gain_pair, shift_pair):
    hidden_wide = hidden.astype(jnp.float32)
    first_act = act_with_rows(hidden_wide, hidden, gain_pair[0], shift_pair[0])
    middle = conv_wide(first_act, conv1_w, block)
    second = act_with_rows(middle, middle, gain_pair[1], shift_pair[1])
    result = conv_wide(second, conv2_w, block)
    return (hidden_wide + result).astype(jnp.bfloat16)


def head_noise(source, head_w, head_gain, head_shift):
    head_input = act_with_rows(source.astype(jnp.float32), source, head_gain, head_shift)
    return jnp.transpose(conv_valid(head_input, head_w), (0, 2, 1, 3))


def with_rows(values):
    return with_halo(values, (("patch", 1),), 1)


def per_device(
    features,
    latent,
    plan_pos,
    blocks_used,
    conv1_w,
    conv2_w,
    norm_gain,
    norm_shift,
    in_w,
    head_w,
    head_gain,
    head_shift,
):
    segment_count = lax.axis_size("segment")
    segment_pos = lax.axis_index("segment")
    last = segment_count - 1
    current = jnp.transpose(features[0], (0, 2, 1, 3))
    for step_no in range(STEPS):
        arrived = from_behind(current, "segment", 1)
        noise_local = head_noise(current, head_w, head_gain, head_shift)
        position = plan_pos + step_no
        sigma_now = sigma_at(position)
        sigma_next = sigma_at(position + 1)
        latent = latent + (sigma_next - sigma_now)[:, None, None, None] * noise_local
        scaled = (latent / jnp.sqrt(sigma_next * sigma_next + 1.0)[:, None, None, None]).astype(
            jnp.bfloat16
        )
        scaled_first = lax.ppermute(scaled, "segment", [(last, 0)])
        entry_rows = conv_valid(
            with_rows(jnp.transpose(scaled_first, (0, 2, 1, 3))), in_w
        ).astype(jnp.bfloat16)
        source = jnp.where(segment_pos == 0, entry_rows, arrived)
        after_one = resnet_unit(source, conv1_w, conv2_w, 0, norm_gain[0, 0], norm_shift[0, 0])
        current = lax.cond(
            blocks_used[0] >= 2,
            lambda hidden: resnet_unit(
                hidden, conv1_w, conv2_w, 1, norm_gain[0, 1], norm_shift[0, 1]
            ),
            lambda hidden: hidden,
            after_one,
        )
    batch_size, lat_count, height, col_count = latent.shape
    col_share = col_count // segment_count
    latent, current = lax.optimization_barrier((latent, current))
    pieces = latent.reshape(batch_size, lat_count, height, segment_count, col_share)
    pieces = jnp.transpose(pieces, (3, 0, 1, 2, 4)).reshape(segment_count, -1, 128)
    latent_part = scatter_from_last(pieces).reshape(batch_size, lat_count, height, col_share)
    return (latent_part, jnp.transpose(current, (0, 2, 1, 3))[None])


def solution(mesh):
    placed = (
        P("segment", None, None, "patch", None),
        P(None, None, "patch", None),
        P(),
        P("segment"),
        P("segment", None, None, None, None),
        P("segment", None, None, None, None),
        P("segment", None, None, None),
        P("segment", None, None, None),
        P(),
        P(),
        P(),
        P(),
    )
    return jax.shard_map(
        per_device,
        mesh=mesh,
        in_specs=placed,
        out_specs=(P(None, None, "patch", "segment"), P("segment", None, None, "patch", None)),
        check_vma=False,
    )
```

```python
import jax
import jax.numpy as jnp
from jax import lax
from jax.sharding import PartitionSpec as P
from jax.experimental import pallas as pl
from jax.experimental.pallas import tpu as pltpu

GROUPS = 32
STEPS = 2
SCHED = 12


epsilon = 1e-05
sigma_top = 3.0
sigma_low = 0.1
rho_power = 7.0


def with_halo(block, sides, width):
    for axis, dim in sides:
        count = lax.axis_size(axis)
        forward = [(i, i + 1) for i in range(count - 1)]
        backward = [(target, source) for source, target in forward]
        low = lax.ppermute(
            lax.slice_in_dim(block, block.shape[dim] - width, None, axis=dim), axis, forward
        )
        high = lax.ppermute(lax.slice_in_dim(block, 0, width, axis=dim), axis, backward)
        block = jnp.concatenate([low, block, high], axis=dim)
    return block


def from_behind(shard, axis, by):
    devices = lax.axis_size(axis)
    pairs = [(i, i + by) for i in range(devices) if 0 <= i + by < devices]
    return lax.ppermute(shard, axis, pairs)


def broadcast(shard, axis, root):
    mine = lax.axis_index(axis) == root
    return lax.psum(jnp.where(mine, shard, jnp.zeros_like(shard)), axis)


def sigma_at(position):
    fraction = position.astype(jnp.float32) / (SCHED - 1)
    top_root = sigma_top ** (1.0 / rho_power)
    low_root = sigma_low ** (1.0 / rho_power)
    return (top_root + fraction * (low_root - top_root)) ** rho_power


def exchange_kernel(
    peers, x_ref, top_ref, bot_ref, o_ref, lo_ref, hi_ref, send_sem, recv_sem, row_send, row_recv
):
    me = lax.axis_index("patch")
    seg = lax.axis_index("segment")
    mesh_ids = pl.DeviceIdType.MESH
    barrier = pltpu.get_barrier_semaphore()
    for dist in range(1, peers):
        pl.semaphore_signal(
            barrier, 1, device_id=(seg, lax.rem(me + dist, peers)), device_id_type=mesh_ids
        )
    pl.semaphore_wait(barrier, peers - 1)
    down = pltpu.make_async_remote_copy(
        src_ref=bot_ref,
        dst_ref=lo_ref,
        send_sem=row_send.at[0],
        recv_sem=row_recv.at[0],
        device_id=(seg, jnp.minimum(me + 1, peers - 1)),
        device_id_type=mesh_ids,
    )
    up = pltpu.make_async_remote_copy(
        src_ref=top_ref,
        dst_ref=hi_ref,
        send_sem=row_send.at[1],
        recv_sem=row_recv.at[1],
        device_id=(seg, jnp.maximum(me - 1, 0)),
        device_id_type=mesh_ids,
    )

    @pl.when(me < peers - 1)
    def _():
        down.start()

    @pl.when(me > 0)
    def _():
        up.start()

    copies = []
    for dist in range(1, peers):
        copy = pltpu.make_async_remote_copy(
            src_ref=x_ref,
            dst_ref=o_ref.at[me],
            send_sem=send_sem.at[dist],
            recv_sem=recv_sem.at[dist],
            device_id=(seg, lax.rem(me + dist, peers)),
            device_id_type=mesh_ids,
        )
        copy.start()
        copies.append(copy)
    o_ref[me] = x_ref[...]

    @pl.when(me == 0)
    def _():
        lo_ref[...] = jnp.zeros(lo_ref.shape, lo_ref.dtype)

    @pl.when(me == peers - 1)
    def _():
        hi_ref[...] = jnp.zeros(hi_ref.shape, hi_ref.dtype)

    for copy in copies:
        copy.wait()

    @pl.when(me < peers - 1)
    def _():
        down.wait_send()
        up.wait_recv()

    @pl.when(me > 0)
    def _():
        up.wait_send()
        down.wait_recv()


def exchange_patch(packed, top, bottom):
    peers = lax.axis_size("patch")
    vmem = pl.BlockSpec(memory_space=pltpu.VMEM)
    return pl.pallas_call(
        lambda *refs: exchange_kernel(peers, *refs),
        out_shape=(
            jax.ShapeDtypeStruct((peers,) + packed.shape, packed.dtype),
            jax.ShapeDtypeStruct(top.shape, top.dtype),
            jax.ShapeDtypeStruct(top.shape, top.dtype),
        ),
        in_specs=[vmem] * 3,
        out_specs=(vmem, vmem, vmem),
        scratch_shapes=[
            pltpu.SemaphoreType.DMA((peers,)),
            pltpu.SemaphoreType.DMA((peers,)),
            pltpu.SemaphoreType.DMA((2,)),
            pltpu.SemaphoreType.DMA((2,)),
        ],
        compiler_params=pltpu.CompilerParams(
            collective_id=0 if top.dtype == jnp.bfloat16 else 1, has_side_effects=True
        ),
        name="exchange_stats_rows",
    )(packed, top, bottom)


def group_moments(values, rows):
    batch_size, height, chan_count, col_count = values.shape
    grouped = values.reshape(batch_size, height, GROUPS, chan_count // GROUPS, col_count)
    local_count = chan_count // GROUPS * height * col_count
    peers = lax.axis_size("patch")
    local_sum = jnp.sum(grouped, axis=(1, 3, 4))
    local_center = local_sum / local_count
    local_dev = jnp.sum(
        jnp.square(grouped - local_center[:, None, :, None, None]), axis=(1, 3, 4)
    )
    flat = jnp.concatenate([local_sum.reshape(-1), local_dev.reshape(-1)])
    width = 128 * ((flat.shape[0] + 127) // 128)
    packed = jnp.zeros((8, width), jnp.float32).at[0, : flat.shape[0]].set(flat)
    every, low, high = exchange_patch(packed, rows[:, 0], rows[:, height - 1])
    every = every[:, 0, :]
    half = batch_size * GROUPS
    sums = every[:, :half].reshape(peers, batch_size, GROUPS)
    devs = every[:, half : 2 * half].reshape(peers, batch_size, GROUPS)
    cell_count = local_count * peers
    center = jnp.sum(sums, axis=0) / cell_count
    between = jnp.sum(jnp.square(sums / local_count - center[None]), axis=0) * local_count
    spread = (jnp.sum(devs, axis=0) + between) / cell_count
    return (center, jnp.sqrt(spread + epsilon)), low, high


def act_with_rows(values, rows, gain, shift):
    moments, low, high = group_moments(values, rows)
    full = jnp.concatenate(
        [low[:, None].astype(jnp.float32), values, high[:, None].astype(jnp.float32)], axis=1
    )
    act = norm_silu(full, moments, gain, shift)
    me = lax.axis_index("patch")
    row = lax.broadcasted_iota(jnp.int32, (1, full.shape[1], 1, 1), 1)
    pad = ((row == 0) & (me == 0)) | ((row == full.shape[1] - 1) & (me == lax.axis_size("patch") - 1))
    return jnp.where(pad, 0.0, act).astype(jnp.bfloat16)


def scatter_kernel(count, x_ref, o_ref, send_sem, recv_sem):
    seg = lax.axis_index("segment")
    me = lax.axis_index("patch")
    last = count - 1
    mesh_ids = pl.DeviceIdType.MESH
    barrier = pltpu.get_barrier_semaphore()

    @pl.when(seg == last)
    def _():
        for target in range(last):
            pl.semaphore_signal(barrier, 1, device_id=(target, me), device_id_type=mesh_ids)
        pl.semaphore_wait(barrier, last)
        copies = []
        for target in range(last):
            copy = pltpu.make_async_remote_copy(
                src_ref=x_ref.at[target],
                dst_ref=o_ref,
                send_sem=send_sem.at[target],
                recv_sem=recv_sem.at[0],
                device_id=(target, me),
                device_id_type=mesh_ids,
            )
            copy.start()
            copies.append(copy)
        o_ref[...] = x_ref[last]
        for copy in copies:
            copy.wait_send()

    @pl.when(seg != last)
    def _():
        pl.semaphore_signal(barrier, 1, device_id=(last, me), device_id_type=mesh_ids)
        pl.semaphore_wait(barrier, 1)
        pltpu.make_async_remote_copy(
            src_ref=x_ref.at[0],
            dst_ref=o_ref,
            send_sem=send_sem.at[0],
            recv_sem=recv_sem.at[0],
            device_id=(last, me),
            device_id_type=mesh_ids,
        ).wait_recv()


def scatter_from_last(pieces):
    count = lax.axis_size("segment")
    vmem = pl.BlockSpec(memory_space=pltpu.VMEM)
    return pl.pallas_call(
        lambda *refs: scatter_kernel(count, *refs),
        out_shape=jax.ShapeDtypeStruct(pieces.shape[1:], pieces.dtype),
        in_specs=[vmem],
        out_specs=vmem,
        scratch_shapes=[pltpu.SemaphoreType.DMA((count,)), pltpu.SemaphoreType.DMA((1,))],
        compiler_params=pltpu.CompilerParams(collective_id=2, has_side_effects=True),
        name="scatter_latent_columns",
    )(pieces)


def norm_silu(values, moments, gain, shift):
    center, root_spread = moments
    batch_size, height, chan_count, col_count = values.shape
    grouped = values.reshape(batch_size, height, GROUPS, chan_count // GROUPS, col_count)
    normed = (
        (grouped - center[:, None, :, None, None]) / root_spread[:, None, :, None, None]
    ).reshape(values.shape)
    normed = normed * gain[None, None, :, None] + shift[None, None, :, None]
    return jax.nn.silu(normed)


def conv_kernel(x_ref, w_ref, o_ref):
    batch, rows = o_ref.shape[0], o_ref.shape[1]
    for b in range(batch):
        for r in range(rows):
            acc = None
            for tap in range(9):
                part = jnp.dot(
                    w_ref[tap], x_ref[tap % 3, b, r + tap // 3], preferred_element_type=jnp.float32
                )
                acc = part if acc is None else acc + part
            o_ref[b, r] = acc


def conv_wide(rows_in, weights, block):
    batch, rows_halo, chans, cols = rows_in.shape
    outs = weights.shape[-2]
    padded = jnp.pad(rows_in, ((0, 0), (0, 0), (0, 0), (1, 1)))
    shifted = jnp.stack([padded[..., j : j + cols] for j in range(3)])
    flops = 2 * 9 * batch * (rows_halo - 2) * cols * chans * outs
    out_shape = (batch, rows_halo - 2, outs, cols)
    return pl.pallas_call(
        conv_kernel,
        grid=(1,),
        out_shape=jax.ShapeDtypeStruct(out_shape, jnp.float32),
        in_specs=[
            pl.BlockSpec(shifted.shape, lambda i: (0, 0, 0, 0, 0)),
            pl.BlockSpec((None, None) + weights.shape[2:], lambda i: (0, block, 0, 0, 0)),
        ],
        out_specs=pl.BlockSpec(out_shape, lambda i: (0, 0, 0, 0)),
        cost_estimate=pl.CostEstimate(
            flops=flops,
            transcendentals=0,
            bytes_accessed=shifted.size * 2 + 9 * chans * outs * 2 + batch * (rows_halo - 2) * outs * cols * 4,
        ),
        name="conv3x3_rows",
    )(shifted, weights)


def conv_valid(rows_in, kernel):
    padded = jnp.pad(rows_in, ((0, 0), (0, 0), (0, 0), (1, 1)))
    height = rows_in.shape[1] - 2
    col_count = rows_in.shape[3]
    accum = jnp.zeros((rows_in.shape[0], height, kernel.shape[1], col_count), jnp.float32)
    for tap_no in range(9):
        row_off, col_off = (tap_no // 3, tap_no % 3)
        window = padded[:, row_off : row_off + height, :, col_off : col_off + col_count]
        accum = accum + jnp.einsum(
            "oi,bhiw->bhow", kernel[tap_no], window, preferred_element_type=jnp.float32
        )
    return accum


def resnet_unit(hidden, conv1_w, conv2_w, block, gain_pair, shift_pair):
    hidden_wide = hidden.astype(jnp.float32)
    first_act = act_with_rows(hidden_wide, hidden, gain_pair[0], shift_pair[0])
    middle = conv_wide(first_act, conv1_w, block)
    second = act_with_rows(middle, middle, gain_pair[1], shift_pair[1])
    result = conv_wide(second, conv2_w, block)
    return (hidden_wide + result).astype(jnp.bfloat16)


def head_noise(source, head_w, head_gain, head_shift):
    head_input = act_with_rows(source.astype(jnp.float32), source, head_gain, head_shift)
    return jnp.transpose(conv_valid(head_input, head_w), (0, 2, 1, 3))


def with_rows(values):
    return with_halo(values, (("patch", 1),), 1)


def per_device(
    features,
    latent,
    plan_pos,
    blocks_used,
    conv1_w,
    conv2_w,
    norm_gain,
    norm_shift,
    in_w,
    head_w,
    head_gain,
    head_shift,
):
    segment_count = lax.axis_size("segment")
    segment_pos = lax.axis_index("segment")
    last = segment_count - 1
    current = jnp.transpose(features[0], (0, 2, 1, 3))
    for step_no in range(STEPS):
        arrived = from_behind(current, "segment", 1)
        noise_local = lax.cond(
            segment_pos == last,
            lambda source: head_noise(source, head_w, head_gain, head_shift),
            lambda source: jnp.zeros(latent.shape, jnp.float32),
            current,
        )
        position = plan_pos + step_no
        sigma_now = sigma_at(position)
        sigma_next = sigma_at(position + 1)
        latent = latent + (sigma_next - sigma_now)[:, None, None, None] * noise_local
        scaled = (latent / jnp.sqrt(sigma_next * sigma_next + 1.0)[:, None, None, None]).astype(
            jnp.bfloat16
        )
        scaled_first = lax.ppermute(scaled, "segment", [(last, 0)])
        entry_rows = conv_valid(
            with_rows(jnp.transpose(scaled_first, (0, 2, 1, 3))), in_w
        ).astype(jnp.bfloat16)
        source = jnp.where(segment_pos == 0, entry_rows, arrived)
        after_one = resnet_unit(source, conv1_w, conv2_w, 0, norm_gain[0, 0], norm_shift[0, 0])
        current = lax.cond(
            blocks_used[0] >= 2,
            lambda hidden: resnet_unit(
                hidden, conv1_w, conv2_w, 1, norm_gain[0, 1], norm_shift[0, 1]
            ),
            lambda hidden: hidden,
            after_one,
        )
    batch_size, lat_count, height, col_count = latent.shape
    col_share = col_count // segment_count
    latent, current = lax.optimization_barrier((latent, current))
    pieces = latent.reshape(batch_size, lat_count, height, segment_count, col_share)
    pieces = jnp.transpose(pieces, (3, 0, 1, 2, 4)).reshape(segment_count, -1, 128)
    latent_part = scatter_from_last(pieces).reshape(batch_size, lat_count, height, col_share)
    return (latent_part, jnp.transpose(current, (0, 2, 1, 3))[None])


def solution(mesh):
    placed = (
        P("segment", None, None, "patch", None),
        P(None, None, "patch", None),
        P(),
        P("segment"),
        P("segment", None, None, None, None),
        P("segment", None, None, None, None),
        P("segment", None, None, None),
        P("segment", None, None, None),
        P(),
        P(),
        P(),
        P(),
    )
    return jax.shard_map(
        per_device,
        mesh=mesh,
        in_specs=placed,
        out_specs=(P(None, None, "patch", "segment"), P("segment", None, None, "patch", None)),
        check_vma=False,
    )
```

```python
import jax
import jax.numpy as jnp
from jax import lax
from jax.sharding import PartitionSpec as P
from jax.experimental import pallas as pl
from jax.experimental.pallas import tpu as pltpu

GROUPS = 32
STEPS = 2
SCHED = 12


epsilon = 1e-05
sigma_top = 3.0
sigma_low = 0.1
rho_power = 7.0


def with_halo(block, sides, width):
    for axis, dim in sides:
        count = lax.axis_size(axis)
        forward = [(i, i + 1) for i in range(count - 1)]
        backward = [(target, source) for source, target in forward]
        low = lax.ppermute(
            lax.slice_in_dim(block, block.shape[dim] - width, None, axis=dim), axis, forward
        )
        high = lax.ppermute(lax.slice_in_dim(block, 0, width, axis=dim), axis, backward)
        block = jnp.concatenate([low, block, high], axis=dim)
    return block


def from_behind(shard, axis, by):
    devices = lax.axis_size(axis)
    pairs = [(i, i + by) for i in range(devices) if 0 <= i + by < devices]
    return lax.ppermute(shard, axis, pairs)


def broadcast(shard, axis, root):
    mine = lax.axis_index(axis) == root
    return lax.psum(jnp.where(mine, shard, jnp.zeros_like(shard)), axis)


def sigma_at(position):
    fraction = position.astype(jnp.float32) / (SCHED - 1)
    top_root = sigma_top ** (1.0 / rho_power)
    low_root = sigma_low ** (1.0 / rho_power)
    return (top_root + fraction * (low_root - top_root)) ** rho_power


def exchange_kernel(
    peers, x_ref, top_ref, bot_ref, o_ref, lo_ref, hi_ref, send_sem, recv_sem, row_send, row_recv
):
    me = lax.axis_index("patch")
    seg = lax.axis_index("segment")
    mesh_ids = pl.DeviceIdType.MESH
    barrier = pltpu.get_barrier_semaphore()
    for dist in range(1, peers):
        pl.semaphore_signal(
            barrier, 1, device_id=(seg, lax.rem(me + dist, peers)), device_id_type=mesh_ids
        )
    pl.semaphore_wait(barrier, peers - 1)
    down = pltpu.make_async_remote_copy(
        src_ref=bot_ref,
        dst_ref=lo_ref,
        send_sem=row_send.at[0],
        recv_sem=row_recv.at[0],
        device_id=(seg, jnp.minimum(me + 1, peers - 1)),
        device_id_type=mesh_ids,
    )
    up = pltpu.make_async_remote_copy(
        src_ref=top_ref,
        dst_ref=hi_ref,
        send_sem=row_send.at[1],
        recv_sem=row_recv.at[1],
        device_id=(seg, jnp.maximum(me - 1, 0)),
        device_id_type=mesh_ids,
    )

    @pl.when(me < peers - 1)
    def _():
        down.start()

    @pl.when(me > 0)
    def _():
        up.start()

    copies = []
    for dist in range(1, peers):
        copy = pltpu.make_async_remote_copy(
            src_ref=x_ref,
            dst_ref=o_ref.at[me],
            send_sem=send_sem.at[dist],
            recv_sem=recv_sem.at[dist],
            device_id=(seg, lax.rem(me + dist, peers)),
            device_id_type=mesh_ids,
        )
        copy.start()
        copies.append(copy)
    o_ref[me] = x_ref[...]

    @pl.when(me == 0)
    def _():
        lo_ref[...] = jnp.zeros(lo_ref.shape, lo_ref.dtype)

    @pl.when(me == peers - 1)
    def _():
        hi_ref[...] = jnp.zeros(hi_ref.shape, hi_ref.dtype)

    for copy in copies:
        copy.wait()

    @pl.when(me < peers - 1)
    def _():
        down.wait_send()
        up.wait_recv()

    @pl.when(me > 0)
    def _():
        up.wait_send()
        down.wait_recv()


def exchange_patch(packed, top, bottom):
    peers = lax.axis_size("patch")
    vmem = pl.BlockSpec(memory_space=pltpu.VMEM)
    return pl.pallas_call(
        lambda *refs: exchange_kernel(peers, *refs),
        out_shape=(
            jax.ShapeDtypeStruct((peers,) + packed.shape, packed.dtype),
            jax.ShapeDtypeStruct(top.shape, top.dtype),
            jax.ShapeDtypeStruct(top.shape, top.dtype),
        ),
        in_specs=[vmem] * 3,
        out_specs=(vmem, vmem, vmem),
        scratch_shapes=[
            pltpu.SemaphoreType.DMA((peers,)),
            pltpu.SemaphoreType.DMA((peers,)),
            pltpu.SemaphoreType.DMA((2,)),
            pltpu.SemaphoreType.DMA((2,)),
        ],
        compiler_params=pltpu.CompilerParams(
            collective_id=0 if top.dtype == jnp.bfloat16 else 1, has_side_effects=True
        ),
        name="exchange_stats_rows",
    )(packed, top, bottom)


def group_moments(values, rows):
    batch_size, height, chan_count, col_count = values.shape
    grouped = values.reshape(batch_size, height, GROUPS, chan_count // GROUPS, col_count)
    local_count = chan_count // GROUPS * height * col_count
    peers = lax.axis_size("patch")
    local_sum = jnp.sum(grouped, axis=(1, 3, 4))
    local_center = local_sum / local_count
    local_dev = jnp.sum(
        jnp.square(grouped - local_center[:, None, :, None, None]), axis=(1, 3, 4)
    )
    flat = jnp.concatenate([local_sum.reshape(-1), local_dev.reshape(-1)])
    width = 128 * ((flat.shape[0] + 127) // 128)
    packed = jnp.zeros((8, width), jnp.float32).at[0, : flat.shape[0]].set(flat)
    every, low, high = exchange_patch(packed, rows[:, 0], rows[:, height - 1])
    every = every[:, 0, :]
    half = batch_size * GROUPS
    sums = every[:, :half].reshape(peers, batch_size, GROUPS)
    devs = every[:, half : 2 * half].reshape(peers, batch_size, GROUPS)
    cell_count = local_count * peers
    center = jnp.sum(sums, axis=0) / cell_count
    between = jnp.sum(jnp.square(sums / local_count - center[None]), axis=0) * local_count
    spread = (jnp.sum(devs, axis=0) + between) / cell_count
    return (center, jnp.sqrt(spread + epsilon)), low, high


def act_with_rows(values, rows, gain, shift):
    moments, low, high = group_moments(values, rows)
    full = jnp.concatenate(
        [low[:, None].astype(jnp.float32), values, high[:, None].astype(jnp.float32)], axis=1
    )
    act = norm_silu(full, moments, gain, shift)
    me = lax.axis_index("patch")
    row = lax.broadcasted_iota(jnp.int32, (1, full.shape[1], 1, 1), 1)
    pad = ((row == 0) & (me == 0)) | ((row == full.shape[1] - 1) & (me == lax.axis_size("patch") - 1))
    return jnp.where(pad, 0.0, act).astype(jnp.bfloat16)


def scatter_kernel(count, x_ref, o_ref, send_sem, recv_sem):
    seg = lax.axis_index("segment")
    me = lax.axis_index("patch")
    last = count - 1
    mesh_ids = pl.DeviceIdType.MESH
    barrier = pltpu.get_barrier_semaphore()

    @pl.when(seg == last)
    def _():
        for target in range(last):
            pl.semaphore_signal(barrier, 1, device_id=(target, me), device_id_type=mesh_ids)
        pl.semaphore_wait(barrier, last)
        copies = []
        for target in range(last):
            copy = pltpu.make_async_remote_copy(
                src_ref=x_ref.at[target],
                dst_ref=o_ref,
                send_sem=send_sem.at[target],
                recv_sem=recv_sem.at[0],
                device_id=(target, me),
                device_id_type=mesh_ids,
            )
            copy.start()
            copies.append(copy)
        o_ref[...] = x_ref[last]
        for copy in copies:
            copy.wait_send()

    @pl.when(seg != last)
    def _():
        pl.semaphore_signal(barrier, 1, device_id=(last, me), device_id_type=mesh_ids)
        pl.semaphore_wait(barrier, 1)
        pltpu.make_async_remote_copy(
            src_ref=x_ref.at[0],
            dst_ref=o_ref,
            send_sem=send_sem.at[0],
            recv_sem=recv_sem.at[0],
            device_id=(last, me),
            device_id_type=mesh_ids,
        ).wait_recv()


def scatter_from_last(pieces):
    count = lax.axis_size("segment")
    vmem = pl.BlockSpec(memory_space=pltpu.VMEM)
    return pl.pallas_call(
        lambda *refs: scatter_kernel(count, *refs),
        out_shape=jax.ShapeDtypeStruct(pieces.shape[1:], pieces.dtype),
        in_specs=[vmem],
        out_specs=vmem,
        scratch_shapes=[pltpu.SemaphoreType.DMA((count,)), pltpu.SemaphoreType.DMA((1,))],
        compiler_params=pltpu.CompilerParams(collective_id=2, has_side_effects=True),
        name="scatter_latent_columns",
    )(pieces)


def norm_silu(values, moments, gain, shift):
    center, root_spread = moments
    batch_size, height, chan_count, col_count = values.shape
    grouped = values.reshape(batch_size, height, GROUPS, chan_count // GROUPS, col_count)
    normed = (
        (grouped - center[:, None, :, None, None]) / root_spread[:, None, :, None, None]
    ).reshape(values.shape)
    normed = normed * gain[None, None, :, None] + shift[None, None, :, None]
    return jax.nn.silu(normed)


def conv_kernel(x_ref, w_ref, o_ref):
    batch, rows = o_ref.shape[0], o_ref.shape[1]
    for b in range(batch):
        for r in range(rows):
            acc = None
            for tap in range(9):
                part = jnp.dot(
                    w_ref[tap], x_ref[tap % 3, b, r + tap // 3], preferred_element_type=jnp.float32
                )
                acc = part if acc is None else acc + part
            o_ref[b, r] = acc


def fused_kernel(
    flags_ref, vals_ref, lo_ref, hi_ref, mean_ref, std_ref, gain_ref, shift_ref, w_ref, o_ref, act_ref
):
    rows, chans, cols = vals_ref.shape
    mean = mean_ref[...]
    std = std_ref[...]
    gain = gain_ref[...]
    shift = shift_ref[...]
    col = lax.broadcasted_iota(jnp.int32, (chans, cols), 1)

    def put(slot, values, keep):
        normed = (values.astype(jnp.float32) - mean) / std * gain + shift
        act = normed / (1.0 + jnp.exp(-normed))
        act = jnp.where(keep, act, 0.0).astype(jnp.bfloat16).astype(jnp.float32)
        act_ref[slot, 1] = act.astype(jnp.bfloat16)
        left = jnp.where(col == 0, 0.0, pltpu.roll(act, 1, 1))
        act_ref[slot, 0] = left.astype(jnp.bfloat16)
        right = jnp.where(col == cols - 1, 0.0, pltpu.roll(act, cols - 1, 1))
        act_ref[slot, 2] = right.astype(jnp.bfloat16)

    put(0, lo_ref[...], flags_ref[0] > 0)
    for r in range(rows):
        put(r + 1, vals_ref[r], True)
    put(rows + 1, hi_ref[...], flags_ref[1] > 0)
    for r in range(rows):
        acc = None
        for tap in range(9):
            part = jnp.dot(
                w_ref[tap], act_ref[r + tap // 3, tap % 3], preferred_element_type=jnp.float32
            )
            acc = part if acc is None else acc + part
        o_ref[r] = acc


def norm_conv(values, moments, low, high, gain, shift, weights, block):
    batch, rows, chans, cols = values.shape
    outs = weights.shape[-2]
    center, root_spread = moments
    per_group = chans // GROUPS
    mean_c = jnp.repeat(center, per_group, axis=1)[:, :, None]
    std_c = jnp.repeat(root_spread, per_group, axis=1)[:, :, None]
    me = lax.axis_index("patch")
    flags = jnp.stack([me > 0, me < lax.axis_size("patch") - 1]).astype(jnp.int32)
    flops = 2 * 9 * batch * rows * cols * chans * outs
    row_spec = pl.BlockSpec((None, chans, cols), lambda b: (b, 0, 0))
    chan_spec = pl.BlockSpec((None, chans, 1), lambda b: (b, 0, 0))
    param_spec = pl.BlockSpec((chans, 1), lambda b: (0, 0))
    return pl.pallas_call(
        fused_kernel,
        grid=(batch,),
        out_shape=jax.ShapeDtypeStruct((batch, rows, outs, cols), jnp.float32),
        in_specs=[
            pl.BlockSpec(memory_space=pltpu.SMEM),
            pl.BlockSpec((None, rows, chans, cols), lambda b: (b, 0, 0, 0)),
            row_spec,
            row_spec,
            chan_spec,
            chan_spec,
            param_spec,
            param_spec,
            pl.BlockSpec((None, None) + weights.shape[2:], lambda b: (0, block, 0, 0, 0)),
        ],
        out_specs=pl.BlockSpec((None, rows, outs, cols), lambda b: (b, 0, 0, 0)),
        scratch_shapes=[pltpu.VMEM((rows + 2, 3, chans, cols), jnp.bfloat16)],
        cost_estimate=pl.CostEstimate(
            flops=flops,
            transcendentals=batch * (rows + 2) * chans * cols,
            bytes_accessed=values.size * values.dtype.itemsize + 9 * chans * outs * 2 + batch * rows * outs * cols * 4,
        ),
        name="norm_conv3x3_rows",
    )(flags, values, low, high, mean_c, std_c, gain[:, None], shift[:, None], weights)


def conv_valid(rows_in, kernel):
    padded = jnp.pad(rows_in, ((0, 0), (0, 0), (0, 0), (1, 1)))
    height = rows_in.shape[1] - 2
    col_count = rows_in.shape[3]
    accum = jnp.zeros((rows_in.shape[0], height, kernel.shape[1], col_count), jnp.float32)
    for tap_no in range(9):
        row_off, col_off = (tap_no // 3, tap_no % 3)
        window = padded[:, row_off : row_off + height, :, col_off : col_off + col_count]
        accum = accum + jnp.einsum(
            "oi,bhiw->bhow", kernel[tap_no], window, preferred_element_type=jnp.float32
        )
    return accum


def resnet_unit(hidden, conv1_w, conv2_w, block, gain_pair, shift_pair):
    hidden_wide = hidden.astype(jnp.float32)
    moments, low, high = group_moments(hidden_wide, hidden)
    middle = norm_conv(hidden, moments, low, high, gain_pair[0], shift_pair[0], conv1_w, block)
    moments, low, high = group_moments(middle, middle)
    result = norm_conv(middle, moments, low, high, gain_pair[1], shift_pair[1], conv2_w, block)
    return (hidden_wide + result).astype(jnp.bfloat16)


def head_noise(source, head_w, head_gain, head_shift):
    head_input = act_with_rows(source.astype(jnp.float32), source, head_gain, head_shift)
    return jnp.transpose(conv_valid(head_input, head_w), (0, 2, 1, 3))


def with_rows(values):
    return with_halo(values, (("patch", 1),), 1)


def per_device(
    features,
    latent,
    plan_pos,
    blocks_used,
    conv1_w,
    conv2_w,
    norm_gain,
    norm_shift,
    in_w,
    head_w,
    head_gain,
    head_shift,
):
    segment_count = lax.axis_size("segment")
    segment_pos = lax.axis_index("segment")
    last = segment_count - 1
    current = jnp.transpose(features[0], (0, 2, 1, 3))
    for step_no in range(STEPS):
        arrived = from_behind(current, "segment", 1)
        noise_local = lax.cond(
            segment_pos == last,
            lambda source: head_noise(source, head_w, head_gain, head_shift),
            lambda source: jnp.zeros(latent.shape, jnp.float32),
            current,
        )
        position = plan_pos + step_no
        sigma_now = sigma_at(position)
        sigma_next = sigma_at(position + 1)
        latent = latent + (sigma_next - sigma_now)[:, None, None, None] * noise_local
        scaled = (latent / jnp.sqrt(sigma_next * sigma_next + 1.0)[:, None, None, None]).astype(
            jnp.bfloat16
        )
        scaled_first = lax.ppermute(scaled, "segment", [(last, 0)])
        entry_rows = conv_valid(
            with_rows(jnp.transpose(scaled_first, (0, 2, 1, 3))), in_w
        ).astype(jnp.bfloat16)
        source = jnp.where(segment_pos == 0, entry_rows, arrived)
        after_one = resnet_unit(source, conv1_w, conv2_w, 0, norm_gain[0, 0], norm_shift[0, 0])
        current = lax.cond(
            blocks_used[0] >= 2,
            lambda hidden: resnet_unit(
                hidden, conv1_w, conv2_w, 1, norm_gain[0, 1], norm_shift[0, 1]
            ),
            lambda hidden: hidden,
            after_one,
        )
    batch_size, lat_count, height, col_count = latent.shape
    col_share = col_count // segment_count
    latent, current = lax.optimization_barrier((latent, current))
    pieces = latent.reshape(batch_size, lat_count, height, segment_count, col_share)
    pieces = jnp.transpose(pieces, (3, 0, 1, 2, 4)).reshape(segment_count, -1, 128)
    latent_part = scatter_from_last(pieces).reshape(batch_size, lat_count, height, col_share)
    return (latent_part, jnp.transpose(current, (0, 2, 1, 3))[None])


def solution(mesh):
    placed = (
        P("segment", None, None, "patch", None),
        P(None, None, "patch", None),
        P(),
        P("segment"),
        P("segment", None, None, None, None),
        P("segment", None, None, None, None),
        P("segment", None, None, None),
        P("segment", None, None, None),
        P(),
        P(),
        P(),
        P(),
    )
    return jax.shard_map(
        per_device,
        mesh=mesh,
        in_specs=placed,
        out_specs=(P(None, None, "patch", "segment"), P("segment", None, None, "patch", None)),
        check_vma=False,
    )
```

```python
import jax
import jax.numpy as jnp
from jax import lax
from jax.sharding import PartitionSpec as P
from jax.experimental import pallas as pl
from jax.experimental.pallas import tpu as pltpu

GROUPS = 32
STEPS = 2
SCHED = 12


epsilon = 1e-05
sigma_top = 3.0
sigma_low = 0.1
rho_power = 7.0


def with_halo(block, sides, width):
    for axis, dim in sides:
        count = lax.axis_size(axis)
        forward = [(i, i + 1) for i in range(count - 1)]
        backward = [(target, source) for source, target in forward]
        low = lax.ppermute(
            lax.slice_in_dim(block, block.shape[dim] - width, None, axis=dim), axis, forward
        )
        high = lax.ppermute(lax.slice_in_dim(block, 0, width, axis=dim), axis, backward)
        block = jnp.concatenate([low, block, high], axis=dim)
    return block


def from_behind(shard, axis, by):
    devices = lax.axis_size(axis)
    pairs = [(i, i + by) for i in range(devices) if 0 <= i + by < devices]
    return lax.ppermute(shard, axis, pairs)


def broadcast(shard, axis, root):
    mine = lax.axis_index(axis) == root
    return lax.psum(jnp.where(mine, shard, jnp.zeros_like(shard)), axis)


def sigma_at(position):
    fraction = position.astype(jnp.float32) / (SCHED - 1)
    top_root = sigma_top ** (1.0 / rho_power)
    low_root = sigma_low ** (1.0 / rho_power)
    return (top_root + fraction * (low_root - top_root)) ** rho_power


def exchange_kernel(
    peers, x_ref, top_ref, bot_ref, o_ref, lo_ref, hi_ref, send_sem, recv_sem, row_send, row_recv
):
    me = lax.axis_index("patch")
    seg = lax.axis_index("segment")
    mesh_ids = pl.DeviceIdType.MESH
    barrier = pltpu.get_barrier_semaphore()
    for dist in range(1, peers):
        pl.semaphore_signal(
            barrier, 1, device_id=(seg, lax.rem(me + dist, peers)), device_id_type=mesh_ids
        )
    pl.semaphore_wait(barrier, peers - 1)
    down = pltpu.make_async_remote_copy(
        src_ref=bot_ref,
        dst_ref=lo_ref,
        send_sem=row_send.at[0],
        recv_sem=row_recv.at[0],
        device_id=(seg, jnp.minimum(me + 1, peers - 1)),
        device_id_type=mesh_ids,
    )
    up = pltpu.make_async_remote_copy(
        src_ref=top_ref,
        dst_ref=hi_ref,
        send_sem=row_send.at[1],
        recv_sem=row_recv.at[1],
        device_id=(seg, jnp.maximum(me - 1, 0)),
        device_id_type=mesh_ids,
    )

    @pl.when(me < peers - 1)
    def _():
        down.start()

    @pl.when(me > 0)
    def _():
        up.start()

    copies = []
    for dist in range(1, peers):
        copy = pltpu.make_async_remote_copy(
            src_ref=x_ref,
            dst_ref=o_ref.at[me],
            send_sem=send_sem.at[dist],
            recv_sem=recv_sem.at[dist],
            device_id=(seg, lax.rem(me + dist, peers)),
            device_id_type=mesh_ids,
        )
        copy.start()
        copies.append(copy)
    o_ref[me] = x_ref[...]

    @pl.when(me == 0)
    def _():
        lo_ref[...] = jnp.zeros(lo_ref.shape, lo_ref.dtype)

    @pl.when(me == peers - 1)
    def _():
        hi_ref[...] = jnp.zeros(hi_ref.shape, hi_ref.dtype)

    for copy in copies:
        copy.wait()

    @pl.when(me < peers - 1)
    def _():
        down.wait_send()
        up.wait_recv()

    @pl.when(me > 0)
    def _():
        up.wait_send()
        down.wait_recv()


def exchange_patch(packed, top, bottom):
    peers = lax.axis_size("patch")
    vmem = pl.BlockSpec(memory_space=pltpu.VMEM)
    return pl.pallas_call(
        lambda *refs: exchange_kernel(peers, *refs),
        out_shape=(
            jax.ShapeDtypeStruct((peers,) + packed.shape, packed.dtype),
            jax.ShapeDtypeStruct(top.shape, top.dtype),
            jax.ShapeDtypeStruct(top.shape, top.dtype),
        ),
        in_specs=[vmem] * 3,
        out_specs=(vmem, vmem, vmem),
        scratch_shapes=[
            pltpu.SemaphoreType.DMA((peers,)),
            pltpu.SemaphoreType.DMA((peers,)),
            pltpu.SemaphoreType.DMA((2,)),
            pltpu.SemaphoreType.DMA((2,)),
        ],
        compiler_params=pltpu.CompilerParams(
            collective_id=0 if top.dtype == jnp.bfloat16 else 1, has_side_effects=True
        ),
        name="exchange_stats_rows",
    )(packed, top, bottom)


def group_moments(values, rows):
    batch_size, height, chan_count, col_count = values.shape
    grouped = values.reshape(batch_size, height, GROUPS, chan_count // GROUPS, col_count)
    local_count = chan_count // GROUPS * height * col_count
    peers = lax.axis_size("patch")
    local_sum = jnp.sum(grouped, axis=(1, 3, 4))
    local_center = local_sum / local_count
    local_dev = jnp.sum(
        jnp.square(grouped - local_center[:, None, :, None, None]), axis=(1, 3, 4)
    )
    flat = jnp.concatenate([local_sum.reshape(-1), local_dev.reshape(-1)])
    width = 128 * ((flat.shape[0] + 127) // 128)
    packed = jnp.pad(flat, (0, width - flat.shape[0]))[None]
    every, low, high = exchange_patch(packed, rows[:, 0], rows[:, height - 1])
    every = every.reshape(peers, width)
    half = batch_size * GROUPS
    sums = every[:, :half].reshape(peers, batch_size, GROUPS)
    devs = every[:, half : 2 * half].reshape(peers, batch_size, GROUPS)
    cell_count = local_count * peers
    center = jnp.sum(sums, axis=0) / cell_count
    between = jnp.sum(jnp.square(sums / local_count - center[None]), axis=0) * local_count
    spread = (jnp.sum(devs, axis=0) + between) / cell_count
    return (center, jnp.sqrt(spread + epsilon)), low, high


def act_with_rows(values, rows, gain, shift):
    moments, low, high = group_moments(values, rows)
    full = jnp.concatenate(
        [low[:, None].astype(jnp.float32), values, high[:, None].astype(jnp.float32)], axis=1
    )
    act = norm_silu(full, moments, gain, shift)
    me = lax.axis_index("patch")
    row = lax.broadcasted_iota(jnp.int32, (1, full.shape[1], 1, 1), 1)
    pad = ((row == 0) & (me == 0)) | ((row == full.shape[1] - 1) & (me == lax.axis_size("patch") - 1))
    return jnp.where(pad, 0.0, act).astype(jnp.bfloat16)


def scatter_kernel(count, x_ref, o_ref, send_sem, recv_sem):
    seg = lax.axis_index("segment")
    me = lax.axis_index("patch")
    last = count - 1
    mesh_ids = pl.DeviceIdType.MESH
    barrier = pltpu.get_barrier_semaphore()

    @pl.when(seg == last)
    def _():
        for target in range(last):
            pl.semaphore_signal(barrier, 1, device_id=(target, me), device_id_type=mesh_ids)
        pl.semaphore_wait(barrier, last)
        copies = []
        for target in range(last):
            copy = pltpu.make_async_remote_copy(
                src_ref=x_ref.at[target],
                dst_ref=o_ref,
                send_sem=send_sem.at[target],
                recv_sem=recv_sem.at[0],
                device_id=(target, me),
                device_id_type=mesh_ids,
            )
            copy.start()
            copies.append(copy)
        o_ref[...] = x_ref[last]
        for copy in copies:
            copy.wait_send()

    @pl.when(seg != last)
    def _():
        pl.semaphore_signal(barrier, 1, device_id=(last, me), device_id_type=mesh_ids)
        pl.semaphore_wait(barrier, 1)
        pltpu.make_async_remote_copy(
            src_ref=x_ref.at[0],
            dst_ref=o_ref,
            send_sem=send_sem.at[0],
            recv_sem=recv_sem.at[0],
            device_id=(last, me),
            device_id_type=mesh_ids,
        ).wait_recv()


def scatter_from_last(pieces):
    count = lax.axis_size("segment")
    vmem = pl.BlockSpec(memory_space=pltpu.VMEM)
    return pl.pallas_call(
        lambda *refs: scatter_kernel(count, *refs),
        out_shape=jax.ShapeDtypeStruct(pieces.shape[1:], pieces.dtype),
        in_specs=[vmem],
        out_specs=vmem,
        scratch_shapes=[pltpu.SemaphoreType.DMA((count,)), pltpu.SemaphoreType.DMA((1,))],
        compiler_params=pltpu.CompilerParams(collective_id=2, has_side_effects=True),
        name="scatter_latent_columns",
    )(pieces)


def norm_silu(values, moments, gain, shift):
    center, root_spread = moments
    batch_size, height, chan_count, col_count = values.shape
    grouped = values.reshape(batch_size, height, GROUPS, chan_count // GROUPS, col_count)
    normed = (
        (grouped - center[:, None, :, None, None]) / root_spread[:, None, :, None, None]
    ).reshape(values.shape)
    normed = normed * gain[None, None, :, None] + shift[None, None, :, None]
    return jax.nn.silu(normed)


def conv_kernel(x_ref, w_ref, o_ref):
    batch, rows = o_ref.shape[0], o_ref.shape[1]
    for b in range(batch):
        for r in range(rows):
            acc = None
            for tap in range(9):
                part = jnp.dot(
                    w_ref[tap], x_ref[tap % 3, b, r + tap // 3], preferred_element_type=jnp.float32
                )
                acc = part if acc is None else acc + part
            o_ref[b, r] = acc


def fused_kernel(flags_ref, vals_ref, lo_ref, hi_ref, stat_ref, par_ref, w_ref, *rest):
    if len(rest) == 3:
        res_ref, o_ref, act_ref = rest
    else:
        res_ref = None
        o_ref, act_ref = rest
    rows, chans, cols = vals_ref.shape
    mean = stat_ref[0]
    std = stat_ref[1]
    gain = par_ref[0]
    shift = par_ref[1]
    col = lax.broadcasted_iota(jnp.int32, (chans, cols), 1)

    def put(slot, values, keep):
        normed = (values.astype(jnp.float32) - mean) / std * gain + shift
        act = normed / (1.0 + jnp.exp(-normed))
        act = jnp.where(keep, act, 0.0).astype(jnp.bfloat16).astype(jnp.float32)
        act_ref[slot, 1] = act.astype(jnp.bfloat16)
        left = jnp.where(col == 0, 0.0, pltpu.roll(act, 1, 1))
        act_ref[slot, 0] = left.astype(jnp.bfloat16)
        right = jnp.where(col == cols - 1, 0.0, pltpu.roll(act, cols - 1, 1))
        act_ref[slot, 2] = right.astype(jnp.bfloat16)

    put(0, lo_ref[...], flags_ref[0] > 0)
    for r in range(rows):
        put(r + 1, vals_ref[r], True)
    put(rows + 1, hi_ref[...], flags_ref[1] > 0)
    for r in range(rows):
        acc = None
        for tap in range(9):
            part = jnp.dot(
                w_ref[tap], act_ref[r + tap // 3, tap % 3], preferred_element_type=jnp.float32
            )
            acc = part if acc is None else acc + part
        if res_ref is not None:
            acc = res_ref[r].astype(jnp.float32) + acc
        o_ref[r] = acc.astype(o_ref.dtype)


def norm_conv(values, moments, low, high, params, norm_no, weights, block, residual=None):
    batch, rows, chans, cols = values.shape
    outs = weights.shape[-2]
    center, root_spread = moments
    per_group = chans // GROUPS
    stats_c = jnp.repeat(jnp.stack([center, root_spread], axis=1), per_group, axis=2)[..., None]
    me = lax.axis_index("patch")
    flags = jnp.stack([me > 0, me < lax.axis_size("patch") - 1]).astype(jnp.int32)
    flops = 2 * 9 * batch * rows * cols * chans * outs
    row_spec = pl.BlockSpec((None, chans, cols), lambda b: (b, 0, 0))
    block_spec = pl.BlockSpec((None, rows, chans, cols), lambda b: (b, 0, 0, 0))
    operands = [flags, values, low, high, stats_c, params, weights]
    in_specs = [
        pl.BlockSpec(memory_space=pltpu.SMEM),
        block_spec,
        row_spec,
        row_spec,
        pl.BlockSpec((None, 2, chans, 1), lambda b: (b, 0, 0, 0)),
        pl.BlockSpec((None, None, 2, chans, 1), lambda b: (block, norm_no, 0, 0, 0)),
        pl.BlockSpec((None, None) + weights.shape[2:], lambda b: (0, block, 0, 0, 0)),
    ]
    out_dtype = jnp.float32
    if residual is not None:
        operands.append(residual)
        in_specs.append(block_spec)
        out_dtype = residual.dtype
    return pl.pallas_call(
        fused_kernel,
        grid=(batch,),
        out_shape=jax.ShapeDtypeStruct((batch, rows, outs, cols), out_dtype),
        in_specs=in_specs,
        out_specs=pl.BlockSpec((None, rows, outs, cols), lambda b: (b, 0, 0, 0)),
        scratch_shapes=[pltpu.VMEM((rows + 2, 3, chans, cols), jnp.bfloat16)],
        cost_estimate=pl.CostEstimate(
            flops=flops,
            transcendentals=batch * (rows + 2) * chans * cols,
            bytes_accessed=values.size * values.dtype.itemsize + 9 * chans * outs * 2 + batch * rows * outs * cols * 4,
        ),
        name="norm_conv3x3_rows",
    )(*operands)


def conv_valid(rows_in, kernel):
    padded = jnp.pad(rows_in, ((0, 0), (0, 0), (0, 0), (1, 1)))
    height = rows_in.shape[1] - 2
    col_count = rows_in.shape[3]
    accum = jnp.zeros((rows_in.shape[0], height, kernel.shape[1], col_count), jnp.float32)
    for tap_no in range(9):
        row_off, col_off = (tap_no // 3, tap_no % 3)
        window = padded[:, row_off : row_off + height, :, col_off : col_off + col_count]
        accum = accum + jnp.einsum(
            "oi,bhiw->bhow", kernel[tap_no], window, preferred_element_type=jnp.float32
        )
    return accum


def resnet_unit(hidden, conv1_w, conv2_w, block, params):
    moments, low, high = group_moments(hidden.astype(jnp.float32), hidden)
    middle = norm_conv(hidden, moments, low, high, params, 0, conv1_w, block)
    moments, low, high = group_moments(middle, middle)
    return norm_conv(middle, moments, low, high, params, 1, conv2_w, block, residual=hidden)


def head_noise(source, head_w, head_gain, head_shift):
    head_input = act_with_rows(source.astype(jnp.float32), source, head_gain, head_shift)
    return jnp.transpose(conv_valid(head_input, head_w), (0, 2, 1, 3))


def with_rows(values):
    return with_halo(values, (("patch", 1),), 1)


def per_device(
    features,
    latent,
    plan_pos,
    blocks_used,
    conv1_w,
    conv2_w,
    norm_gain,
    norm_shift,
    in_w,
    head_w,
    head_gain,
    head_shift,
):
    segment_count = lax.axis_size("segment")
    segment_pos = lax.axis_index("segment")
    last = segment_count - 1
    current = jnp.transpose(features[0], (0, 2, 1, 3))
    params = jnp.stack([norm_gain[0], norm_shift[0]], axis=2)[..., None]
    for step_no in range(STEPS):
        arrived = from_behind(current, "segment", 1)
        noise_local = lax.cond(
            segment_pos == last,
            lambda source: head_noise(source, head_w, head_gain, head_shift),
            lambda source: jnp.zeros(latent.shape, jnp.float32),
            current,
        )
        position = plan_pos + step_no
        sigma_now = sigma_at(position)
        sigma_next = sigma_at(position + 1)
        latent = latent + (sigma_next - sigma_now)[:, None, None, None] * noise_local
        scaled = (latent / jnp.sqrt(sigma_next * sigma_next + 1.0)[:, None, None, None]).astype(
            jnp.bfloat16
        )
        scaled_first = lax.ppermute(scaled, "segment", [(last, 0)])
        entry_rows = conv_valid(
            with_rows(jnp.transpose(scaled_first, (0, 2, 1, 3))), in_w
        ).astype(jnp.bfloat16)
        source = jnp.where(segment_pos == 0, entry_rows, arrived)
        after_one = resnet_unit(source, conv1_w, conv2_w, 0, params)
        current = lax.cond(
            blocks_used[0] >= 2,
            lambda hidden: resnet_unit(hidden, conv1_w, conv2_w, 1, params),
            lambda hidden: hidden,
            after_one,
        )
    batch_size, lat_count, height, col_count = latent.shape
    col_share = col_count // segment_count
    latent, current = lax.optimization_barrier((latent, current))
    pieces = latent.reshape(batch_size, lat_count, height, segment_count, col_share)
    pieces = jnp.transpose(pieces, (3, 0, 1, 2, 4)).reshape(segment_count, -1, 128)
    latent_part = scatter_from_last(pieces).reshape(batch_size, lat_count, height, col_share)
    return (latent_part, jnp.transpose(current, (0, 2, 1, 3))[None])


def solution(mesh):
    placed = (
        P("segment", None, None, "patch", None),
        P(None, None, "patch", None),
        P(),
        P("segment"),
        P("segment", None, None, None, None),
        P("segment", None, None, None, None),
        P("segment", None, None, None),
        P("segment", None, None, None),
        P(),
        P(),
        P(),
        P(),
    )
    return jax.shard_map(
        per_device,
        mesh=mesh,
        in_specs=placed,
        out_specs=(P(None, None, "patch", "segment"), P("segment", None, None, "patch", None)),
        check_vma=False,
    )
```

```python
import jax
import jax.numpy as jnp
from jax import lax
from jax.sharding import PartitionSpec as P
from jax.experimental import pallas as pl
from jax.experimental.pallas import tpu as pltpu

GROUPS = 32
STEPS = 2
SCHED = 12


epsilon = 1e-05
sigma_top = 3.0
sigma_low = 0.1
rho_power = 7.0


def with_halo(block, sides, width):
    for axis, dim in sides:
        count = lax.axis_size(axis)
        forward = [(i, i + 1) for i in range(count - 1)]
        backward = [(target, source) for source, target in forward]
        low = lax.ppermute(
            lax.slice_in_dim(block, block.shape[dim] - width, None, axis=dim), axis, forward
        )
        high = lax.ppermute(lax.slice_in_dim(block, 0, width, axis=dim), axis, backward)
        block = jnp.concatenate([low, block, high], axis=dim)
    return block


def from_behind(shard, axis, by):
    devices = lax.axis_size(axis)
    pairs = [(i, i + by) for i in range(devices) if 0 <= i + by < devices]
    return lax.ppermute(shard, axis, pairs)


def broadcast(shard, axis, root):
    mine = lax.axis_index(axis) == root
    return lax.psum(jnp.where(mine, shard, jnp.zeros_like(shard)), axis)


def sigma_at(position):
    fraction = position.astype(jnp.float32) / (SCHED - 1)
    top_root = sigma_top ** (1.0 / rho_power)
    low_root = sigma_low ** (1.0 / rho_power)
    return (top_root + fraction * (low_root - top_root)) ** rho_power


def exchange_kernel(
    peers, x_ref, top_ref, bot_ref, o_ref, lo_ref, hi_ref, send_sem, recv_sem, row_send, row_recv
):
    me = lax.axis_index("patch")
    seg = lax.axis_index("segment")
    mesh_ids = pl.DeviceIdType.MESH
    barrier = pltpu.get_barrier_semaphore()
    for dist in range(1, peers):
        pl.semaphore_signal(
            barrier, 1, device_id=(seg, lax.rem(me + dist, peers)), device_id_type=mesh_ids
        )
    pl.semaphore_wait(barrier, peers - 1)
    down = pltpu.make_async_remote_copy(
        src_ref=bot_ref,
        dst_ref=lo_ref,
        send_sem=row_send.at[0],
        recv_sem=row_recv.at[0],
        device_id=(seg, jnp.minimum(me + 1, peers - 1)),
        device_id_type=mesh_ids,
    )
    up = pltpu.make_async_remote_copy(
        src_ref=top_ref,
        dst_ref=hi_ref,
        send_sem=row_send.at[1],
        recv_sem=row_recv.at[1],
        device_id=(seg, jnp.maximum(me - 1, 0)),
        device_id_type=mesh_ids,
    )

    @pl.when(me < peers - 1)
    def _():
        down.start()

    @pl.when(me > 0)
    def _():
        up.start()

    copies = []
    for dist in range(1, peers):
        copy = pltpu.make_async_remote_copy(
            src_ref=x_ref,
            dst_ref=o_ref.at[me],
            send_sem=send_sem.at[dist],
            recv_sem=recv_sem.at[dist],
            device_id=(seg, lax.rem(me + dist, peers)),
            device_id_type=mesh_ids,
        )
        copy.start()
        copies.append(copy)
    o_ref[me] = x_ref[...]

    @pl.when(me == 0)
    def _():
        lo_ref[...] = jnp.zeros(lo_ref.shape, lo_ref.dtype)

    @pl.when(me == peers - 1)
    def _():
        hi_ref[...] = jnp.zeros(hi_ref.shape, hi_ref.dtype)

    for copy in copies:
        copy.wait()

    @pl.when(me < peers - 1)
    def _():
        down.wait_send()
        up.wait_recv()

    @pl.when(me > 0)
    def _():
        up.wait_send()
        down.wait_recv()


def exchange_patch(packed, top, bottom):
    peers = lax.axis_size("patch")
    vmem = pl.BlockSpec(memory_space=pltpu.VMEM)
    return pl.pallas_call(
        lambda *refs: exchange_kernel(peers, *refs),
        out_shape=(
            jax.ShapeDtypeStruct((peers,) + packed.shape, packed.dtype),
            jax.ShapeDtypeStruct(top.shape, top.dtype),
            jax.ShapeDtypeStruct(top.shape, top.dtype),
        ),
        in_specs=[vmem] * 3,
        out_specs=(vmem, vmem, vmem),
        scratch_shapes=[
            pltpu.SemaphoreType.DMA((peers,)),
            pltpu.SemaphoreType.DMA((peers,)),
            pltpu.SemaphoreType.DMA((2,)),
            pltpu.SemaphoreType.DMA((2,)),
        ],
        compiler_params=pltpu.CompilerParams(
            collective_id=0 if top.dtype == jnp.bfloat16 else 1, has_side_effects=True
        ),
        name="exchange_stats_rows",
    )(packed, top, bottom)


def group_moments(values, rows):
    batch_size, height, chan_count, col_count = values.shape
    grouped = values.reshape(batch_size, height, GROUPS, chan_count // GROUPS, col_count)
    local_count = chan_count // GROUPS * height * col_count
    peers = lax.axis_size("patch")
    local_sum = jnp.sum(grouped, axis=(1, 3, 4))
    local_center = local_sum / local_count
    local_dev = jnp.sum(
        jnp.square(grouped - local_center[:, None, :, None, None]), axis=(1, 3, 4)
    )
    flat = jnp.concatenate([local_sum.reshape(-1), local_dev.reshape(-1)])
    width = 128 * ((flat.shape[0] + 127) // 128)
    packed = jnp.pad(flat, (0, width - flat.shape[0]))[None]
    every, low, high = exchange_patch(packed, rows[:, 0], rows[:, height - 1])
    every = every.reshape(peers, width)
    half = batch_size * GROUPS
    sums = every[:, :half].reshape(peers, batch_size, GROUPS)
    devs = every[:, half : 2 * half].reshape(peers, batch_size, GROUPS)
    cell_count = local_count * peers
    center = jnp.sum(sums, axis=0) / cell_count
    between = jnp.sum(jnp.square(sums / local_count - center[None]), axis=0) * local_count
    spread = (jnp.sum(devs, axis=0) + between) / cell_count
    return (center, jnp.sqrt(spread + epsilon)), low, high


def act_with_rows(values, rows, gain, shift):
    moments, low, high = group_moments(values, rows)
    full = jnp.concatenate(
        [low[:, None].astype(jnp.float32), values, high[:, None].astype(jnp.float32)], axis=1
    )
    act = norm_silu(full, moments, gain, shift)
    me = lax.axis_index("patch")
    row = lax.broadcasted_iota(jnp.int32, (1, full.shape[1], 1, 1), 1)
    pad = ((row == 0) & (me == 0)) | ((row == full.shape[1] - 1) & (me == lax.axis_size("patch") - 1))
    return jnp.where(pad, 0.0, act).astype(jnp.bfloat16)


def scatter_kernel(count, x_ref, o_ref, send_sem, recv_sem):
    seg = lax.axis_index("segment")
    me = lax.axis_index("patch")
    last = count - 1
    mesh_ids = pl.DeviceIdType.MESH
    barrier = pltpu.get_barrier_semaphore()

    @pl.when(seg == last)
    def _():
        for target in range(last):
            pl.semaphore_signal(barrier, 1, device_id=(target, me), device_id_type=mesh_ids)
        pl.semaphore_wait(barrier, last)
        copies = []
        for target in range(last):
            copy = pltpu.make_async_remote_copy(
                src_ref=x_ref.at[target],
                dst_ref=o_ref,
                send_sem=send_sem.at[target],
                recv_sem=recv_sem.at[0],
                device_id=(target, me),
                device_id_type=mesh_ids,
            )
            copy.start()
            copies.append(copy)
        o_ref[...] = x_ref[last]
        for copy in copies:
            copy.wait_send()

    @pl.when(seg != last)
    def _():
        pl.semaphore_signal(barrier, 1, device_id=(last, me), device_id_type=mesh_ids)
        pl.semaphore_wait(barrier, 1)
        pltpu.make_async_remote_copy(
            src_ref=x_ref.at[0],
            dst_ref=o_ref,
            send_sem=send_sem.at[0],
            recv_sem=recv_sem.at[0],
            device_id=(last, me),
            device_id_type=mesh_ids,
        ).wait_recv()


def scatter_from_last(pieces):
    count = lax.axis_size("segment")
    vmem = pl.BlockSpec(memory_space=pltpu.VMEM)
    return pl.pallas_call(
        lambda *refs: scatter_kernel(count, *refs),
        out_shape=jax.ShapeDtypeStruct(pieces.shape[1:], pieces.dtype),
        in_specs=[vmem],
        out_specs=vmem,
        scratch_shapes=[pltpu.SemaphoreType.DMA((count,)), pltpu.SemaphoreType.DMA((1,))],
        compiler_params=pltpu.CompilerParams(collective_id=2, has_side_effects=True),
        name="scatter_latent_columns",
    )(pieces)


def norm_silu(values, moments, gain, shift):
    center, root_spread = moments
    batch_size, height, chan_count, col_count = values.shape
    grouped = values.reshape(batch_size, height, GROUPS, chan_count // GROUPS, col_count)
    normed = (
        (grouped - center[:, None, :, None, None]) / root_spread[:, None, :, None, None]
    ).reshape(values.shape)
    normed = normed * gain[None, None, :, None] + shift[None, None, :, None]
    return jax.nn.silu(normed)


def conv_kernel(x_ref, w_ref, o_ref):
    batch, rows = o_ref.shape[0], o_ref.shape[1]
    for b in range(batch):
        for r in range(rows):
            acc = None
            for tap in range(9):
                part = jnp.dot(
                    w_ref[tap], x_ref[tap % 3, b, r + tap // 3], preferred_element_type=jnp.float32
                )
                acc = part if acc is None else acc + part
            o_ref[b, r] = acc


def fused_kernel(flags_ref, vals_ref, lo_ref, hi_ref, stat_ref, par_ref, w_ref, *rest):
    if len(rest) == 3:
        res_ref, o_ref, act_ref = rest
    else:
        res_ref = None
        o_ref, act_ref = rest
    rows, chans, cols = vals_ref.shape
    mean = stat_ref[0]
    std = stat_ref[1]
    gain = par_ref[0]
    shift = par_ref[1]
    col = lax.broadcasted_iota(jnp.int32, (chans, cols), 1)

    def put(slot, values, keep):
        normed = (values.astype(jnp.float32) - mean) / std * gain + shift
        act = normed / (1.0 + jnp.exp(-normed))
        act = jnp.where(keep, act, 0.0).astype(jnp.bfloat16).astype(jnp.float32)
        act_ref[slot, 1] = act.astype(jnp.bfloat16)
        left = jnp.where(col == 0, 0.0, pltpu.roll(act, 1, 1))
        act_ref[slot, 0] = left.astype(jnp.bfloat16)
        right = jnp.where(col == cols - 1, 0.0, pltpu.roll(act, cols - 1, 1))
        act_ref[slot, 2] = right.astype(jnp.bfloat16)

    put(0, lo_ref[...], flags_ref[0] > 0)
    for r in range(rows):
        put(r + 1, vals_ref[r], True)
    put(rows + 1, hi_ref[...], flags_ref[1] > 0)
    for r in range(rows):
        acc = None
        for tap in range(9):
            part = jnp.dot(
                w_ref[tap], act_ref[r + tap // 3, tap % 3], preferred_element_type=jnp.float32
            )
            acc = part if acc is None else acc + part
        if res_ref is not None:
            acc = res_ref[r].astype(jnp.float32) + acc
        o_ref[r] = acc.astype(o_ref.dtype)


def norm_conv(values, moments, low, high, params, norm_no, weights, block, residual=None):
    batch, rows, chans, cols = values.shape
    outs = weights.shape[-2]
    center, root_spread = moments
    per_group = chans // GROUPS
    stats_c = jnp.repeat(jnp.stack([center, root_spread], axis=1), per_group, axis=2)[..., None]
    me = lax.axis_index("patch")
    flags = jnp.stack([me > 0, me < lax.axis_size("patch") - 1]).astype(jnp.int32)
    flops = 2 * 9 * batch * rows * cols * chans * outs
    row_spec = pl.BlockSpec((None, chans, cols), lambda b: (b, 0, 0))
    block_spec = pl.BlockSpec((None, rows, chans, cols), lambda b: (b, 0, 0, 0))
    operands = [flags, values, low, high, stats_c, params, weights]
    in_specs = [
        pl.BlockSpec(memory_space=pltpu.SMEM),
        block_spec,
        row_spec,
        row_spec,
        pl.BlockSpec((None, 2, chans, 1), lambda b: (b, 0, 0, 0)),
        pl.BlockSpec((None, None, 2, chans, 1), lambda b: (block, norm_no, 0, 0, 0)),
        pl.BlockSpec((None, None) + weights.shape[2:], lambda b: (0, block, 0, 0, 0)),
    ]
    out_dtype = jnp.float32
    if residual is not None:
        operands.append(residual)
        in_specs.append(block_spec)
        out_dtype = residual.dtype
    return pl.pallas_call(
        fused_kernel,
        grid=(batch,),
        out_shape=jax.ShapeDtypeStruct((batch, rows, outs, cols), out_dtype),
        in_specs=in_specs,
        out_specs=pl.BlockSpec((None, rows, outs, cols), lambda b: (b, 0, 0, 0)),
        scratch_shapes=[pltpu.VMEM((rows + 2, 3, chans, cols), jnp.bfloat16)],
        cost_estimate=pl.CostEstimate(
            flops=flops,
            transcendentals=batch * (rows + 2) * chans * cols,
            bytes_accessed=values.size * values.dtype.itemsize + 9 * chans * outs * 2 + batch * rows * outs * cols * 4,
        ),
        name="norm_conv3x3_rows",
    )(*operands)


def conv_valid(rows_in, kernel):
    padded = jnp.pad(rows_in, ((0, 0), (0, 0), (0, 0), (1, 1)))
    height = rows_in.shape[1] - 2
    col_count = rows_in.shape[3]
    accum = jnp.zeros((rows_in.shape[0], height, kernel.shape[1], col_count), jnp.float32)
    for tap_no in range(9):
        row_off, col_off = (tap_no // 3, tap_no % 3)
        window = padded[:, row_off : row_off + height, :, col_off : col_off + col_count]
        accum = accum + jnp.einsum(
            "oi,bhiw->bhow", kernel[tap_no], window, preferred_element_type=jnp.float32
        )
    return accum


def resnet_unit(hidden, conv1_w, conv2_w, block, params):
    moments, low, high = group_moments(hidden.astype(jnp.float32), hidden)
    middle = norm_conv(hidden, moments, low, high, params, 0, conv1_w, block)
    moments, low, high = group_moments(middle, middle)
    return norm_conv(middle, moments, low, high, params, 1, conv2_w, block, residual=hidden)


def head_noise(source, head_w, head_params):
    moments, low, high = group_moments(source.astype(jnp.float32), source)
    noise = norm_conv(source, moments, low, high, head_params, 0, head_w[None, None], 0)
    return jnp.transpose(noise, (0, 2, 1, 3))


def with_rows(values):
    return with_halo(values, (("patch", 1),), 1)


def per_device(
    features,
    latent,
    plan_pos,
    blocks_used,
    conv1_w,
    conv2_w,
    norm_gain,
    norm_shift,
    in_w,
    head_w,
    head_gain,
    head_shift,
):
    segment_count = lax.axis_size("segment")
    segment_pos = lax.axis_index("segment")
    last = segment_count - 1
    current = jnp.transpose(features[0], (0, 2, 1, 3))
    params = jnp.stack([norm_gain[0], norm_shift[0]], axis=2)[..., None]
    head_params = jnp.stack([head_gain, head_shift])[None, None, :, :, None]
    for step_no in range(STEPS):
        arrived = from_behind(current, "segment", 1)
        noise_local = lax.cond(
            segment_pos == last,
            lambda source: head_noise(source, head_w, head_params),
            lambda source: jnp.zeros(latent.shape, jnp.float32),
            current,
        )
        position = plan_pos + step_no
        sigma_now = sigma_at(position)
        sigma_next = sigma_at(position + 1)
        latent = latent + (sigma_next - sigma_now)[:, None, None, None] * noise_local
        scaled = (latent / jnp.sqrt(sigma_next * sigma_next + 1.0)[:, None, None, None]).astype(
            jnp.bfloat16
        )
        scaled_first = lax.ppermute(scaled, "segment", [(last, 0)])
        entry_rows = conv_valid(
            with_rows(jnp.transpose(scaled_first, (0, 2, 1, 3))), in_w
        ).astype(jnp.bfloat16)
        source = jnp.where(segment_pos == 0, entry_rows, arrived)
        after_one = resnet_unit(source, conv1_w, conv2_w, 0, params)
        current = lax.cond(
            blocks_used[0] >= 2,
            lambda hidden: resnet_unit(hidden, conv1_w, conv2_w, 1, params),
            lambda hidden: hidden,
            after_one,
        )
    batch_size, lat_count, height, col_count = latent.shape
    col_share = col_count // segment_count
    latent, current = lax.optimization_barrier((latent, current))
    pieces = latent.reshape(batch_size, lat_count, height, segment_count, col_share)
    pieces = jnp.transpose(pieces, (3, 0, 1, 2, 4)).reshape(segment_count, -1, 128)
    latent_part = scatter_from_last(pieces).reshape(batch_size, lat_count, height, col_share)
    return (latent_part, jnp.transpose(current, (0, 2, 1, 3))[None])


def solution(mesh):
    placed = (
        P("segment", None, None, "patch", None),
        P(None, None, "patch", None),
        P(),
        P("segment"),
        P("segment", None, None, None, None),
        P("segment", None, None, None, None),
        P("segment", None, None, None),
        P("segment", None, None, None),
        P(),
        P(),
        P(),
        P(),
    )
    return jax.shard_map(
        per_device,
        mesh=mesh,
        in_specs=placed,
        out_specs=(P(None, None, "patch", "segment"), P("segment", None, None, "patch", None)),
        check_vma=False,
    )
```

```python
import jax
import jax.numpy as jnp
from jax import lax
from jax.sharding import PartitionSpec as P
from jax.experimental import pallas as pl
from jax.experimental.pallas import tpu as pltpu

GROUPS = 32
STEPS = 2
SCHED = 12


epsilon = 1e-05
sigma_top = 3.0
sigma_low = 0.1
rho_power = 7.0


def with_halo(block, sides, width):
    for axis, dim in sides:
        count = lax.axis_size(axis)
        forward = [(i, i + 1) for i in range(count - 1)]
        backward = [(target, source) for source, target in forward]
        low = lax.ppermute(
            lax.slice_in_dim(block, block.shape[dim] - width, None, axis=dim), axis, forward
        )
        high = lax.ppermute(lax.slice_in_dim(block, 0, width, axis=dim), axis, backward)
        block = jnp.concatenate([low, block, high], axis=dim)
    return block


def from_behind(shard, axis, by):
    devices = lax.axis_size(axis)
    pairs = [(i, i + by) for i in range(devices) if 0 <= i + by < devices]
    return lax.ppermute(shard, axis, pairs)


def broadcast(shard, axis, root):
    mine = lax.axis_index(axis) == root
    return lax.psum(jnp.where(mine, shard, jnp.zeros_like(shard)), axis)


def sigma_at(position):
    fraction = position.astype(jnp.float32) / (SCHED - 1)
    top_root = sigma_top ** (1.0 / rho_power)
    low_root = sigma_low ** (1.0 / rho_power)
    return (top_root + fraction * (low_root - top_root)) ** rho_power


def exchange_kernel(
    peers, x_ref, top_ref, bot_ref, o_ref, lo_ref, hi_ref, send_sem, recv_sem, row_send, row_recv
):
    me = lax.axis_index("patch")
    seg = lax.axis_index("segment")
    mesh_ids = pl.DeviceIdType.MESH
    barrier = pltpu.get_barrier_semaphore()
    for dist in range(1, peers):
        pl.semaphore_signal(
            barrier, 1, device_id=(seg, lax.rem(me + dist, peers)), device_id_type=mesh_ids
        )
    pl.semaphore_wait(barrier, peers - 1)
    down = pltpu.make_async_remote_copy(
        src_ref=bot_ref,
        dst_ref=lo_ref,
        send_sem=row_send.at[0],
        recv_sem=row_recv.at[0],
        device_id=(seg, jnp.minimum(me + 1, peers - 1)),
        device_id_type=mesh_ids,
    )
    up = pltpu.make_async_remote_copy(
        src_ref=top_ref,
        dst_ref=hi_ref,
        send_sem=row_send.at[1],
        recv_sem=row_recv.at[1],
        device_id=(seg, jnp.maximum(me - 1, 0)),
        device_id_type=mesh_ids,
    )

    @pl.when(me < peers - 1)
    def _():
        down.start()

    @pl.when(me > 0)
    def _():
        up.start()

    copies = []
    for dist in range(1, peers):
        copy = pltpu.make_async_remote_copy(
            src_ref=x_ref,
            dst_ref=o_ref.at[me],
            send_sem=send_sem.at[dist],
            recv_sem=recv_sem.at[dist],
            device_id=(seg, lax.rem(me + dist, peers)),
            device_id_type=mesh_ids,
        )
        copy.start()
        copies.append(copy)
    o_ref[me] = x_ref[...]

    @pl.when(me == 0)
    def _():
        lo_ref[...] = jnp.zeros(lo_ref.shape, lo_ref.dtype)

    @pl.when(me == peers - 1)
    def _():
        hi_ref[...] = jnp.zeros(hi_ref.shape, hi_ref.dtype)

    for copy in copies:
        copy.wait()

    @pl.when(me < peers - 1)
    def _():
        down.wait_send()
        up.wait_recv()

    @pl.when(me > 0)
    def _():
        up.wait_send()
        down.wait_recv()


def exchange_patch(packed, top, bottom):
    peers = lax.axis_size("patch")
    vmem = pl.BlockSpec(memory_space=pltpu.VMEM)
    return pl.pallas_call(
        lambda *refs: exchange_kernel(peers, *refs),
        out_shape=(
            jax.ShapeDtypeStruct((peers,) + packed.shape, packed.dtype),
            jax.ShapeDtypeStruct(top.shape, top.dtype),
            jax.ShapeDtypeStruct(top.shape, top.dtype),
        ),
        in_specs=[vmem] * 3,
        out_specs=(vmem, vmem, vmem),
        scratch_shapes=[
            pltpu.SemaphoreType.DMA((peers,)),
            pltpu.SemaphoreType.DMA((peers,)),
            pltpu.SemaphoreType.DMA((2,)),
            pltpu.SemaphoreType.DMA((2,)),
        ],
        compiler_params=pltpu.CompilerParams(
            collective_id=0 if top.dtype == jnp.bfloat16 else 1, has_side_effects=True
        ),
        name="exchange_stats_rows",
    )(packed, top, bottom)


def group_moments(values, rows):
    batch_size, height, chan_count, col_count = values.shape
    grouped = values.reshape(batch_size, height, GROUPS, chan_count // GROUPS, col_count)
    local_count = chan_count // GROUPS * height * col_count
    peers = lax.axis_size("patch")
    local_sum = jnp.sum(grouped, axis=(1, 3, 4))
    local_center = local_sum / local_count
    local_dev = jnp.sum(
        jnp.square(grouped - local_center[:, None, :, None, None]), axis=(1, 3, 4)
    )
    flat = jnp.concatenate([local_sum.reshape(-1), local_dev.reshape(-1)])
    width = 128 * ((flat.shape[0] + 127) // 128)
    packed = jnp.pad(flat, (0, width - flat.shape[0]))[None]
    every, low, high = exchange_patch(packed, rows[:, 0], rows[:, height - 1])
    every = every.reshape(peers, width)
    half = batch_size * GROUPS
    sums = every[:, :half].reshape(peers, batch_size, GROUPS)
    devs = every[:, half : 2 * half].reshape(peers, batch_size, GROUPS)
    cell_count = local_count * peers
    center = jnp.sum(sums, axis=0) / cell_count
    between = jnp.sum(jnp.square(sums / local_count - center[None]), axis=0) * local_count
    spread = (jnp.sum(devs, axis=0) + between) / cell_count
    return (center, jnp.sqrt(spread + epsilon)), low, high


def act_with_rows(values, rows, gain, shift):
    moments, low, high = group_moments(values, rows)
    full = jnp.concatenate(
        [low[:, None].astype(jnp.float32), values, high[:, None].astype(jnp.float32)], axis=1
    )
    act = norm_silu(full, moments, gain, shift)
    me = lax.axis_index("patch")
    row = lax.broadcasted_iota(jnp.int32, (1, full.shape[1], 1, 1), 1)
    pad = ((row == 0) & (me == 0)) | ((row == full.shape[1] - 1) & (me == lax.axis_size("patch") - 1))
    return jnp.where(pad, 0.0, act).astype(jnp.bfloat16)


def scatter_kernel(count, x_ref, o_ref, send_sem, recv_sem):
    seg = lax.axis_index("segment")
    me = lax.axis_index("patch")
    last = count - 1
    mesh_ids = pl.DeviceIdType.MESH
    barrier = pltpu.get_barrier_semaphore()

    @pl.when(seg == last)
    def _():
        for target in range(last):
            pl.semaphore_signal(barrier, 1, device_id=(target, me), device_id_type=mesh_ids)
        pl.semaphore_wait(barrier, last)
        copies = []
        for target in range(last):
            copy = pltpu.make_async_remote_copy(
                src_ref=x_ref.at[target],
                dst_ref=o_ref,
                send_sem=send_sem.at[target],
                recv_sem=recv_sem.at[0],
                device_id=(target, me),
                device_id_type=mesh_ids,
            )
            copy.start()
            copies.append(copy)
        o_ref[...] = x_ref[last]
        for copy in copies:
            copy.wait_send()

    @pl.when(seg != last)
    def _():
        pl.semaphore_signal(barrier, 1, device_id=(last, me), device_id_type=mesh_ids)
        pl.semaphore_wait(barrier, 1)
        pltpu.make_async_remote_copy(
            src_ref=x_ref.at[0],
            dst_ref=o_ref,
            send_sem=send_sem.at[0],
            recv_sem=recv_sem.at[0],
            device_id=(last, me),
            device_id_type=mesh_ids,
        ).wait_recv()


def scatter_from_last(pieces):
    count = lax.axis_size("segment")
    vmem = pl.BlockSpec(memory_space=pltpu.VMEM)
    return pl.pallas_call(
        lambda *refs: scatter_kernel(count, *refs),
        out_shape=jax.ShapeDtypeStruct(pieces.shape[1:], pieces.dtype),
        in_specs=[vmem],
        out_specs=vmem,
        scratch_shapes=[pltpu.SemaphoreType.DMA((count,)), pltpu.SemaphoreType.DMA((1,))],
        compiler_params=pltpu.CompilerParams(collective_id=2, has_side_effects=True),
        name="scatter_latent_columns",
    )(pieces)


def norm_silu(values, moments, gain, shift):
    center, root_spread = moments
    batch_size, height, chan_count, col_count = values.shape
    grouped = values.reshape(batch_size, height, GROUPS, chan_count // GROUPS, col_count)
    normed = (
        (grouped - center[:, None, :, None, None]) / root_spread[:, None, :, None, None]
    ).reshape(values.shape)
    normed = normed * gain[None, None, :, None] + shift[None, None, :, None]
    return jax.nn.silu(normed)


def conv_kernel(x_ref, w_ref, o_ref):
    batch, rows = o_ref.shape[0], o_ref.shape[1]
    for b in range(batch):
        for r in range(rows):
            acc = None
            for tap in range(9):
                part = jnp.dot(
                    w_ref[tap], x_ref[tap % 3, b, r + tap // 3], preferred_element_type=jnp.float32
                )
                acc = part if acc is None else acc + part
            o_ref[b, r] = acc


def fused_kernel(flags_ref, vals_ref, lo_ref, hi_ref, stat_ref, par_ref, w_ref, *rest):
    if len(rest) == 3:
        res_ref, o_ref, act_ref = rest
    else:
        res_ref = None
        o_ref, act_ref = rest
    rows, chans, cols = vals_ref.shape
    mean = stat_ref[0]
    std = stat_ref[1]
    gain = par_ref[0]
    shift = par_ref[1]
    col = lax.broadcasted_iota(jnp.int32, (chans, cols), 1)

    def put(slot, values, keep):
        normed = (values.astype(jnp.float32) - mean) / std * gain + shift
        act = normed / (1.0 + jnp.exp(-normed))
        act = jnp.where(keep, act, 0.0).astype(jnp.bfloat16).astype(jnp.float32)
        act_ref[slot, 1] = act.astype(jnp.bfloat16)
        left = jnp.where(col == 0, 0.0, pltpu.roll(act, 1, 1))
        act_ref[slot, 0] = left.astype(jnp.bfloat16)
        right = jnp.where(col == cols - 1, 0.0, pltpu.roll(act, cols - 1, 1))
        act_ref[slot, 2] = right.astype(jnp.bfloat16)

    put(0, lo_ref[...], flags_ref[0] > 0)

    def put_row(r, carry):
        put(r + 1, vals_ref[r], True)
        return carry

    lax.fori_loop(0, rows, put_row, 0)
    put(rows + 1, hi_ref[...], flags_ref[1] > 0)

    def conv_row(r, carry):
        acc = None
        for tap in range(9):
            part = jnp.dot(
                w_ref[tap], act_ref[r + tap // 3, tap % 3], preferred_element_type=jnp.float32
            )
            acc = part if acc is None else acc + part
        if res_ref is not None:
            acc = res_ref[r].astype(jnp.float32) + acc
        o_ref[r] = acc.astype(o_ref.dtype)
        return carry

    lax.fori_loop(0, rows, conv_row, 0)


def norm_conv(values, moments, low, high, params, norm_no, weights, block, residual=None):
    batch, rows, chans, cols = values.shape
    outs = weights.shape[-2]
    center, root_spread = moments
    per_group = chans // GROUPS
    stats_c = jnp.repeat(jnp.stack([center, root_spread], axis=1), per_group, axis=2)[..., None]
    me = lax.axis_index("patch")
    flags = jnp.stack([me > 0, me < lax.axis_size("patch") - 1]).astype(jnp.int32)
    flops = 2 * 9 * batch * rows * cols * chans * outs
    row_spec = pl.BlockSpec((None, chans, cols), lambda b: (b, 0, 0))
    block_spec = pl.BlockSpec((None, rows, chans, cols), lambda b: (b, 0, 0, 0))
    operands = [flags, values, low, high, stats_c, params, weights]
    in_specs = [
        pl.BlockSpec(memory_space=pltpu.SMEM),
        block_spec,
        row_spec,
        row_spec,
        pl.BlockSpec((None, 2, chans, 1), lambda b: (b, 0, 0, 0)),
        pl.BlockSpec((None, None, 2, chans, 1), lambda b: (block, norm_no, 0, 0, 0)),
        pl.BlockSpec((None, None) + weights.shape[2:], lambda b: (0, block, 0, 0, 0)),
    ]
    out_dtype = jnp.float32
    if residual is not None:
        operands.append(residual)
        in_specs.append(block_spec)
        out_dtype = residual.dtype
    return pl.pallas_call(
        fused_kernel,
        grid=(batch,),
        out_shape=jax.ShapeDtypeStruct((batch, rows, outs, cols), out_dtype),
        in_specs=in_specs,
        out_specs=pl.BlockSpec((None, rows, outs, cols), lambda b: (b, 0, 0, 0)),
        scratch_shapes=[pltpu.VMEM((rows + 2, 3, chans, cols), jnp.bfloat16)],
        cost_estimate=pl.CostEstimate(
            flops=flops,
            transcendentals=batch * (rows + 2) * chans * cols,
            bytes_accessed=values.size * values.dtype.itemsize + 9 * chans * outs * 2 + batch * rows * outs * cols * 4,
        ),
        name="norm_conv3x3_rows",
    )(*operands)


def conv_valid(rows_in, kernel):
    padded = jnp.pad(rows_in, ((0, 0), (0, 0), (0, 0), (1, 1)))
    height = rows_in.shape[1] - 2
    col_count = rows_in.shape[3]
    accum = jnp.zeros((rows_in.shape[0], height, kernel.shape[1], col_count), jnp.float32)
    for tap_no in range(9):
        row_off, col_off = (tap_no // 3, tap_no % 3)
        window = padded[:, row_off : row_off + height, :, col_off : col_off + col_count]
        accum = accum + jnp.einsum(
            "oi,bhiw->bhow", kernel[tap_no], window, preferred_element_type=jnp.float32
        )
    return accum


def resnet_unit(hidden, conv1_w, conv2_w, block, params):
    moments, low, high = group_moments(hidden.astype(jnp.float32), hidden)
    middle = norm_conv(hidden, moments, low, high, params, 0, conv1_w, block)
    moments, low, high = group_moments(middle, middle)
    return norm_conv(middle, moments, low, high, params, 1, conv2_w, block, residual=hidden)


def head_noise(source, head_w, head_gain, head_shift):
    head_input = act_with_rows(source.astype(jnp.float32), source, head_gain, head_shift)
    return jnp.transpose(conv_valid(head_input, head_w), (0, 2, 1, 3))


def with_rows(values):
    return with_halo(values, (("patch", 1),), 1)


def per_device(
    features,
    latent,
    plan_pos,
    blocks_used,
    conv1_w,
    conv2_w,
    norm_gain,
    norm_shift,
    in_w,
    head_w,
    head_gain,
    head_shift,
):
    segment_count = lax.axis_size("segment")
    segment_pos = lax.axis_index("segment")
    last = segment_count - 1
    current = jnp.transpose(features[0], (0, 2, 1, 3))
    params = jnp.stack([norm_gain[0], norm_shift[0]], axis=2)[..., None]
    for step_no in range(STEPS):
        arrived = from_behind(current, "segment", 1)
        noise_local = lax.cond(
            segment_pos == last,
            lambda source: head_noise(source, head_w, head_gain, head_shift),
            lambda source: jnp.zeros(latent.shape, jnp.float32),
            current,
        )
        position = plan_pos + step_no
        sigma_now = sigma_at(position)
        sigma_next = sigma_at(position + 1)
        latent = latent + (sigma_next - sigma_now)[:, None, None, None] * noise_local
        scaled = (latent / jnp.sqrt(sigma_next * sigma_next + 1.0)[:, None, None, None]).astype(
            jnp.bfloat16
        )
        scaled_first = lax.ppermute(scaled, "segment", [(last, 0)])
        entry_rows = conv_valid(
            with_rows(jnp.transpose(scaled_first, (0, 2, 1, 3))), in_w
        ).astype(jnp.bfloat16)
        source = jnp.where(segment_pos == 0, entry_rows, arrived)
        after_one = resnet_unit(source, conv1_w, conv2_w, 0, params)
        current = lax.cond(
            blocks_used[0] >= 2,
            lambda hidden: resnet_unit(hidden, conv1_w, conv2_w, 1, params),
            lambda hidden: hidden,
            after_one,
        )
    batch_size, lat_count, height, col_count = latent.shape
    col_share = col_count // segment_count
    latent, current = lax.optimization_barrier((latent, current))
    pieces = latent.reshape(batch_size, lat_count, height, segment_count, col_share)
    pieces = jnp.transpose(pieces, (3, 0, 1, 2, 4)).reshape(segment_count, -1, 128)
    latent_part = scatter_from_last(pieces).reshape(batch_size, lat_count, height, col_share)
    return (latent_part, jnp.transpose(current, (0, 2, 1, 3))[None])


def solution(mesh):
    placed = (
        P("segment", None, None, "patch", None),
        P(None, None, "patch", None),
        P(),
        P("segment"),
        P("segment", None, None, None, None),
        P("segment", None, None, None, None),
        P("segment", None, None, None),
        P("segment", None, None, None),
        P(),
        P(),
        P(),
        P(),
    )
    return jax.shard_map(
        per_device,
        mesh=mesh,
        in_specs=placed,
        out_specs=(P(None, None, "patch", "segment"), P("segment", None, None, "patch", None)),
        check_vma=False,
    )
```

```python
import jax
import jax.numpy as jnp
from jax import lax
from jax.sharding import PartitionSpec as P
from jax.experimental import pallas as pl
from jax.experimental.pallas import tpu as pltpu

GROUPS = 32
STEPS = 2
SCHED = 12


epsilon = 1e-05
sigma_top = 3.0
sigma_low = 0.1
rho_power = 7.0


def with_halo(block, sides, width):
    for axis, dim in sides:
        count = lax.axis_size(axis)
        forward = [(i, i + 1) for i in range(count - 1)]
        backward = [(target, source) for source, target in forward]
        low = lax.ppermute(
            lax.slice_in_dim(block, block.shape[dim] - width, None, axis=dim), axis, forward
        )
        high = lax.ppermute(lax.slice_in_dim(block, 0, width, axis=dim), axis, backward)
        block = jnp.concatenate([low, block, high], axis=dim)
    return block


def from_behind(shard, axis, by):
    devices = lax.axis_size(axis)
    pairs = [(i, i + by) for i in range(devices) if 0 <= i + by < devices]
    return lax.ppermute(shard, axis, pairs)


def broadcast(shard, axis, root):
    mine = lax.axis_index(axis) == root
    return lax.psum(jnp.where(mine, shard, jnp.zeros_like(shard)), axis)


def sigma_at(position):
    fraction = position.astype(jnp.float32) / (SCHED - 1)
    top_root = sigma_top ** (1.0 / rho_power)
    low_root = sigma_low ** (1.0 / rho_power)
    return (top_root + fraction * (low_root - top_root)) ** rho_power


def exchange_kernel(
    peers, x_ref, top_ref, bot_ref, o_ref, lo_ref, hi_ref, send_sem, recv_sem, row_send, row_recv
):
    me = lax.axis_index("patch")
    seg = lax.axis_index("segment")
    mesh_ids = pl.DeviceIdType.MESH
    barrier = pltpu.get_barrier_semaphore()
    for dist in range(1, peers):
        pl.semaphore_signal(
            barrier, 1, device_id=(seg, lax.rem(me + dist, peers)), device_id_type=mesh_ids
        )
    pl.semaphore_wait(barrier, peers - 1)
    down = pltpu.make_async_remote_copy(
        src_ref=bot_ref,
        dst_ref=lo_ref,
        send_sem=row_send.at[0],
        recv_sem=row_recv.at[0],
        device_id=(seg, jnp.minimum(me + 1, peers - 1)),
        device_id_type=mesh_ids,
    )
    up = pltpu.make_async_remote_copy(
        src_ref=top_ref,
        dst_ref=hi_ref,
        send_sem=row_send.at[1],
        recv_sem=row_recv.at[1],
        device_id=(seg, jnp.maximum(me - 1, 0)),
        device_id_type=mesh_ids,
    )

    @pl.when(me < peers - 1)
    def _():
        down.start()

    @pl.when(me > 0)
    def _():
        up.start()

    copies = []
    for dist in range(1, peers):
        copy = pltpu.make_async_remote_copy(
            src_ref=x_ref,
            dst_ref=o_ref.at[me],
            send_sem=send_sem.at[dist],
            recv_sem=recv_sem.at[dist],
            device_id=(seg, lax.rem(me + dist, peers)),
            device_id_type=mesh_ids,
        )
        copy.start()
        copies.append(copy)
    o_ref[me] = x_ref[...]

    @pl.when(me == 0)
    def _():
        lo_ref[...] = jnp.zeros(lo_ref.shape, lo_ref.dtype)

    @pl.when(me == peers - 1)
    def _():
        hi_ref[...] = jnp.zeros(hi_ref.shape, hi_ref.dtype)

    for copy in copies:
        copy.wait()

    @pl.when(me < peers - 1)
    def _():
        down.wait_send()
        up.wait_recv()

    @pl.when(me > 0)
    def _():
        up.wait_send()
        down.wait_recv()


def exchange_patch(packed, top, bottom):
    peers = lax.axis_size("patch")
    vmem = pl.BlockSpec(memory_space=pltpu.VMEM)
    return pl.pallas_call(
        lambda *refs: exchange_kernel(peers, *refs),
        out_shape=(
            jax.ShapeDtypeStruct((peers,) + packed.shape, packed.dtype),
            jax.ShapeDtypeStruct(top.shape, top.dtype),
            jax.ShapeDtypeStruct(top.shape, top.dtype),
        ),
        in_specs=[vmem] * 3,
        out_specs=(vmem, vmem, vmem),
        scratch_shapes=[
            pltpu.SemaphoreType.DMA((peers,)),
            pltpu.SemaphoreType.DMA((peers,)),
            pltpu.SemaphoreType.DMA((2,)),
            pltpu.SemaphoreType.DMA((2,)),
        ],
        compiler_params=pltpu.CompilerParams(
            collective_id=0 if top.dtype == jnp.bfloat16 else 1, has_side_effects=True
        ),
        name="exchange_stats_rows",
    )(packed, top, bottom)


def group_moments(values, rows):
    batch_size, height, chan_count, col_count = values.shape
    grouped = values.reshape(batch_size, height, GROUPS, chan_count // GROUPS, col_count)
    local_count = chan_count // GROUPS * height * col_count
    peers = lax.axis_size("patch")
    local_sum = jnp.sum(grouped, axis=(1, 3, 4))
    local_center = local_sum / local_count
    local_dev = jnp.sum(
        jnp.square(grouped - local_center[:, None, :, None, None]), axis=(1, 3, 4)
    )
    flat = jnp.concatenate([local_sum.reshape(-1), local_dev.reshape(-1)])
    width = 128 * ((flat.shape[0] + 127) // 128)
    packed = jnp.pad(flat, (0, width - flat.shape[0]))[None]
    every, low, high = exchange_patch(packed, rows[:, 0], rows[:, height - 1])
    every = every.reshape(peers, width)
    half = batch_size * GROUPS
    sums = every[:, :half].reshape(peers, batch_size, GROUPS)
    devs = every[:, half : 2 * half].reshape(peers, batch_size, GROUPS)
    cell_count = local_count * peers
    center = jnp.sum(sums, axis=0) / cell_count
    between = jnp.sum(jnp.square(sums / local_count - center[None]), axis=0) * local_count
    spread = (jnp.sum(devs, axis=0) + between) / cell_count
    return (center, jnp.sqrt(spread + epsilon)), low, high


def act_with_rows(values, rows, gain, shift):
    moments, low, high = group_moments(values, rows)
    full = jnp.concatenate(
        [low[:, None].astype(jnp.float32), values, high[:, None].astype(jnp.float32)], axis=1
    )
    act = norm_silu(full, moments, gain, shift)
    me = lax.axis_index("patch")
    row = lax.broadcasted_iota(jnp.int32, (1, full.shape[1], 1, 1), 1)
    pad = ((row == 0) & (me == 0)) | ((row == full.shape[1] - 1) & (me == lax.axis_size("patch") - 1))
    return jnp.where(pad, 0.0, act).astype(jnp.bfloat16)


def scatter_kernel(count, x_ref, o_ref, send_sem, recv_sem):
    seg = lax.axis_index("segment")
    me = lax.axis_index("patch")
    last = count - 1
    mesh_ids = pl.DeviceIdType.MESH
    barrier = pltpu.get_barrier_semaphore()

    @pl.when(seg == last)
    def _():
        for target in range(last):
            pl.semaphore_signal(barrier, 1, device_id=(target, me), device_id_type=mesh_ids)
        pl.semaphore_wait(barrier, last)
        copies = []
        for target in range(last):
            copy = pltpu.make_async_remote_copy(
                src_ref=x_ref.at[target],
                dst_ref=o_ref,
                send_sem=send_sem.at[target],
                recv_sem=recv_sem.at[0],
                device_id=(target, me),
                device_id_type=mesh_ids,
            )
            copy.start()
            copies.append(copy)
        o_ref[...] = x_ref[last]
        for copy in copies:
            copy.wait_send()

    @pl.when(seg != last)
    def _():
        pl.semaphore_signal(barrier, 1, device_id=(last, me), device_id_type=mesh_ids)
        pl.semaphore_wait(barrier, 1)
        pltpu.make_async_remote_copy(
            src_ref=x_ref.at[0],
            dst_ref=o_ref,
            send_sem=send_sem.at[0],
            recv_sem=recv_sem.at[0],
            device_id=(last, me),
            device_id_type=mesh_ids,
        ).wait_recv()


def scatter_from_last(pieces):
    count = lax.axis_size("segment")
    vmem = pl.BlockSpec(memory_space=pltpu.VMEM)
    return pl.pallas_call(
        lambda *refs: scatter_kernel(count, *refs),
        out_shape=jax.ShapeDtypeStruct(pieces.shape[1:], pieces.dtype),
        in_specs=[vmem],
        out_specs=vmem,
        scratch_shapes=[pltpu.SemaphoreType.DMA((count,)), pltpu.SemaphoreType.DMA((1,))],
        compiler_params=pltpu.CompilerParams(collective_id=2, has_side_effects=True),
        name="scatter_latent_columns",
    )(pieces)


def norm_silu(values, moments, gain, shift):
    center, root_spread = moments
    batch_size, height, chan_count, col_count = values.shape
    grouped = values.reshape(batch_size, height, GROUPS, chan_count // GROUPS, col_count)
    normed = (
        (grouped - center[:, None, :, None, None]) / root_spread[:, None, :, None, None]
    ).reshape(values.shape)
    normed = normed * gain[None, None, :, None] + shift[None, None, :, None]
    return jax.nn.silu(normed)


def conv_kernel(x_ref, w_ref, o_ref):
    batch, rows = o_ref.shape[0], o_ref.shape[1]
    for b in range(batch):
        for r in range(rows):
            acc = None
            for tap in range(9):
                part = jnp.dot(
                    w_ref[tap], x_ref[tap % 3, b, r + tap // 3], preferred_element_type=jnp.float32
                )
                acc = part if acc is None else acc + part
            o_ref[b, r] = acc


def fused_kernel(flags_ref, vals_ref, lo_ref, hi_ref, stat_ref, par_ref, w_ref, *rest):
    if len(rest) == 3:
        res_ref, o_ref, act_ref = rest
    else:
        res_ref = None
        o_ref, act_ref = rest
    rows, chans, cols = vals_ref.shape
    mean = stat_ref[0]
    std = stat_ref[1]
    gain = par_ref[0]
    shift = par_ref[1]
    col = lax.broadcasted_iota(jnp.int32, (chans, cols), 1)

    def put(slot, values, keep):
        normed = (values.astype(jnp.float32) - mean) / std * gain + shift
        act = normed / (1.0 + jnp.exp(-normed))
        act = jnp.where(keep, act, 0.0).astype(jnp.bfloat16).astype(jnp.float32)
        act_ref[slot, 1] = act.astype(jnp.bfloat16)
        left = jnp.where(col == 0, 0.0, pltpu.roll(act, 1, 1))
        act_ref[slot, 0] = left.astype(jnp.bfloat16)
        right = jnp.where(col == cols - 1, 0.0, pltpu.roll(act, cols - 1, 1))
        act_ref[slot, 2] = right.astype(jnp.bfloat16)

    put(0, lo_ref[...], flags_ref[0] > 0)
    for r in range(rows):
        put(r + 1, vals_ref[r], True)
    put(rows + 1, hi_ref[...], flags_ref[1] > 0)
    for r in range(rows):
        acc = None
        for tap in range(9):
            part = jnp.dot(
                w_ref[tap], act_ref[r + tap // 3, tap % 3], preferred_element_type=jnp.float32
            )
            acc = part if acc is None else acc + part
        if res_ref is not None:
            acc = res_ref[r].astype(jnp.float32) + acc
        o_ref[r] = acc.astype(o_ref.dtype)


def norm_conv(values, moments, low, high, params, norm_no, weights, block, residual=None):
    batch, rows, chans, cols = values.shape
    outs = weights.shape[-2]
    center, root_spread = moments
    per_group = chans // GROUPS
    stats_c = jnp.repeat(jnp.stack([center, root_spread], axis=1), per_group, axis=2)[..., None]
    me = lax.axis_index("patch")
    flags = jnp.stack([me > 0, me < lax.axis_size("patch") - 1]).astype(jnp.int32)
    flops = 2 * 9 * batch * rows * cols * chans * outs
    row_spec = pl.BlockSpec((None, chans, cols), lambda b: (b, 0, 0))
    block_spec = pl.BlockSpec((None, rows, chans, cols), lambda b: (b, 0, 0, 0))
    operands = [flags, values, low, high, stats_c, params, weights]
    in_specs = [
        pl.BlockSpec(memory_space=pltpu.SMEM),
        block_spec,
        row_spec,
        row_spec,
        pl.BlockSpec((None, 2, chans, 1), lambda b: (b, 0, 0, 0)),
        pl.BlockSpec((None, None, 2, chans, 1), lambda b: (block, norm_no, 0, 0, 0)),
        pl.BlockSpec((None, None) + weights.shape[2:], lambda b: (0, block, 0, 0, 0)),
    ]
    out_dtype = jnp.float32
    if residual is not None:
        operands.append(residual)
        in_specs.append(block_spec)
        out_dtype = residual.dtype
    return pl.pallas_call(
        fused_kernel,
        grid=(batch,),
        out_shape=jax.ShapeDtypeStruct((batch, rows, outs, cols), out_dtype),
        in_specs=in_specs,
        out_specs=pl.BlockSpec((None, rows, outs, cols), lambda b: (b, 0, 0, 0)),
        scratch_shapes=[pltpu.VMEM((rows + 2, 3, chans, cols), jnp.bfloat16)],
        cost_estimate=pl.CostEstimate(
            flops=flops,
            transcendentals=batch * (rows + 2) * chans * cols,
            bytes_accessed=values.size * values.dtype.itemsize + 9 * chans * outs * 2 + batch * rows * outs * cols * 4,
        ),
        name="norm_conv3x3_rows",
    )(*operands)


def conv_valid(rows_in, kernel):
    padded = jnp.pad(rows_in, ((0, 0), (0, 0), (0, 0), (1, 1)))
    height = rows_in.shape[1] - 2
    col_count = rows_in.shape[3]
    accum = jnp.zeros((rows_in.shape[0], height, kernel.shape[1], col_count), jnp.float32)
    for tap_no in range(9):
        row_off, col_off = (tap_no // 3, tap_no % 3)
        window = padded[:, row_off : row_off + height, :, col_off : col_off + col_count]
        accum = accum + jnp.einsum(
            "oi,bhiw->bhow", kernel[tap_no], window, preferred_element_type=jnp.float32
        )
    return accum


def resnet_unit(hidden, conv1_w, conv2_w, block, params):
    moments, low, high = group_moments(hidden.astype(jnp.float32), hidden)
    middle = norm_conv(hidden, moments, low, high, params, 0, conv1_w, block)
    moments, low, high = group_moments(middle, middle)
    return norm_conv(middle, moments, low, high, params, 1, conv2_w, block, residual=hidden)


def head_noise(source, head_w, head_gain, head_shift):
    head_input = act_with_rows(source.astype(jnp.float32), source, head_gain, head_shift)
    return jnp.transpose(conv_valid(head_input, head_w), (0, 2, 1, 3))


def with_rows(values):
    return with_halo(values, (("patch", 1),), 1)


def per_device(
    features,
    latent,
    plan_pos,
    blocks_used,
    conv1_w,
    conv2_w,
    norm_gain,
    norm_shift,
    in_w,
    head_w,
    head_gain,
    head_shift,
):
    segment_count = lax.axis_size("segment")
    segment_pos = lax.axis_index("segment")
    last = segment_count - 1
    current = jnp.transpose(features[0], (0, 2, 1, 3))
    params = jnp.stack([norm_gain[0], norm_shift[0]], axis=2)[..., None]
    for step_no in range(STEPS):
        arrived = from_behind(current, "segment", 1)
        noise_local = lax.cond(
            segment_pos == last,
            lambda source: head_noise(source, head_w, head_gain, head_shift),
            lambda source: jnp.zeros(latent.shape, jnp.float32),
            current,
        )
        position = plan_pos + step_no
        sigma_now = sigma_at(position)
        sigma_next = sigma_at(position + 1)
        latent = latent + (sigma_next - sigma_now)[:, None, None, None] * noise_local
        scaled = (latent / jnp.sqrt(sigma_next * sigma_next + 1.0)[:, None, None, None]).astype(
            jnp.bfloat16
        )
        scaled_rows = jnp.transpose(scaled, (0, 2, 1, 3))
        peers = lax.axis_size("patch")
        origin = last * peers
        height = scaled_rows.shape[1]
        body = lax.ppermute(
            scaled_rows, ("segment", "patch"), [(origin + p, p) for p in range(peers)]
        )
        above = lax.ppermute(
            scaled_rows[:, height - 1 :],
            ("segment", "patch"),
            [(origin + p, p + 1) for p in range(peers - 1)],
        )
        below = lax.ppermute(
            scaled_rows[:, :1], ("segment", "patch"), [(origin + p, p - 1) for p in range(1, peers)]
        )
        entry_rows = conv_valid(
            jnp.concatenate([above, body, below], axis=1), in_w
        ).astype(jnp.bfloat16)
        source = jnp.where(segment_pos == 0, entry_rows, arrived)
        after_one = resnet_unit(source, conv1_w, conv2_w, 0, params)
        current = lax.cond(
            blocks_used[0] >= 2,
            lambda hidden: resnet_unit(hidden, conv1_w, conv2_w, 1, params),
            lambda hidden: hidden,
            after_one,
        )
    batch_size, lat_count, height, col_count = latent.shape
    col_share = col_count // segment_count
    latent, current = lax.optimization_barrier((latent, current))
    pieces = latent.reshape(batch_size, lat_count, height, segment_count, col_share)
    pieces = jnp.transpose(pieces, (3, 0, 1, 2, 4)).reshape(segment_count, -1, 128)
    latent_part = scatter_from_last(pieces).reshape(batch_size, lat_count, height, col_share)
    return (latent_part, jnp.transpose(current, (0, 2, 1, 3))[None])


def solution(mesh):
    placed = (
        P("segment", None, None, "patch", None),
        P(None, None, "patch", None),
        P(),
        P("segment"),
        P("segment", None, None, None, None),
        P("segment", None, None, None, None),
        P("segment", None, None, None),
        P("segment", None, None, None),
        P(),
        P(),
        P(),
        P(),
    )
    return jax.shard_map(
        per_device,
        mesh=mesh,
        in_specs=placed,
        out_specs=(P(None, None, "patch", "segment"), P("segment", None, None, "patch", None)),
        check_vma=False,
    )
```

```python
import jax
import jax.numpy as jnp
from jax import lax
from jax.sharding import PartitionSpec as P
from jax.experimental import pallas as pl
from jax.experimental.pallas import tpu as pltpu

GROUPS = 32
STEPS = 2
SCHED = 12


epsilon = 1e-05
sigma_top = 3.0
sigma_low = 0.1
rho_power = 7.0


def with_halo(block, sides, width):
    for axis, dim in sides:
        count = lax.axis_size(axis)
        forward = [(i, i + 1) for i in range(count - 1)]
        backward = [(target, source) for source, target in forward]
        low = lax.ppermute(
            lax.slice_in_dim(block, block.shape[dim] - width, None, axis=dim), axis, forward
        )
        high = lax.ppermute(lax.slice_in_dim(block, 0, width, axis=dim), axis, backward)
        block = jnp.concatenate([low, block, high], axis=dim)
    return block


def from_behind(shard, axis, by):
    devices = lax.axis_size(axis)
    pairs = [(i, i + by) for i in range(devices) if 0 <= i + by < devices]
    return lax.ppermute(shard, axis, pairs)


def broadcast(shard, axis, root):
    mine = lax.axis_index(axis) == root
    return lax.psum(jnp.where(mine, shard, jnp.zeros_like(shard)), axis)


def sigma_at(position):
    fraction = position.astype(jnp.float32) / (SCHED - 1)
    top_root = sigma_top ** (1.0 / rho_power)
    low_root = sigma_low ** (1.0 / rho_power)
    return (top_root + fraction * (low_root - top_root)) ** rho_power


def exchange_kernel(
    peers, x_ref, top_ref, bot_ref, o_ref, lo_ref, hi_ref, send_sem, recv_sem, row_send, row_recv
):
    me = lax.axis_index("patch")
    seg = lax.axis_index("segment")
    mesh_ids = pl.DeviceIdType.MESH
    barrier = pltpu.get_barrier_semaphore()
    for dist in range(1, peers):
        pl.semaphore_signal(
            barrier, 1, device_id=(seg, lax.rem(me + dist, peers)), device_id_type=mesh_ids
        )
    pl.semaphore_wait(barrier, peers - 1)
    down = pltpu.make_async_remote_copy(
        src_ref=bot_ref,
        dst_ref=lo_ref,
        send_sem=row_send.at[0],
        recv_sem=row_recv.at[0],
        device_id=(seg, jnp.minimum(me + 1, peers - 1)),
        device_id_type=mesh_ids,
    )
    up = pltpu.make_async_remote_copy(
        src_ref=top_ref,
        dst_ref=hi_ref,
        send_sem=row_send.at[1],
        recv_sem=row_recv.at[1],
        device_id=(seg, jnp.maximum(me - 1, 0)),
        device_id_type=mesh_ids,
    )

    @pl.when(me < peers - 1)
    def _():
        down.start()

    @pl.when(me > 0)
    def _():
        up.start()

    copies = []
    for dist in range(1, peers):
        copy = pltpu.make_async_remote_copy(
            src_ref=x_ref,
            dst_ref=o_ref.at[me],
            send_sem=send_sem.at[dist],
            recv_sem=recv_sem.at[dist],
            device_id=(seg, lax.rem(me + dist, peers)),
            device_id_type=mesh_ids,
        )
        copy.start()
        copies.append(copy)
    o_ref[me] = x_ref[...]

    @pl.when(me == 0)
    def _():
        lo_ref[...] = jnp.zeros(lo_ref.shape, lo_ref.dtype)

    @pl.when(me == peers - 1)
    def _():
        hi_ref[...] = jnp.zeros(hi_ref.shape, hi_ref.dtype)

    for copy in copies:
        copy.wait()

    @pl.when(me < peers - 1)
    def _():
        down.wait_send()
        up.wait_recv()

    @pl.when(me > 0)
    def _():
        up.wait_send()
        down.wait_recv()


def exchange_patch(packed, top, bottom):
    peers = lax.axis_size("patch")
    vmem = pl.BlockSpec(memory_space=pltpu.VMEM)
    return pl.pallas_call(
        lambda *refs: exchange_kernel(peers, *refs),
        out_shape=(
            jax.ShapeDtypeStruct((peers,) + packed.shape, packed.dtype),
            jax.ShapeDtypeStruct(top.shape, top.dtype),
            jax.ShapeDtypeStruct(top.shape, top.dtype),
        ),
        in_specs=[vmem] * 3,
        out_specs=(vmem, vmem, vmem),
        scratch_shapes=[
            pltpu.SemaphoreType.DMA((peers,)),
            pltpu.SemaphoreType.DMA((peers,)),
            pltpu.SemaphoreType.DMA((2,)),
            pltpu.SemaphoreType.DMA((2,)),
        ],
        compiler_params=pltpu.CompilerParams(
            collective_id=0 if top.dtype == jnp.bfloat16 else 1, has_side_effects=True
        ),
        name="exchange_stats_rows",
    )(packed, top, bottom)


def group_moments(values, rows):
    batch_size, height, chan_count, col_count = values.shape
    grouped = values.reshape(batch_size, height, GROUPS, chan_count // GROUPS, col_count)
    local_count = chan_count // GROUPS * height * col_count
    peers = lax.axis_size("patch")
    local_sum = jnp.sum(grouped, axis=(1, 3, 4))
    local_center = local_sum / local_count
    local_dev = jnp.sum(
        jnp.square(grouped - local_center[:, None, :, None, None]), axis=(1, 3, 4)
    )
    flat = jnp.concatenate([local_sum.reshape(-1), local_dev.reshape(-1)])
    width = 128 * ((flat.shape[0] + 127) // 128)
    packed = jnp.pad(flat, (0, width - flat.shape[0]))[None]
    every, low, high = exchange_patch(packed, rows[:, 0], rows[:, height - 1])
    every = every.reshape(peers, width)
    half = batch_size * GROUPS
    sums = every[:, :half].reshape(peers, batch_size, GROUPS)
    devs = every[:, half : 2 * half].reshape(peers, batch_size, GROUPS)
    cell_count = local_count * peers
    center = jnp.sum(sums, axis=0) / cell_count
    between = jnp.sum(jnp.square(sums / local_count - center[None]), axis=0) * local_count
    spread = (jnp.sum(devs, axis=0) + between) / cell_count
    return (center, jnp.sqrt(spread + epsilon)), low, high


def act_with_rows(values, rows, gain, shift):
    moments, low, high = group_moments(values, rows)
    full = jnp.concatenate(
        [low[:, None].astype(jnp.float32), values, high[:, None].astype(jnp.float32)], axis=1
    )
    act = norm_silu(full, moments, gain, shift)
    me = lax.axis_index("patch")
    row = lax.broadcasted_iota(jnp.int32, (1, full.shape[1], 1, 1), 1)
    pad = ((row == 0) & (me == 0)) | ((row == full.shape[1] - 1) & (me == lax.axis_size("patch") - 1))
    return jnp.where(pad, 0.0, act).astype(jnp.bfloat16)


def scatter_kernel(count, x_ref, o_ref, send_sem, recv_sem):
    seg = lax.axis_index("segment")
    me = lax.axis_index("patch")
    last = 0
    mesh_ids = pl.DeviceIdType.MESH
    barrier = pltpu.get_barrier_semaphore()

    @pl.when(seg == last)
    def _():
        for target in range(1, count):
            pl.semaphore_signal(barrier, 1, device_id=(target, me), device_id_type=mesh_ids)
        pl.semaphore_wait(barrier, count - 1)
        copies = []
        for target in range(1, count):
            copy = pltpu.make_async_remote_copy(
                src_ref=x_ref.at[target],
                dst_ref=o_ref,
                send_sem=send_sem.at[target],
                recv_sem=recv_sem.at[0],
                device_id=(target, me),
                device_id_type=mesh_ids,
            )
            copy.start()
            copies.append(copy)
        o_ref[...] = x_ref[last]
        for copy in copies:
            copy.wait_send()

    @pl.when(seg != last)
    def _():
        pl.semaphore_signal(barrier, 1, device_id=(last, me), device_id_type=mesh_ids)
        pl.semaphore_wait(barrier, 1)
        pltpu.make_async_remote_copy(
            src_ref=x_ref.at[0],
            dst_ref=o_ref,
            send_sem=send_sem.at[0],
            recv_sem=recv_sem.at[0],
            device_id=(last, me),
            device_id_type=mesh_ids,
        ).wait_recv()


def scatter_from_last(pieces):
    count = lax.axis_size("segment")
    vmem = pl.BlockSpec(memory_space=pltpu.VMEM)
    return pl.pallas_call(
        lambda *refs: scatter_kernel(count, *refs),
        out_shape=jax.ShapeDtypeStruct(pieces.shape[1:], pieces.dtype),
        in_specs=[vmem],
        out_specs=vmem,
        scratch_shapes=[pltpu.SemaphoreType.DMA((count,)), pltpu.SemaphoreType.DMA((1,))],
        compiler_params=pltpu.CompilerParams(collective_id=2, has_side_effects=True),
        name="scatter_latent_columns",
    )(pieces)


def norm_silu(values, moments, gain, shift):
    center, root_spread = moments
    batch_size, height, chan_count, col_count = values.shape
    grouped = values.reshape(batch_size, height, GROUPS, chan_count // GROUPS, col_count)
    normed = (
        (grouped - center[:, None, :, None, None]) / root_spread[:, None, :, None, None]
    ).reshape(values.shape)
    normed = normed * gain[None, None, :, None] + shift[None, None, :, None]
    return jax.nn.silu(normed)


def conv_kernel(x_ref, w_ref, o_ref):
    batch, rows = o_ref.shape[0], o_ref.shape[1]
    for b in range(batch):
        for r in range(rows):
            acc = None
            for tap in range(9):
                part = jnp.dot(
                    w_ref[tap], x_ref[tap % 3, b, r + tap // 3], preferred_element_type=jnp.float32
                )
                acc = part if acc is None else acc + part
            o_ref[b, r] = acc


def fused_kernel(flags_ref, vals_ref, lo_ref, hi_ref, stat_ref, par_ref, w_ref, *rest):
    if len(rest) == 3:
        res_ref, o_ref, act_ref = rest
    else:
        res_ref = None
        o_ref, act_ref = rest
    rows, chans, cols = vals_ref.shape
    mean = stat_ref[0]
    std = stat_ref[1]
    gain = par_ref[0]
    shift = par_ref[1]
    col = lax.broadcasted_iota(jnp.int32, (chans, cols), 1)

    def put(slot, values, keep):
        normed = (values.astype(jnp.float32) - mean) / std * gain + shift
        act = normed / (1.0 + jnp.exp(-normed))
        act = jnp.where(keep, act, 0.0).astype(jnp.bfloat16).astype(jnp.float32)
        act_ref[slot, 1] = act.astype(jnp.bfloat16)
        left = jnp.where(col == 0, 0.0, pltpu.roll(act, 1, 1))
        act_ref[slot, 0] = left.astype(jnp.bfloat16)
        right = jnp.where(col == cols - 1, 0.0, pltpu.roll(act, cols - 1, 1))
        act_ref[slot, 2] = right.astype(jnp.bfloat16)

    put(0, lo_ref[...], flags_ref[0] > 0)
    for r in range(rows):
        put(r + 1, vals_ref[r], True)
    put(rows + 1, hi_ref[...], flags_ref[1] > 0)
    for r in range(rows):
        acc = None
        for tap in range(9):
            part = jnp.dot(
                w_ref[tap], act_ref[r + tap // 3, tap % 3], preferred_element_type=jnp.float32
            )
            acc = part if acc is None else acc + part
        if res_ref is not None:
            acc = res_ref[r].astype(jnp.float32) + acc
        o_ref[r] = acc.astype(o_ref.dtype)


def norm_conv(values, moments, low, high, params, norm_no, weights, block, residual=None):
    batch, rows, chans, cols = values.shape
    outs = weights.shape[-2]
    center, root_spread = moments
    per_group = chans // GROUPS
    stats_c = jnp.repeat(jnp.stack([center, root_spread], axis=1), per_group, axis=2)[..., None]
    me = lax.axis_index("patch")
    flags = jnp.stack([me > 0, me < lax.axis_size("patch") - 1]).astype(jnp.int32)
    flops = 2 * 9 * batch * rows * cols * chans * outs
    row_spec = pl.BlockSpec((None, chans, cols), lambda b: (b, 0, 0))
    block_spec = pl.BlockSpec((None, rows, chans, cols), lambda b: (b, 0, 0, 0))
    operands = [flags, values, low, high, stats_c, params, weights]
    in_specs = [
        pl.BlockSpec(memory_space=pltpu.SMEM),
        block_spec,
        row_spec,
        row_spec,
        pl.BlockSpec((None, 2, chans, 1), lambda b: (b, 0, 0, 0)),
        pl.BlockSpec((None, None, 2, chans, 1), lambda b: (block, norm_no, 0, 0, 0)),
        pl.BlockSpec((None, None) + weights.shape[2:], lambda b: (0, block, 0, 0, 0)),
    ]
    out_dtype = jnp.float32
    if residual is not None:
        operands.append(residual)
        in_specs.append(block_spec)
        out_dtype = residual.dtype
    return pl.pallas_call(
        fused_kernel,
        grid=(batch,),
        out_shape=jax.ShapeDtypeStruct((batch, rows, outs, cols), out_dtype),
        in_specs=in_specs,
        out_specs=pl.BlockSpec((None, rows, outs, cols), lambda b: (b, 0, 0, 0)),
        scratch_shapes=[pltpu.VMEM((rows + 2, 3, chans, cols), jnp.bfloat16)],
        cost_estimate=pl.CostEstimate(
            flops=flops,
            transcendentals=batch * (rows + 2) * chans * cols,
            bytes_accessed=values.size * values.dtype.itemsize + 9 * chans * outs * 2 + batch * rows * outs * cols * 4,
        ),
        name="norm_conv3x3_rows",
    )(*operands)


def conv_valid(rows_in, kernel):
    padded = jnp.pad(rows_in, ((0, 0), (0, 0), (0, 0), (1, 1)))
    height = rows_in.shape[1] - 2
    col_count = rows_in.shape[3]
    accum = jnp.zeros((rows_in.shape[0], height, kernel.shape[1], col_count), jnp.float32)
    for tap_no in range(9):
        row_off, col_off = (tap_no // 3, tap_no % 3)
        window = padded[:, row_off : row_off + height, :, col_off : col_off + col_count]
        accum = accum + jnp.einsum(
            "oi,bhiw->bhow", kernel[tap_no], window, preferred_element_type=jnp.float32
        )
    return accum


def resnet_unit(hidden, conv1_w, conv2_w, block, params):
    moments, low, high = group_moments(hidden.astype(jnp.float32), hidden)
    middle = norm_conv(hidden, moments, low, high, params, 0, conv1_w, block)
    moments, low, high = group_moments(middle, middle)
    return norm_conv(middle, moments, low, high, params, 1, conv2_w, block, residual=hidden)


def head_noise(source, head_w, head_gain, head_shift):
    head_input = act_with_rows(source.astype(jnp.float32), source, head_gain, head_shift)
    return jnp.transpose(conv_valid(head_input, head_w), (0, 2, 1, 3))


def with_rows(values):
    return with_halo(values, (("patch", 1),), 1)


def per_device(
    features,
    latent,
    plan_pos,
    blocks_used,
    conv1_w,
    conv2_w,
    norm_gain,
    norm_shift,
    in_w,
    head_w,
    head_gain,
    head_shift,
):
    segment_count = lax.axis_size("segment")
    segment_pos = lax.axis_index("segment")
    last = segment_count - 1
    current = jnp.transpose(features[0], (0, 2, 1, 3))
    params = jnp.stack([norm_gain[0], norm_shift[0]], axis=2)[..., None]
    for step_no in range(STEPS):
        arrived = from_behind(current, "segment", 1)
        noise_local = lax.cond(
            segment_pos == last,
            lambda source: head_noise(source, head_w, head_gain, head_shift),
            lambda source: jnp.zeros(latent.shape, jnp.float32),
            current,
        )
        position = plan_pos + step_no
        sigma_now = sigma_at(position)
        sigma_next = sigma_at(position + 1)
        latent = latent + (sigma_next - sigma_now)[:, None, None, None] * noise_local
        scaled = (latent / jnp.sqrt(sigma_next * sigma_next + 1.0)[:, None, None, None]).astype(
            jnp.bfloat16
        )
        scaled_rows = jnp.transpose(scaled, (0, 2, 1, 3))
        peers = lax.axis_size("patch")
        origin = last * peers
        height = scaled_rows.shape[1]
        body = lax.ppermute(
            scaled_rows, ("segment", "patch"), [(origin + p, p) for p in range(peers)]
        )
        above = lax.ppermute(
            scaled_rows[:, height - 1 :],
            ("segment", "patch"),
            [(origin + p, p + 1) for p in range(peers - 1)],
        )
        below = lax.ppermute(
            scaled_rows[:, :1], ("segment", "patch"), [(origin + p, p - 1) for p in range(1, peers)]
        )
        entry_rows = conv_valid(
            jnp.concatenate([above, body, below], axis=1), in_w
        ).astype(jnp.bfloat16)
        if step_no == STEPS - 1:
            latent_first = lax.ppermute(
                latent, ("segment", "patch"), [(origin + p, p) for p in range(peers)]
            )
        source = jnp.where(segment_pos == 0, entry_rows, arrived)
        after_one = resnet_unit(source, conv1_w, conv2_w, 0, params)
        current = lax.cond(
            blocks_used[0] >= 2,
            lambda hidden: resnet_unit(hidden, conv1_w, conv2_w, 1, params),
            lambda hidden: hidden,
            after_one,
        )
    batch_size, lat_count, height, col_count = latent.shape
    col_share = col_count // segment_count
    latent, current = lax.optimization_barrier((latent_first, current))
    pieces = latent.reshape(batch_size, lat_count, height, segment_count, col_share)
    pieces = jnp.transpose(pieces, (3, 0, 1, 2, 4)).reshape(segment_count, -1, 128)
    latent_part = scatter_from_last(pieces).reshape(batch_size, lat_count, height, col_share)
    return (latent_part, jnp.transpose(current, (0, 2, 1, 3))[None])


def solution(mesh):
    placed = (
        P("segment", None, None, "patch", None),
        P(None, None, "patch", None),
        P(),
        P("segment"),
        P("segment", None, None, None, None),
        P("segment", None, None, None, None),
        P("segment", None, None, None),
        P("segment", None, None, None),
        P(),
        P(),
        P(),
        P(),
    )
    return jax.shard_map(
        per_device,
        mesh=mesh,
        in_specs=placed,
        out_specs=(P(None, None, "patch", "segment"), P("segment", None, None, "patch", None)),
        check_vma=False,
    )
```

```python
import jax
import jax.numpy as jnp
from jax import lax
from jax.sharding import PartitionSpec as P
from jax.experimental import pallas as pl
from jax.experimental.pallas import tpu as pltpu

GROUPS = 32
STEPS = 2
SCHED = 12


epsilon = 1e-05
sigma_top = 3.0
sigma_low = 0.1
rho_power = 7.0


def with_halo(block, sides, width):
    for axis, dim in sides:
        count = lax.axis_size(axis)
        forward = [(i, i + 1) for i in range(count - 1)]
        backward = [(target, source) for source, target in forward]
        low = lax.ppermute(
            lax.slice_in_dim(block, block.shape[dim] - width, None, axis=dim), axis, forward
        )
        high = lax.ppermute(lax.slice_in_dim(block, 0, width, axis=dim), axis, backward)
        block = jnp.concatenate([low, block, high], axis=dim)
    return block


def from_behind(shard, axis, by):
    devices = lax.axis_size(axis)
    pairs = [(i, i + by) for i in range(devices) if 0 <= i + by < devices]
    return lax.ppermute(shard, axis, pairs)


def broadcast(shard, axis, root):
    mine = lax.axis_index(axis) == root
    return lax.psum(jnp.where(mine, shard, jnp.zeros_like(shard)), axis)


def sigma_at(position):
    fraction = position.astype(jnp.float32) / (SCHED - 1)
    top_root = sigma_top ** (1.0 / rho_power)
    low_root = sigma_low ** (1.0 / rho_power)
    return (top_root + fraction * (low_root - top_root)) ** rho_power


def exchange_kernel(
    peers, x_ref, top_ref, bot_ref, o_ref, lo_ref, hi_ref, send_sem, recv_sem, row_send, row_recv
):
    me = lax.axis_index("patch")
    seg = lax.axis_index("segment")
    mesh_ids = pl.DeviceIdType.MESH
    barrier = pltpu.get_barrier_semaphore()
    for dist in range(1, peers):
        pl.semaphore_signal(
            barrier, 1, device_id=(seg, lax.rem(me + dist, peers)), device_id_type=mesh_ids
        )
    pl.semaphore_wait(barrier, peers - 1)
    down = pltpu.make_async_remote_copy(
        src_ref=bot_ref,
        dst_ref=lo_ref,
        send_sem=row_send.at[0],
        recv_sem=row_recv.at[0],
        device_id=(seg, jnp.minimum(me + 1, peers - 1)),
        device_id_type=mesh_ids,
    )
    up = pltpu.make_async_remote_copy(
        src_ref=top_ref,
        dst_ref=hi_ref,
        send_sem=row_send.at[1],
        recv_sem=row_recv.at[1],
        device_id=(seg, jnp.maximum(me - 1, 0)),
        device_id_type=mesh_ids,
    )

    @pl.when(me < peers - 1)
    def _():
        down.start()

    @pl.when(me > 0)
    def _():
        up.start()

    copies = []
    for dist in range(1, peers):
        copy = pltpu.make_async_remote_copy(
            src_ref=x_ref,
            dst_ref=o_ref.at[me],
            send_sem=send_sem.at[dist],
            recv_sem=recv_sem.at[dist],
            device_id=(seg, lax.rem(me + dist, peers)),
            device_id_type=mesh_ids,
        )
        copy.start()
        copies.append(copy)
    o_ref[me] = x_ref[...]

    @pl.when(me == 0)
    def _():
        lo_ref[...] = jnp.zeros(lo_ref.shape, lo_ref.dtype)

    @pl.when(me == peers - 1)
    def _():
        hi_ref[...] = jnp.zeros(hi_ref.shape, hi_ref.dtype)

    for copy in copies:
        copy.wait()

    @pl.when(me < peers - 1)
    def _():
        down.wait_send()
        up.wait_recv()

    @pl.when(me > 0)
    def _():
        up.wait_send()
        down.wait_recv()


def exchange_patch(packed, top, bottom, kernel_id=None):
    peers = lax.axis_size("patch")
    vmem = pl.BlockSpec(memory_space=pltpu.VMEM)
    return pl.pallas_call(
        lambda *refs: exchange_kernel(peers, *refs),
        out_shape=(
            jax.ShapeDtypeStruct((peers,) + packed.shape, packed.dtype),
            jax.ShapeDtypeStruct(top.shape, top.dtype),
            jax.ShapeDtypeStruct(top.shape, top.dtype),
        ),
        in_specs=[vmem] * 3,
        out_specs=(vmem, vmem, vmem),
        scratch_shapes=[
            pltpu.SemaphoreType.DMA((peers,)),
            pltpu.SemaphoreType.DMA((peers,)),
            pltpu.SemaphoreType.DMA((2,)),
            pltpu.SemaphoreType.DMA((2,)),
        ],
        compiler_params=pltpu.CompilerParams(
            collective_id=(0 if top.dtype == jnp.bfloat16 else 1) if kernel_id is None else kernel_id,
            has_side_effects=True,
        ),
        name="exchange_stats_rows",
    )(packed, top, bottom)


def local_pack(values):
    batch_size, height, chan_count, col_count = values.shape
    grouped = values.reshape(batch_size, height, GROUPS, chan_count // GROUPS, col_count)
    local_count = chan_count // GROUPS * height * col_count
    local_sum = jnp.sum(grouped, axis=(1, 3, 4))
    local_center = local_sum / local_count
    local_dev = jnp.sum(
        jnp.square(grouped - local_center[:, None, :, None, None]), axis=(1, 3, 4)
    )
    flat = jnp.concatenate([local_sum.reshape(-1), local_dev.reshape(-1)])
    width = 128 * ((flat.shape[0] + 127) // 128)
    return jnp.pad(flat, (0, width - flat.shape[0]))


def combine_stats(every, batch_size, local_count):
    peers = every.shape[0]
    half = batch_size * GROUPS
    sums = every[:, :half].reshape(peers, batch_size, GROUPS)
    devs = every[:, half : 2 * half].reshape(peers, batch_size, GROUPS)
    cell_count = local_count * peers
    center = jnp.sum(sums, axis=0) / cell_count
    between = jnp.sum(jnp.square(sums / local_count - center[None]), axis=0) * local_count
    spread = (jnp.sum(devs, axis=0) + between) / cell_count
    return (center, jnp.sqrt(spread + epsilon))


def group_moments(values, rows):
    batch_size, height, chan_count, col_count = values.shape
    packed = local_pack(values)
    every, low, high = exchange_patch(packed[None], rows[:, 0], rows[:, height - 1])
    every = every.reshape(lax.axis_size("patch"), packed.shape[0])
    local_count = chan_count // GROUPS * height * col_count
    return combine_stats(every, batch_size, local_count), low, high


def group_moments_pair(rows_a, rows_b):
    batch_size, height, chan_count, col_count = rows_a.shape
    pack_a = local_pack(rows_a.astype(jnp.float32))
    pack_b = local_pack(rows_b.astype(jnp.float32))
    width = pack_a.shape[0]
    top = jnp.concatenate([rows_a[:, 0], rows_b[:, 0]], axis=0)
    bottom = jnp.concatenate([rows_a[:, height - 1], rows_b[:, height - 1]], axis=0)
    every, low, high = exchange_patch(
        jnp.concatenate([pack_a, pack_b])[None], top, bottom, kernel_id=3
    )
    every = every.reshape(lax.axis_size("patch"), 2 * width)
    local_count = chan_count // GROUPS * height * col_count
    first = (
        combine_stats(every[:, :width], batch_size, local_count),
        low[:batch_size],
        high[:batch_size],
    )
    second = (
        combine_stats(every[:, width:], batch_size, local_count),
        low[batch_size:],
        high[batch_size:],
    )
    return first, second


def act_with_rows(values, rows, gain, shift, shared=None):
    moments, low, high = group_moments(values, rows) if shared is None else shared
    full = jnp.concatenate(
        [low[:, None].astype(jnp.float32), values, high[:, None].astype(jnp.float32)], axis=1
    )
    act = norm_silu(full, moments, gain, shift)
    me = lax.axis_index("patch")
    row = lax.broadcasted_iota(jnp.int32, (1, full.shape[1], 1, 1), 1)
    pad = ((row == 0) & (me == 0)) | ((row == full.shape[1] - 1) & (me == lax.axis_size("patch") - 1))
    return jnp.where(pad, 0.0, act).astype(jnp.bfloat16)


def scatter_kernel(count, x_ref, o_ref, send_sem, recv_sem):
    seg = lax.axis_index("segment")
    me = lax.axis_index("patch")
    last = count - 1
    mesh_ids = pl.DeviceIdType.MESH
    barrier = pltpu.get_barrier_semaphore()

    @pl.when(seg == last)
    def _():
        for target in range(last):
            pl.semaphore_signal(barrier, 1, device_id=(target, me), device_id_type=mesh_ids)
        pl.semaphore_wait(barrier, last)
        copies = []
        for target in range(last):
            copy = pltpu.make_async_remote_copy(
                src_ref=x_ref.at[target],
                dst_ref=o_ref,
                send_sem=send_sem.at[target],
                recv_sem=recv_sem.at[0],
                device_id=(target, me),
                device_id_type=mesh_ids,
            )
            copy.start()
            copies.append(copy)
        o_ref[...] = x_ref[last]
        for copy in copies:
            copy.wait_send()

    @pl.when(seg != last)
    def _():
        pl.semaphore_signal(barrier, 1, device_id=(last, me), device_id_type=mesh_ids)
        pl.semaphore_wait(barrier, 1)
        pltpu.make_async_remote_copy(
            src_ref=x_ref.at[0],
            dst_ref=o_ref,
            send_sem=send_sem.at[0],
            recv_sem=recv_sem.at[0],
            device_id=(last, me),
            device_id_type=mesh_ids,
        ).wait_recv()


def scatter_from_last(pieces):
    count = lax.axis_size("segment")
    vmem = pl.BlockSpec(memory_space=pltpu.VMEM)
    return pl.pallas_call(
        lambda *refs: scatter_kernel(count, *refs),
        out_shape=jax.ShapeDtypeStruct(pieces.shape[1:], pieces.dtype),
        in_specs=[vmem],
        out_specs=vmem,
        scratch_shapes=[pltpu.SemaphoreType.DMA((count,)), pltpu.SemaphoreType.DMA((1,))],
        compiler_params=pltpu.CompilerParams(collective_id=2, has_side_effects=True),
        name="scatter_latent_columns",
    )(pieces)


def norm_silu(values, moments, gain, shift):
    center, root_spread = moments
    batch_size, height, chan_count, col_count = values.shape
    grouped = values.reshape(batch_size, height, GROUPS, chan_count // GROUPS, col_count)
    normed = (
        (grouped - center[:, None, :, None, None]) / root_spread[:, None, :, None, None]
    ).reshape(values.shape)
    normed = normed * gain[None, None, :, None] + shift[None, None, :, None]
    return jax.nn.silu(normed)


def conv_kernel(x_ref, w_ref, o_ref):
    batch, rows = o_ref.shape[0], o_ref.shape[1]
    for b in range(batch):
        for r in range(rows):
            acc = None
            for tap in range(9):
                part = jnp.dot(
                    w_ref[tap], x_ref[tap % 3, b, r + tap // 3], preferred_element_type=jnp.float32
                )
                acc = part if acc is None else acc + part
            o_ref[b, r] = acc


def fused_kernel(flags_ref, vals_ref, lo_ref, hi_ref, stat_ref, par_ref, w_ref, *rest):
    if len(rest) == 3:
        res_ref, o_ref, act_ref = rest
    else:
        res_ref = None
        o_ref, act_ref = rest
    rows, chans, cols = vals_ref.shape
    mean = stat_ref[0]
    std = stat_ref[1]
    gain = par_ref[0]
    shift = par_ref[1]
    col = lax.broadcasted_iota(jnp.int32, (chans, cols), 1)

    def put(slot, values, keep):
        normed = (values.astype(jnp.float32) - mean) / std * gain + shift
        act = normed / (1.0 + jnp.exp(-normed))
        act = jnp.where(keep, act, 0.0).astype(jnp.bfloat16).astype(jnp.float32)
        act_ref[slot, 1] = act.astype(jnp.bfloat16)
        left = jnp.where(col == 0, 0.0, pltpu.roll(act, 1, 1))
        act_ref[slot, 0] = left.astype(jnp.bfloat16)
        right = jnp.where(col == cols - 1, 0.0, pltpu.roll(act, cols - 1, 1))
        act_ref[slot, 2] = right.astype(jnp.bfloat16)

    put(0, lo_ref[...], flags_ref[0] > 0)
    for r in range(rows):
        put(r + 1, vals_ref[r], True)
    put(rows + 1, hi_ref[...], flags_ref[1] > 0)
    for r in range(rows):
        acc = None
        for tap in range(9):
            part = jnp.dot(
                w_ref[tap], act_ref[r + tap // 3, tap % 3], preferred_element_type=jnp.float32
            )
            acc = part if acc is None else acc + part
        if res_ref is not None:
            acc = res_ref[r].astype(jnp.float32) + acc
        o_ref[r] = acc.astype(o_ref.dtype)


def norm_conv(values, moments, low, high, params, norm_no, weights, block, residual=None):
    batch, rows, chans, cols = values.shape
    outs = weights.shape[-2]
    center, root_spread = moments
    per_group = chans // GROUPS
    stats_c = jnp.repeat(jnp.stack([center, root_spread], axis=1), per_group, axis=2)[..., None]
    me = lax.axis_index("patch")
    flags = jnp.stack([me > 0, me < lax.axis_size("patch") - 1]).astype(jnp.int32)
    flops = 2 * 9 * batch * rows * cols * chans * outs
    row_spec = pl.BlockSpec((None, chans, cols), lambda b: (b, 0, 0))
    block_spec = pl.BlockSpec((None, rows, chans, cols), lambda b: (b, 0, 0, 0))
    operands = [flags, values, low, high, stats_c, params, weights]
    in_specs = [
        pl.BlockSpec(memory_space=pltpu.SMEM),
        block_spec,
        row_spec,
        row_spec,
        pl.BlockSpec((None, 2, chans, 1), lambda b: (b, 0, 0, 0)),
        pl.BlockSpec((None, None, 2, chans, 1), lambda b: (block, norm_no, 0, 0, 0)),
        pl.BlockSpec((None, None) + weights.shape[2:], lambda b: (0, block, 0, 0, 0)),
    ]
    out_dtype = jnp.float32
    if residual is not None:
        operands.append(residual)
        in_specs.append(block_spec)
        out_dtype = residual.dtype
    return pl.pallas_call(
        fused_kernel,
        grid=(batch,),
        out_shape=jax.ShapeDtypeStruct((batch, rows, outs, cols), out_dtype),
        in_specs=in_specs,
        out_specs=pl.BlockSpec((None, rows, outs, cols), lambda b: (b, 0, 0, 0)),
        scratch_shapes=[pltpu.VMEM((rows + 2, 3, chans, cols), jnp.bfloat16)],
        cost_estimate=pl.CostEstimate(
            flops=flops,
            transcendentals=batch * (rows + 2) * chans * cols,
            bytes_accessed=values.size * values.dtype.itemsize + 9 * chans * outs * 2 + batch * rows * outs * cols * 4,
        ),
        name="norm_conv3x3_rows",
    )(*operands)


def conv_valid(rows_in, kernel):
    padded = jnp.pad(rows_in, ((0, 0), (0, 0), (0, 0), (1, 1)))
    height = rows_in.shape[1] - 2
    col_count = rows_in.shape[3]
    accum = jnp.zeros((rows_in.shape[0], height, kernel.shape[1], col_count), jnp.float32)
    for tap_no in range(9):
        row_off, col_off = (tap_no // 3, tap_no % 3)
        window = padded[:, row_off : row_off + height, :, col_off : col_off + col_count]
        accum = accum + jnp.einsum(
            "oi,bhiw->bhow", kernel[tap_no], window, preferred_element_type=jnp.float32
        )
    return accum


def resnet_unit(hidden, conv1_w, conv2_w, block, params, shared=None):
    if shared is None:
        shared = group_moments(hidden.astype(jnp.float32), hidden)
    moments, low, high = shared
    middle = norm_conv(hidden, moments, low, high, params, 0, conv1_w, block)
    moments, low, high = group_moments(middle, middle)
    return norm_conv(middle, moments, low, high, params, 1, conv2_w, block, residual=hidden)


def head_noise(source, head_w, head_gain, head_shift, shared=None):
    head_input = act_with_rows(source.astype(jnp.float32), source, head_gain, head_shift, shared)
    return jnp.transpose(conv_valid(head_input, head_w), (0, 2, 1, 3))


def with_rows(values):
    return with_halo(values, (("patch", 1),), 1)


def per_device(
    features,
    latent,
    plan_pos,
    blocks_used,
    conv1_w,
    conv2_w,
    norm_gain,
    norm_shift,
    in_w,
    head_w,
    head_gain,
    head_shift,
):
    segment_count = lax.axis_size("segment")
    segment_pos = lax.axis_index("segment")
    last = segment_count - 1
    current = jnp.transpose(features[0], (0, 2, 1, 3))
    params = jnp.stack([norm_gain[0], norm_shift[0]], axis=2)[..., None]
    for step_no in range(STEPS):
        arrived = from_behind(current, "segment", 1)
        if step_no == 0:
            head_shared, arrived_shared = group_moments_pair(current, arrived)
            noise_local = lax.cond(
                segment_pos == last,
                lambda source, shared: head_noise(source, head_w, head_gain, head_shift, shared),
                lambda source, shared: jnp.zeros(latent.shape, jnp.float32),
                current,
                head_shared,
            )
        else:
            noise_local = lax.cond(
                segment_pos == last,
                lambda source: head_noise(source, head_w, head_gain, head_shift),
                lambda source: jnp.zeros(latent.shape, jnp.float32),
                current,
            )
        position = plan_pos + step_no
        sigma_now = sigma_at(position)
        sigma_next = sigma_at(position + 1)
        latent = latent + (sigma_next - sigma_now)[:, None, None, None] * noise_local
        scaled = (latent / jnp.sqrt(sigma_next * sigma_next + 1.0)[:, None, None, None]).astype(
            jnp.bfloat16
        )
        scaled_rows = jnp.transpose(scaled, (0, 2, 1, 3))
        peers = lax.axis_size("patch")
        origin = last * peers
        height = scaled_rows.shape[1]
        body = lax.ppermute(
            scaled_rows, ("segment", "patch"), [(origin + p, p) for p in range(peers)]
        )
        above = lax.ppermute(
            scaled_rows[:, height - 1 :],
            ("segment", "patch"),
            [(origin + p, p + 1) for p in range(peers - 1)],
        )
        below = lax.ppermute(
            scaled_rows[:, :1], ("segment", "patch"), [(origin + p, p - 1) for p in range(1, peers)]
        )
        entry_rows = conv_valid(
            jnp.concatenate([above, body, below], axis=1), in_w
        ).astype(jnp.bfloat16)
        source = jnp.where(segment_pos == 0, entry_rows, arrived)
        if step_no == 0:
            first_shared = lax.cond(
                segment_pos == 0,
                lambda hidden, shared: group_moments(hidden.astype(jnp.float32), hidden),
                lambda hidden, shared: shared,
                source,
                arrived_shared,
            )
            after_one = resnet_unit(source, conv1_w, conv2_w, 0, params, first_shared)
        else:
            after_one = resnet_unit(source, conv1_w, conv2_w, 0, params)
        current = lax.cond(
            blocks_used[0] >= 2,
            lambda hidden: resnet_unit(hidden, conv1_w, conv2_w, 1, params),
            lambda hidden: hidden,
            after_one,
        )
    batch_size, lat_count, height, col_count = latent.shape
    col_share = col_count // segment_count
    latent, current = lax.optimization_barrier((latent, current))
    pieces = latent.reshape(batch_size, lat_count, height, segment_count, col_share)
    pieces = jnp.transpose(pieces, (3, 0, 1, 2, 4)).reshape(segment_count, -1, 128)
    latent_part = scatter_from_last(pieces).reshape(batch_size, lat_count, height, col_share)
    return (latent_part, jnp.transpose(current, (0, 2, 1, 3))[None])


def solution(mesh):
    placed = (
        P("segment", None, None, "patch", None),
        P(None, None, "patch", None),
        P(),
        P("segment"),
        P("segment", None, None, None, None),
        P("segment", None, None, None, None),
        P("segment", None, None, None),
        P("segment", None, None, None),
        P(),
        P(),
        P(),
        P(),
    )
    return jax.shard_map(
        per_device,
        mesh=mesh,
        in_specs=placed,
        out_specs=(P(None, None, "patch", "segment"), P("segment", None, None, "patch", None)),
        check_vma=False,
    )
```

```python
import jax
import jax.numpy as jnp
from jax import lax
from jax.sharding import PartitionSpec as P
from jax.experimental import pallas as pl
from jax.experimental.pallas import tpu as pltpu

GROUPS = 32
STEPS = 2
SCHED = 12


epsilon = 1e-05
sigma_top = 3.0
sigma_low = 0.1
rho_power = 7.0


def with_halo(block, sides, width):
    for axis, dim in sides:
        count = lax.axis_size(axis)
        forward = [(i, i + 1) for i in range(count - 1)]
        backward = [(target, source) for source, target in forward]
        low = lax.ppermute(
            lax.slice_in_dim(block, block.shape[dim] - width, None, axis=dim), axis, forward
        )
        high = lax.ppermute(lax.slice_in_dim(block, 0, width, axis=dim), axis, backward)
        block = jnp.concatenate([low, block, high], axis=dim)
    return block


def from_behind(shard, axis, by):
    devices = lax.axis_size(axis)
    pairs = [(i, i + by) for i in range(devices) if 0 <= i + by < devices]
    return lax.ppermute(shard, axis, pairs)


def broadcast(shard, axis, root):
    mine = lax.axis_index(axis) == root
    return lax.psum(jnp.where(mine, shard, jnp.zeros_like(shard)), axis)


def sigma_at(position):
    fraction = position.astype(jnp.float32) / (SCHED - 1)
    top_root = sigma_top ** (1.0 / rho_power)
    low_root = sigma_low ** (1.0 / rho_power)
    return (top_root + fraction * (low_root - top_root)) ** rho_power


def exchange_kernel(
    peers, x_ref, top_ref, bot_ref, o_ref, lo_ref, hi_ref, send_sem, recv_sem, row_send, row_recv
):
    me = lax.axis_index("patch")
    seg = lax.axis_index("segment")
    mesh_ids = pl.DeviceIdType.MESH
    barrier = pltpu.get_barrier_semaphore()
    for dist in range(1, peers):
        pl.semaphore_signal(
            barrier, 1, device_id=(seg, lax.rem(me + dist, peers)), device_id_type=mesh_ids
        )
    pl.semaphore_wait(barrier, peers - 1)
    down = pltpu.make_async_remote_copy(
        src_ref=bot_ref,
        dst_ref=lo_ref,
        send_sem=row_send.at[0],
        recv_sem=row_recv.at[0],
        device_id=(seg, jnp.minimum(me + 1, peers - 1)),
        device_id_type=mesh_ids,
    )
    up = pltpu.make_async_remote_copy(
        src_ref=top_ref,
        dst_ref=hi_ref,
        send_sem=row_send.at[1],
        recv_sem=row_recv.at[1],
        device_id=(seg, jnp.maximum(me - 1, 0)),
        device_id_type=mesh_ids,
    )

    @pl.when(me < peers - 1)
    def _():
        down.start()

    @pl.when(me > 0)
    def _():
        up.start()

    copies = []
    for dist in range(1, peers):
        copy = pltpu.make_async_remote_copy(
            src_ref=x_ref,
            dst_ref=o_ref.at[me],
            send_sem=send_sem.at[dist],
            recv_sem=recv_sem.at[dist],
            device_id=(seg, lax.rem(me + dist, peers)),
            device_id_type=mesh_ids,
        )
        copy.start()
        copies.append(copy)
    o_ref[me] = x_ref[...]

    @pl.when(me == 0)
    def _():
        lo_ref[...] = jnp.zeros(lo_ref.shape, lo_ref.dtype)

    @pl.when(me == peers - 1)
    def _():
        hi_ref[...] = jnp.zeros(hi_ref.shape, hi_ref.dtype)

    for copy in copies:
        copy.wait()

    @pl.when(me < peers - 1)
    def _():
        down.wait_send()
        up.wait_recv()

    @pl.when(me > 0)
    def _():
        up.wait_send()
        down.wait_recv()


def exchange_patch(packed, top, bottom):
    peers = lax.axis_size("patch")
    vmem = pl.BlockSpec(memory_space=pltpu.VMEM)
    return pl.pallas_call(
        lambda *refs: exchange_kernel(peers, *refs),
        out_shape=(
            jax.ShapeDtypeStruct((peers,) + packed.shape, packed.dtype),
            jax.ShapeDtypeStruct(top.shape, top.dtype),
            jax.ShapeDtypeStruct(top.shape, top.dtype),
        ),
        in_specs=[vmem] * 3,
        out_specs=(vmem, vmem, vmem),
        scratch_shapes=[
            pltpu.SemaphoreType.DMA((peers,)),
            pltpu.SemaphoreType.DMA((peers,)),
            pltpu.SemaphoreType.DMA((2,)),
            pltpu.SemaphoreType.DMA((2,)),
        ],
        compiler_params=pltpu.CompilerParams(
            collective_id=0 if top.dtype == jnp.bfloat16 else 1, has_side_effects=True
        ),
        name="exchange_stats_rows",
    )(packed, top, bottom)


def group_moments(values, rows):
    batch_size, height, chan_count, col_count = values.shape
    grouped = values.reshape(batch_size, height, GROUPS, chan_count // GROUPS, col_count)
    local_count = chan_count // GROUPS * height * col_count
    peers = lax.axis_size("patch")
    local_sum = jnp.sum(grouped, axis=(1, 3, 4))
    local_center = local_sum / local_count
    local_dev = jnp.sum(
        jnp.square(grouped - local_center[:, None, :, None, None]), axis=(1, 3, 4)
    )
    flat = jnp.concatenate([local_sum.reshape(-1), local_dev.reshape(-1)])
    width = 128 * ((flat.shape[0] + 127) // 128)
    packed = jnp.pad(flat, (0, width - flat.shape[0]))[None]
    every, low, high = exchange_patch(packed, rows[:, 0], rows[:, height - 1])
    every = every.reshape(peers, width)
    half = batch_size * GROUPS
    sums = every[:, :half].reshape(peers, batch_size, GROUPS)
    devs = every[:, half : 2 * half].reshape(peers, batch_size, GROUPS)
    cell_count = local_count * peers
    center = jnp.sum(sums, axis=0) / cell_count
    between = jnp.sum(jnp.square(sums / local_count - center[None]), axis=0) * local_count
    spread = (jnp.sum(devs, axis=0) + between) / cell_count
    return (center, jnp.sqrt(spread + epsilon)), low, high


def act_with_rows(values, rows, gain, shift):
    moments, low, high = group_moments(values, rows)
    full = jnp.concatenate(
        [low[:, None].astype(jnp.float32), values, high[:, None].astype(jnp.float32)], axis=1
    )
    act = norm_silu(full, moments, gain, shift)
    me = lax.axis_index("patch")
    row = lax.broadcasted_iota(jnp.int32, (1, full.shape[1], 1, 1), 1)
    pad = ((row == 0) & (me == 0)) | ((row == full.shape[1] - 1) & (me == lax.axis_size("patch") - 1))
    return jnp.where(pad, 0.0, act).astype(jnp.bfloat16)


def scatter_kernel(count, x_ref, o_ref, send_sem, recv_sem):
    seg = lax.axis_index("segment")
    me = lax.axis_index("patch")
    last = count - 1
    mesh_ids = pl.DeviceIdType.MESH
    barrier = pltpu.get_barrier_semaphore()

    @pl.when(seg == last)
    def _():
        for target in range(last):
            pl.semaphore_signal(barrier, 1, device_id=(target, me), device_id_type=mesh_ids)
        pl.semaphore_wait(barrier, last)
        copies = []
        for target in range(last):
            copy = pltpu.make_async_remote_copy(
                src_ref=x_ref.at[target],
                dst_ref=o_ref,
                send_sem=send_sem.at[target],
                recv_sem=recv_sem.at[0],
                device_id=(target, me),
                device_id_type=mesh_ids,
            )
            copy.start()
            copies.append(copy)
        o_ref[...] = x_ref[last]
        for copy in copies:
            copy.wait_send()

    @pl.when(seg != last)
    def _():
        pl.semaphore_signal(barrier, 1, device_id=(last, me), device_id_type=mesh_ids)
        pl.semaphore_wait(barrier, 1)
        pltpu.make_async_remote_copy(
            src_ref=x_ref.at[0],
            dst_ref=o_ref,
            send_sem=send_sem.at[0],
            recv_sem=recv_sem.at[0],
            device_id=(last, me),
            device_id_type=mesh_ids,
        ).wait_recv()


def scatter_from_last(pieces):
    count = lax.axis_size("segment")
    vmem = pl.BlockSpec(memory_space=pltpu.VMEM)
    return pl.pallas_call(
        lambda *refs: scatter_kernel(count, *refs),
        out_shape=jax.ShapeDtypeStruct(pieces.shape[1:], pieces.dtype),
        in_specs=[vmem],
        out_specs=vmem,
        scratch_shapes=[pltpu.SemaphoreType.DMA((count,)), pltpu.SemaphoreType.DMA((1,))],
        compiler_params=pltpu.CompilerParams(collective_id=2, has_side_effects=True),
        name="scatter_latent_columns",
    )(pieces)


def norm_silu(values, moments, gain, shift):
    center, root_spread = moments
    batch_size, height, chan_count, col_count = values.shape
    grouped = values.reshape(batch_size, height, GROUPS, chan_count // GROUPS, col_count)
    normed = (
        (grouped - center[:, None, :, None, None]) / root_spread[:, None, :, None, None]
    ).reshape(values.shape)
    normed = normed * gain[None, None, :, None] + shift[None, None, :, None]
    return jax.nn.silu(normed)


def conv_kernel(x_ref, w_ref, o_ref):
    batch, rows = o_ref.shape[0], o_ref.shape[1]
    for b in range(batch):
        for r in range(rows):
            acc = None
            for tap in range(9):
                part = jnp.dot(
                    w_ref[tap], x_ref[tap % 3, b, r + tap // 3], preferred_element_type=jnp.float32
                )
                acc = part if acc is None else acc + part
            o_ref[b, r] = acc


def fused_kernel(flags_ref, vals_ref, lo_ref, hi_ref, stat_ref, par_ref, w_ref, *rest):
    if len(rest) == 3:
        res_ref, o_ref, act_ref = rest
    else:
        res_ref = None
        o_ref, act_ref = rest
    rows, chans, cols = vals_ref.shape
    mean = stat_ref[0]
    std = stat_ref[1]
    gain = par_ref[0]
    shift = par_ref[1]
    col = lax.broadcasted_iota(jnp.int32, (chans, cols), 1)

    def put(slot, values, keep):
        normed = (values.astype(jnp.float32) - mean) / std * gain + shift
        act = normed / (1.0 + jnp.exp(-normed))
        act = jnp.where(keep, act, 0.0).astype(jnp.bfloat16).astype(jnp.float32)
        act_ref[slot, 1] = act.astype(jnp.bfloat16)
        left = jnp.where(col == 0, 0.0, pltpu.roll(act, 1, 1))
        act_ref[slot, 0] = left.astype(jnp.bfloat16)
        right = jnp.where(col == cols - 1, 0.0, pltpu.roll(act, cols - 1, 1))
        act_ref[slot, 2] = right.astype(jnp.bfloat16)

    put(0, lo_ref[...], flags_ref[0] > 0)
    for r in range(rows):
        put(r + 1, vals_ref[r], True)
    put(rows + 1, hi_ref[...], flags_ref[1] > 0)
    for r in range(rows):
        acc = None
        for tap in range(9):
            part = jnp.dot(
                w_ref[tap], act_ref[r + tap // 3, tap % 3], preferred_element_type=jnp.float32
            )
            acc = part if acc is None else acc + part
        if res_ref is not None:
            acc = res_ref[r].astype(jnp.float32) + acc
        o_ref[r] = acc.astype(o_ref.dtype)


def norm_conv(values, moments, low, high, params, norm_no, weights, block, residual=None):
    batch, rows, chans, cols = values.shape
    outs = weights.shape[-2]
    center, root_spread = moments
    per_group = chans // GROUPS
    stats_c = jnp.repeat(jnp.stack([center, root_spread], axis=1), per_group, axis=2)[..., None]
    me = lax.axis_index("patch")
    flags = jnp.stack([me > 0, me < lax.axis_size("patch") - 1]).astype(jnp.int32)
    flops = 2 * 9 * batch * rows * cols * chans * outs
    row_spec = pl.BlockSpec((None, chans, cols), lambda b: (b, 0, 0))
    block_spec = pl.BlockSpec((None, rows, chans, cols), lambda b: (b, 0, 0, 0))
    operands = [flags, values, low, high, stats_c, params, weights]
    in_specs = [
        pl.BlockSpec(memory_space=pltpu.SMEM),
        block_spec,
        row_spec,
        row_spec,
        pl.BlockSpec((None, 2, chans, 1), lambda b: (b, 0, 0, 0)),
        pl.BlockSpec((None, None, 2, chans, 1), lambda b: (block, norm_no, 0, 0, 0)),
        pl.BlockSpec((None, None) + weights.shape[2:], lambda b: (0, block, 0, 0, 0)),
    ]
    out_dtype = jnp.float32
    if residual is not None:
        operands.append(residual)
        in_specs.append(block_spec)
        out_dtype = residual.dtype
    return pl.pallas_call(
        fused_kernel,
        grid=(batch,),
        out_shape=jax.ShapeDtypeStruct((batch, rows, outs, cols), out_dtype),
        in_specs=in_specs,
        out_specs=pl.BlockSpec((None, rows, outs, cols), lambda b: (b, 0, 0, 0)),
        scratch_shapes=[pltpu.VMEM((rows + 2, 3, chans, cols), jnp.bfloat16)],
        cost_estimate=pl.CostEstimate(
            flops=flops,
            transcendentals=batch * (rows + 2) * chans * cols,
            bytes_accessed=values.size * values.dtype.itemsize + 9 * chans * outs * 2 + batch * rows * outs * cols * 4,
        ),
        name="norm_conv3x3_rows",
    )(*operands)


def conv_valid(rows_in, kernel):
    padded = jnp.pad(rows_in, ((0, 0), (0, 0), (0, 0), (1, 1)))
    height = rows_in.shape[1] - 2
    col_count = rows_in.shape[3]
    accum = jnp.zeros((rows_in.shape[0], height, kernel.shape[1], col_count), jnp.float32)
    for tap_no in range(9):
        row_off, col_off = (tap_no // 3, tap_no % 3)
        window = padded[:, row_off : row_off + height, :, col_off : col_off + col_count]
        accum = accum + jnp.einsum(
            "oi,bhiw->bhow", kernel[tap_no], window, preferred_element_type=jnp.float32
        )
    return accum


def resnet_unit(hidden, conv1_w, conv2_w, block, params):
    moments, low, high = group_moments(hidden.astype(jnp.float32), hidden)
    middle = norm_conv(hidden, moments, low, high, params, 0, conv1_w, block)
    moments, low, high = group_moments(middle, middle)
    return norm_conv(middle, moments, low, high, params, 1, conv2_w, block, residual=hidden)


def head_noise(source, head_w, head_gain, head_shift):
    head_input = act_with_rows(source.astype(jnp.float32), source, head_gain, head_shift)
    return jnp.transpose(conv_valid(head_input, head_w), (0, 2, 1, 3))


def conv_stacked(rows_in, kernel):
    padded = jnp.pad(rows_in, ((0, 0), (0, 0), (0, 0), (1, 1)))
    height = rows_in.shape[1] - 2
    col_count = rows_in.shape[3]
    windows = jnp.concatenate(
        [
            padded[:, tap // 3 : tap // 3 + height, :, tap % 3 : tap % 3 + col_count]
            for tap in range(9)
        ],
        axis=2,
    )
    flat = jnp.transpose(kernel, (1, 0, 2)).reshape(kernel.shape[1], -1)
    return jnp.einsum("ok,bhkw->bhow", flat, windows, preferred_element_type=jnp.float32)


def with_rows(values):
    return with_halo(values, (("patch", 1),), 1)


def per_device(
    features,
    latent,
    plan_pos,
    blocks_used,
    conv1_w,
    conv2_w,
    norm_gain,
    norm_shift,
    in_w,
    head_w,
    head_gain,
    head_shift,
):
    segment_count = lax.axis_size("segment")
    segment_pos = lax.axis_index("segment")
    last = segment_count - 1
    current = jnp.transpose(features[0], (0, 2, 1, 3))
    params = jnp.stack([norm_gain[0], norm_shift[0]], axis=2)[..., None]
    for step_no in range(STEPS):
        arrived = from_behind(current, "segment", 1)
        noise_local = lax.cond(
            segment_pos == last,
            lambda source: head_noise(source, head_w, head_gain, head_shift),
            lambda source: jnp.zeros(latent.shape, jnp.float32),
            current,
        )
        position = plan_pos + step_no
        sigma_now = sigma_at(position)
        sigma_next = sigma_at(position + 1)
        latent = latent + (sigma_next - sigma_now)[:, None, None, None] * noise_local
        scaled = (latent / jnp.sqrt(sigma_next * sigma_next + 1.0)[:, None, None, None]).astype(
            jnp.bfloat16
        )
        scaled_rows = jnp.transpose(scaled, (0, 2, 1, 3))
        peers = lax.axis_size("patch")
        origin = last * peers
        height = scaled_rows.shape[1]
        body = lax.ppermute(
            scaled_rows, ("segment", "patch"), [(origin + p, p) for p in range(peers)]
        )
        above = lax.ppermute(
            scaled_rows[:, height - 1 :],
            ("segment", "patch"),
            [(origin + p, p + 1) for p in range(peers - 1)],
        )
        below = lax.ppermute(
            scaled_rows[:, :1], ("segment", "patch"), [(origin + p, p - 1) for p in range(1, peers)]
        )
        entry_rows = conv_stacked(
            jnp.concatenate([above, body, below], axis=1), in_w
        ).astype(jnp.bfloat16)
        source = jnp.where(segment_pos == 0, entry_rows, arrived)
        after_one = resnet_unit(source, conv1_w, conv2_w, 0, params)
        current = lax.cond(
            blocks_used[0] >= 2,
            lambda hidden: resnet_unit(hidden, conv1_w, conv2_w, 1, params),
            lambda hidden: hidden,
            after_one,
        )
    batch_size, lat_count, height, col_count = latent.shape
    col_share = col_count // segment_count
    latent, current = lax.optimization_barrier((latent, current))
    pieces = latent.reshape(batch_size, lat_count, height, segment_count, col_share)
    pieces = jnp.transpose(pieces, (3, 0, 1, 2, 4)).reshape(segment_count, -1, 128)
    latent_part = scatter_from_last(pieces).reshape(batch_size, lat_count, height, col_share)
    return (latent_part, jnp.transpose(current, (0, 2, 1, 3))[None])


def solution(mesh):
    placed = (
        P("segment", None, None, "patch", None),
        P(None, None, "patch", None),
        P(),
        P("segment"),
        P("segment", None, None, None, None),
        P("segment", None, None, None, None),
        P("segment", None, None, None),
        P("segment", None, None, None),
        P(),
        P(),
        P(),
        P(),
    )
    return jax.shard_map(
        per_device,
        mesh=mesh,
        in_specs=placed,
        out_specs=(P(None, None, "patch", "segment"), P("segment", None, None, "patch", None)),
        check_vma=False,
    )
```

```python
import jax
import jax.numpy as jnp
from jax import lax
from jax.sharding import PartitionSpec as P
from jax.experimental import pallas as pl
from jax.experimental.pallas import tpu as pltpu

GROUPS = 32
STEPS = 2
SCHED = 12


epsilon = 1e-05
sigma_top = 3.0
sigma_low = 0.1
rho_power = 7.0


def with_halo(block, sides, width):
    for axis, dim in sides:
        count = lax.axis_size(axis)
        forward = [(i, i + 1) for i in range(count - 1)]
        backward = [(target, source) for source, target in forward]
        low = lax.ppermute(
            lax.slice_in_dim(block, block.shape[dim] - width, None, axis=dim), axis, forward
        )
        high = lax.ppermute(lax.slice_in_dim(block, 0, width, axis=dim), axis, backward)
        block = jnp.concatenate([low, block, high], axis=dim)
    return block


def from_behind(shard, axis, by):
    devices = lax.axis_size(axis)
    pairs = [(i, i + by) for i in range(devices) if 0 <= i + by < devices]
    return lax.ppermute(shard, axis, pairs)


def broadcast(shard, axis, root):
    mine = lax.axis_index(axis) == root
    return lax.psum(jnp.where(mine, shard, jnp.zeros_like(shard)), axis)


def sigma_at(position):
    fraction = position.astype(jnp.float32) / (SCHED - 1)
    top_root = sigma_top ** (1.0 / rho_power)
    low_root = sigma_low ** (1.0 / rho_power)
    return (top_root + fraction * (low_root - top_root)) ** rho_power


def exchange_kernel(
    peers, x_ref, top_ref, bot_ref, o_ref, lo_ref, hi_ref, send_sem, recv_sem, row_send, row_recv
):
    me = lax.axis_index("patch")
    seg = lax.axis_index("segment")
    mesh_ids = pl.DeviceIdType.MESH
    barrier = pltpu.get_barrier_semaphore()
    for dist in range(1, peers):
        pl.semaphore_signal(
            barrier, 1, device_id=(seg, lax.rem(me + dist, peers)), device_id_type=mesh_ids
        )
    pl.semaphore_wait(barrier, peers - 1)
    down = pltpu.make_async_remote_copy(
        src_ref=bot_ref,
        dst_ref=lo_ref,
        send_sem=row_send.at[0],
        recv_sem=row_recv.at[0],
        device_id=(seg, jnp.minimum(me + 1, peers - 1)),
        device_id_type=mesh_ids,
    )
    up = pltpu.make_async_remote_copy(
        src_ref=top_ref,
        dst_ref=hi_ref,
        send_sem=row_send.at[1],
        recv_sem=row_recv.at[1],
        device_id=(seg, jnp.maximum(me - 1, 0)),
        device_id_type=mesh_ids,
    )

    @pl.when(me < peers - 1)
    def _():
        down.start()

    @pl.when(me > 0)
    def _():
        up.start()

    copies = []
    for dist in range(1, peers):
        copy = pltpu.make_async_remote_copy(
            src_ref=x_ref,
            dst_ref=o_ref.at[me],
            send_sem=send_sem.at[dist],
            recv_sem=recv_sem.at[dist],
            device_id=(seg, lax.rem(me + dist, peers)),
            device_id_type=mesh_ids,
        )
        copy.start()
        copies.append(copy)
    o_ref[me] = x_ref[...]

    @pl.when(me == 0)
    def _():
        lo_ref[...] = jnp.zeros(lo_ref.shape, lo_ref.dtype)

    @pl.when(me == peers - 1)
    def _():
        hi_ref[...] = jnp.zeros(hi_ref.shape, hi_ref.dtype)

    for copy in copies:
        copy.wait()

    @pl.when(me < peers - 1)
    def _():
        down.wait_send()
        up.wait_recv()

    @pl.when(me > 0)
    def _():
        up.wait_send()
        down.wait_recv()


def exchange_patch(packed, top, bottom):
    peers = lax.axis_size("patch")
    vmem = pl.BlockSpec(memory_space=pltpu.VMEM)
    return pl.pallas_call(
        lambda *refs: exchange_kernel(peers, *refs),
        out_shape=(
            jax.ShapeDtypeStruct((peers,) + packed.shape, packed.dtype),
            jax.ShapeDtypeStruct(top.shape, top.dtype),
            jax.ShapeDtypeStruct(top.shape, top.dtype),
        ),
        in_specs=[vmem] * 3,
        out_specs=(vmem, vmem, vmem),
        scratch_shapes=[
            pltpu.SemaphoreType.DMA((peers,)),
            pltpu.SemaphoreType.DMA((peers,)),
            pltpu.SemaphoreType.DMA((2,)),
            pltpu.SemaphoreType.DMA((2,)),
        ],
        compiler_params=pltpu.CompilerParams(
            collective_id=0 if top.dtype == jnp.bfloat16 else 1, has_side_effects=True
        ),
        name="exchange_stats_rows",
    )(packed, top, bottom)


def group_moments(values, rows):
    batch_size, height, chan_count, col_count = values.shape
    grouped = values.reshape(batch_size, height, GROUPS, chan_count // GROUPS, col_count)
    local_count = chan_count // GROUPS * height * col_count
    peers = lax.axis_size("patch")
    local_sum = jnp.sum(grouped, axis=(1, 3, 4))
    local_center = local_sum / local_count
    local_dev = jnp.sum(
        jnp.square(grouped - local_center[:, None, :, None, None]), axis=(1, 3, 4)
    )
    flat = jnp.concatenate([local_sum.reshape(-1), local_dev.reshape(-1)])
    width = 128 * ((flat.shape[0] + 127) // 128)
    packed = jnp.pad(flat, (0, width - flat.shape[0]))[None]
    every, low, high = exchange_patch(packed, rows[:, 0], rows[:, height - 1])
    every = every.reshape(peers, width)
    half = batch_size * GROUPS
    sums = every[:, :half].reshape(peers, batch_size, GROUPS)
    devs = every[:, half : 2 * half].reshape(peers, batch_size, GROUPS)
    cell_count = local_count * peers
    center = jnp.sum(sums, axis=0) / cell_count
    between = jnp.sum(jnp.square(sums / local_count - center[None]), axis=0) * local_count
    spread = (jnp.sum(devs, axis=0) + between) / cell_count
    return (center, jnp.sqrt(spread + epsilon)), low, high


def act_with_rows(values, rows, gain, shift):
    moments, low, high = group_moments(values, rows)
    full = jnp.concatenate(
        [low[:, None].astype(jnp.float32), values, high[:, None].astype(jnp.float32)], axis=1
    )
    act = norm_silu(full, moments, gain, shift)
    me = lax.axis_index("patch")
    row = lax.broadcasted_iota(jnp.int32, (1, full.shape[1], 1, 1), 1)
    pad = ((row == 0) & (me == 0)) | ((row == full.shape[1] - 1) & (me == lax.axis_size("patch") - 1))
    return jnp.where(pad, 0.0, act).astype(jnp.bfloat16)


def scatter_kernel(count, x_ref, o_ref, send_sem, recv_sem):
    seg = lax.axis_index("segment")
    me = lax.axis_index("patch")
    last = count - 1
    mesh_ids = pl.DeviceIdType.MESH
    barrier = pltpu.get_barrier_semaphore()

    @pl.when(seg == last)
    def _():
        for target in range(last):
            pl.semaphore_signal(barrier, 1, device_id=(target, me), device_id_type=mesh_ids)
        pl.semaphore_wait(barrier, last)
        copies = []
        for target in range(last):
            copy = pltpu.make_async_remote_copy(
                src_ref=x_ref.at[target],
                dst_ref=o_ref,
                send_sem=send_sem.at[target],
                recv_sem=recv_sem.at[0],
                device_id=(target, me),
                device_id_type=mesh_ids,
            )
            copy.start()
            copies.append(copy)
        o_ref[...] = x_ref[last]
        for copy in copies:
            copy.wait_send()

    @pl.when(seg != last)
    def _():
        pl.semaphore_signal(barrier, 1, device_id=(last, me), device_id_type=mesh_ids)
        pl.semaphore_wait(barrier, 1)
        pltpu.make_async_remote_copy(
            src_ref=x_ref.at[0],
            dst_ref=o_ref,
            send_sem=send_sem.at[0],
            recv_sem=recv_sem.at[0],
            device_id=(last, me),
            device_id_type=mesh_ids,
        ).wait_recv()


def scatter_from_last(pieces):
    count = lax.axis_size("segment")
    vmem = pl.BlockSpec(memory_space=pltpu.VMEM)
    return pl.pallas_call(
        lambda *refs: scatter_kernel(count, *refs),
        out_shape=jax.ShapeDtypeStruct(pieces.shape[1:], pieces.dtype),
        in_specs=[vmem],
        out_specs=vmem,
        scratch_shapes=[pltpu.SemaphoreType.DMA((count,)), pltpu.SemaphoreType.DMA((1,))],
        compiler_params=pltpu.CompilerParams(collective_id=2, has_side_effects=True),
        name="scatter_latent_columns",
    )(pieces)


def norm_silu(values, moments, gain, shift):
    center, root_spread = moments
    batch_size, height, chan_count, col_count = values.shape
    grouped = values.reshape(batch_size, height, GROUPS, chan_count // GROUPS, col_count)
    normed = (
        (grouped - center[:, None, :, None, None]) / root_spread[:, None, :, None, None]
    ).reshape(values.shape)
    normed = normed * gain[None, None, :, None] + shift[None, None, :, None]
    return jax.nn.silu(normed)


def conv_kernel(x_ref, w_ref, o_ref):
    batch, rows = o_ref.shape[0], o_ref.shape[1]
    for b in range(batch):
        for r in range(rows):
            acc = None
            for tap in range(9):
                part = jnp.dot(
                    w_ref[tap], x_ref[tap % 3, b, r + tap // 3], preferred_element_type=jnp.float32
                )
                acc = part if acc is None else acc + part
            o_ref[b, r] = acc


def fused_kernel(flags_ref, vals_ref, lo_ref, hi_ref, stat_ref, par_ref, w_ref, *rest):
    if len(rest) == 3:
        res_ref, o_ref, act_ref = rest
    else:
        res_ref = None
        o_ref, act_ref = rest
    rows, chans, cols = vals_ref.shape
    mean = stat_ref[0]
    std = stat_ref[1]
    gain = par_ref[0]
    shift = par_ref[1]
    col = lax.broadcasted_iota(jnp.int32, (chans, cols), 1)

    def put(slot, values, keep):
        normed = (values.astype(jnp.float32) - mean) / std * gain + shift
        act = normed / (1.0 + jnp.exp(-normed))
        act = jnp.where(keep, act, 0.0).astype(jnp.bfloat16).astype(jnp.float32)
        act_ref[slot, 1] = act.astype(jnp.bfloat16)
        left = jnp.where(col == 0, 0.0, pltpu.roll(act, 1, 1))
        act_ref[slot, 0] = left.astype(jnp.bfloat16)
        right = jnp.where(col == cols - 1, 0.0, pltpu.roll(act, cols - 1, 1))
        act_ref[slot, 2] = right.astype(jnp.bfloat16)

    put(0, lo_ref[...], flags_ref[0] > 0)
    for r in range(rows):
        put(r + 1, vals_ref[r], True)
    put(rows + 1, hi_ref[...], flags_ref[1] > 0)
    for r in range(rows):
        acc = None
        for tap in range(9):
            part = jnp.dot(
                w_ref[tap], act_ref[r + tap // 3, tap % 3], preferred_element_type=jnp.float32
            )
            acc = part if acc is None else acc + part
        if res_ref is not None:
            acc = res_ref[r].astype(jnp.float32) + acc
        o_ref[r] = acc.astype(o_ref.dtype)


def norm_conv(values, moments, low, high, params, norm_no, weights, block, residual=None):
    batch, rows, chans, cols = values.shape
    outs = weights.shape[-2]
    center, root_spread = moments
    per_group = chans // GROUPS
    stats_c = jnp.repeat(jnp.stack([center, root_spread], axis=1), per_group, axis=2)[..., None]
    me = lax.axis_index("patch")
    flags = jnp.stack([me > 0, me < lax.axis_size("patch") - 1]).astype(jnp.int32)
    flops = 2 * 9 * batch * rows * cols * chans * outs
    row_spec = pl.BlockSpec((None, chans, cols), lambda b: (b, 0, 0))
    block_spec = pl.BlockSpec((None, rows, chans, cols), lambda b: (b, 0, 0, 0))
    operands = [flags, values, low, high, stats_c, params, weights]
    in_specs = [
        pl.BlockSpec(memory_space=pltpu.SMEM),
        block_spec,
        row_spec,
        row_spec,
        pl.BlockSpec((None, 2, chans, 1), lambda b: (b, 0, 0, 0)),
        pl.BlockSpec((None, None, 2, chans, 1), lambda b: (block, norm_no, 0, 0, 0)),
        pl.BlockSpec((None, None) + weights.shape[2:], lambda b: (0, block, 0, 0, 0)),
    ]
    out_dtype = jnp.float32
    if residual is not None:
        operands.append(residual)
        in_specs.append(block_spec)
        out_dtype = residual.dtype
    return pl.pallas_call(
        fused_kernel,
        grid=(batch,),
        out_shape=jax.ShapeDtypeStruct((batch, rows, outs, cols), out_dtype),
        in_specs=in_specs,
        out_specs=pl.BlockSpec((None, rows, outs, cols), lambda b: (b, 0, 0, 0)),
        scratch_shapes=[pltpu.VMEM((rows + 2, 3, chans, cols), jnp.bfloat16)],
        cost_estimate=pl.CostEstimate(
            flops=flops,
            transcendentals=batch * (rows + 2) * chans * cols,
            bytes_accessed=values.size * values.dtype.itemsize + 9 * chans * outs * 2 + batch * rows * outs * cols * 4,
        ),
        name="norm_conv3x3_rows",
    )(*operands)


def conv_valid(rows_in, kernel):
    padded = jnp.pad(rows_in, ((0, 0), (0, 0), (0, 0), (1, 1)))
    height = rows_in.shape[1] - 2
    col_count = rows_in.shape[3]
    accum = jnp.zeros((rows_in.shape[0], height, kernel.shape[1], col_count), jnp.float32)
    for tap_no in range(9):
        row_off, col_off = (tap_no // 3, tap_no % 3)
        window = padded[:, row_off : row_off + height, :, col_off : col_off + col_count]
        accum = accum + jnp.einsum(
            "oi,bhiw->bhow", kernel[tap_no], window, preferred_element_type=jnp.float32
        )
    return accum


def resnet_unit(hidden, conv1_w, conv2_w, block, params):
    moments, low, high = group_moments(hidden.astype(jnp.float32), hidden)
    middle = norm_conv(hidden, moments, low, high, params, 0, conv1_w, block)
    moments, low, high = group_moments(middle, middle)
    return norm_conv(middle, moments, low, high, params, 1, conv2_w, block, residual=hidden)


def head_noise(source, head_w, head_gain, head_shift):
    head_input = act_with_rows(source.astype(jnp.float32), source, head_gain, head_shift)
    return jnp.transpose(conv_taps_after(head_input, head_w), (0, 2, 1, 3))


def conv_stacked(rows_in, kernel):
    padded = jnp.pad(rows_in, ((0, 0), (0, 0), (0, 0), (1, 1)))
    height = rows_in.shape[1] - 2
    col_count = rows_in.shape[3]
    windows = jnp.concatenate(
        [
            padded[:, tap // 3 : tap // 3 + height, :, tap % 3 : tap % 3 + col_count]
            for tap in range(9)
        ],
        axis=2,
    )
    flat = jnp.transpose(kernel, (1, 0, 2)).reshape(kernel.shape[1], -1)
    return jnp.einsum("ok,bhkw->bhow", flat, windows, preferred_element_type=jnp.float32)


def conv_taps_after(rows_in, kernel):
    batch, rows_halo, chans, cols = rows_in.shape
    height = rows_halo - 2
    outs = kernel.shape[1]
    stacked = kernel.reshape(9 * outs, chans)
    partial = jnp.einsum("kc,bhcw->bhkw", stacked, rows_in, preferred_element_type=jnp.float32)
    partial = jnp.pad(partial, ((0, 0), (0, 0), (0, 0), (1, 1)))
    accum = jnp.zeros((batch, height, outs, cols), jnp.float32)
    for tap in range(9):
        row_off, col_off = (tap // 3, tap % 3)
        accum = accum + partial[
            :, row_off : row_off + height, tap * outs : (tap + 1) * outs, col_off : col_off + cols
        ]
    return accum


def with_rows(values):
    return with_halo(values, (("patch", 1),), 1)


def per_device(
    features,
    latent,
    plan_pos,
    blocks_used,
    conv1_w,
    conv2_w,
    norm_gain,
    norm_shift,
    in_w,
    head_w,
    head_gain,
    head_shift,
):
    segment_count = lax.axis_size("segment")
    segment_pos = lax.axis_index("segment")
    last = segment_count - 1
    current = jnp.transpose(features[0], (0, 2, 1, 3))
    params = jnp.stack([norm_gain[0], norm_shift[0]], axis=2)[..., None]
    for step_no in range(STEPS):
        arrived = from_behind(current, "segment", 1)
        noise_local = lax.cond(
            segment_pos == last,
            lambda source: head_noise(source, head_w, head_gain, head_shift),
            lambda source: jnp.zeros(latent.shape, jnp.float32),
            current,
        )
        position = plan_pos + step_no
        sigma_now = sigma_at(position)
        sigma_next = sigma_at(position + 1)
        latent = latent + (sigma_next - sigma_now)[:, None, None, None] * noise_local
        scaled = (latent / jnp.sqrt(sigma_next * sigma_next + 1.0)[:, None, None, None]).astype(
            jnp.bfloat16
        )
        scaled_rows = jnp.transpose(scaled, (0, 2, 1, 3))
        peers = lax.axis_size("patch")
        origin = last * peers
        height = scaled_rows.shape[1]
        body = lax.ppermute(
            scaled_rows, ("segment", "patch"), [(origin + p, p) for p in range(peers)]
        )
        above = lax.ppermute(
            scaled_rows[:, height - 1 :],
            ("segment", "patch"),
            [(origin + p, p + 1) for p in range(peers - 1)],
        )
        below = lax.ppermute(
            scaled_rows[:, :1], ("segment", "patch"), [(origin + p, p - 1) for p in range(1, peers)]
        )
        entry_rows = conv_stacked(
            jnp.concatenate([above, body, below], axis=1), in_w
        ).astype(jnp.bfloat16)
        source = jnp.where(segment_pos == 0, entry_rows, arrived)
        after_one = resnet_unit(source, conv1_w, conv2_w, 0, params)
        current = lax.cond(
            blocks_used[0] >= 2,
            lambda hidden: resnet_unit(hidden, conv1_w, conv2_w, 1, params),
            lambda hidden: hidden,
            after_one,
        )
    batch_size, lat_count, height, col_count = latent.shape
    col_share = col_count // segment_count
    latent, current = lax.optimization_barrier((latent, current))
    pieces = latent.reshape(batch_size, lat_count, height, segment_count, col_share)
    pieces = jnp.transpose(pieces, (3, 0, 1, 2, 4)).reshape(segment_count, -1, 128)
    latent_part = scatter_from_last(pieces).reshape(batch_size, lat_count, height, col_share)
    return (latent_part, jnp.transpose(current, (0, 2, 1, 3))[None])


def solution(mesh):
    placed = (
        P("segment", None, None, "patch", None),
        P(None, None, "patch", None),
        P(),
        P("segment"),
        P("segment", None, None, None, None),
        P("segment", None, None, None, None),
        P("segment", None, None, None),
        P("segment", None, None, None),
        P(),
        P(),
        P(),
        P(),
    )
    return jax.shard_map(
        per_device,
        mesh=mesh,
        in_specs=placed,
        out_specs=(P(None, None, "patch", "segment"), P("segment", None, None, "patch", None)),
        check_vma=False,
    )
```

```python
import jax
import jax.numpy as jnp
from jax import lax
from jax.sharding import PartitionSpec as P
from jax.experimental import pallas as pl
from jax.experimental.pallas import tpu as pltpu

GROUPS = 32
STEPS = 2
SCHED = 12


epsilon = 1e-05
sigma_top = 3.0
sigma_low = 0.1
rho_power = 7.0


def with_halo(block, sides, width):
    for axis, dim in sides:
        count = lax.axis_size(axis)
        forward = [(i, i + 1) for i in range(count - 1)]
        backward = [(target, source) for source, target in forward]
        low = lax.ppermute(
            lax.slice_in_dim(block, block.shape[dim] - width, None, axis=dim), axis, forward
        )
        high = lax.ppermute(lax.slice_in_dim(block, 0, width, axis=dim), axis, backward)
        block = jnp.concatenate([low, block, high], axis=dim)
    return block


def from_behind(shard, axis, by):
    devices = lax.axis_size(axis)
    pairs = [(i, i + by) for i in range(devices) if 0 <= i + by < devices]
    return lax.ppermute(shard, axis, pairs)


def broadcast(shard, axis, root):
    mine = lax.axis_index(axis) == root
    return lax.psum(jnp.where(mine, shard, jnp.zeros_like(shard)), axis)


def sigma_at(position):
    fraction = position.astype(jnp.float32) / (SCHED - 1)
    top_root = sigma_top ** (1.0 / rho_power)
    low_root = sigma_low ** (1.0 / rho_power)
    return (top_root + fraction * (low_root - top_root)) ** rho_power


def exchange_kernel(
    peers, x_ref, top_ref, bot_ref, o_ref, lo_ref, hi_ref, send_sem, recv_sem, row_send, row_recv
):
    me = lax.axis_index("patch")
    seg = lax.axis_index("segment")
    mesh_ids = pl.DeviceIdType.MESH
    barrier = pltpu.get_barrier_semaphore()
    for dist in range(1, peers):
        pl.semaphore_signal(
            barrier, 1, device_id=(seg, lax.rem(me + dist, peers)), device_id_type=mesh_ids
        )
    pl.semaphore_wait(barrier, peers - 1)
    down = pltpu.make_async_remote_copy(
        src_ref=bot_ref,
        dst_ref=lo_ref,
        send_sem=row_send.at[0],
        recv_sem=row_recv.at[0],
        device_id=(seg, jnp.minimum(me + 1, peers - 1)),
        device_id_type=mesh_ids,
    )
    up = pltpu.make_async_remote_copy(
        src_ref=top_ref,
        dst_ref=hi_ref,
        send_sem=row_send.at[1],
        recv_sem=row_recv.at[1],
        device_id=(seg, jnp.maximum(me - 1, 0)),
        device_id_type=mesh_ids,
    )

    @pl.when(me < peers - 1)
    def _():
        down.start()

    @pl.when(me > 0)
    def _():
        up.start()

    copies = []
    for dist in range(1, peers):
        copy = pltpu.make_async_remote_copy(
            src_ref=x_ref,
            dst_ref=o_ref.at[me],
            send_sem=send_sem.at[dist],
            recv_sem=recv_sem.at[dist],
            device_id=(seg, lax.rem(me + dist, peers)),
            device_id_type=mesh_ids,
        )
        copy.start()
        copies.append(copy)
    o_ref[me] = x_ref[...]

    @pl.when(me == 0)
    def _():
        lo_ref[...] = jnp.zeros(lo_ref.shape, lo_ref.dtype)

    @pl.when(me == peers - 1)
    def _():
        hi_ref[...] = jnp.zeros(hi_ref.shape, hi_ref.dtype)

    for copy in copies:
        copy.wait()

    @pl.when(me < peers - 1)
    def _():
        down.wait_send()
        up.wait_recv()

    @pl.when(me > 0)
    def _():
        up.wait_send()
        down.wait_recv()


def exchange_patch(packed, top, bottom):
    peers = lax.axis_size("patch")
    vmem = pl.BlockSpec(memory_space=pltpu.VMEM)
    return pl.pallas_call(
        lambda *refs: exchange_kernel(peers, *refs),
        out_shape=(
            jax.ShapeDtypeStruct((peers,) + packed.shape, packed.dtype),
            jax.ShapeDtypeStruct(top.shape, top.dtype),
            jax.ShapeDtypeStruct(top.shape, top.dtype),
        ),
        in_specs=[vmem] * 3,
        out_specs=(vmem, vmem, vmem),
        scratch_shapes=[
            pltpu.SemaphoreType.DMA((peers,)),
            pltpu.SemaphoreType.DMA((peers,)),
            pltpu.SemaphoreType.DMA((2,)),
            pltpu.SemaphoreType.DMA((2,)),
        ],
        compiler_params=pltpu.CompilerParams(
            collective_id=0 if top.dtype == jnp.bfloat16 else 1, has_side_effects=True
        ),
        name="exchange_stats_rows",
    )(packed, top, bottom)


def group_moments(values, rows):
    batch_size, height, chan_count, col_count = values.shape
    grouped = values.reshape(batch_size, height, GROUPS, chan_count // GROUPS, col_count)
    local_count = chan_count // GROUPS * height * col_count
    peers = lax.axis_size("patch")
    local_sum = jnp.sum(grouped, axis=(1, 3, 4))
    local_center = local_sum / local_count
    local_dev = jnp.sum(
        jnp.square(grouped - local_center[:, None, :, None, None]), axis=(1, 3, 4)
    )
    flat = jnp.concatenate([local_sum.reshape(-1), local_dev.reshape(-1)])
    width = 128 * ((flat.shape[0] + 127) // 128)
    packed = jnp.pad(flat, (0, width - flat.shape[0]))[None]
    every, low, high = exchange_patch(packed, rows[:, 0], rows[:, height - 1])
    every = every.reshape(peers, width)
    half = batch_size * GROUPS
    sums = every[:, :half].reshape(peers, batch_size, GROUPS)
    devs = every[:, half : 2 * half].reshape(peers, batch_size, GROUPS)
    cell_count = local_count * peers
    center = jnp.sum(sums, axis=0) / cell_count
    between = jnp.sum(jnp.square(sums / local_count - center[None]), axis=0) * local_count
    spread = (jnp.sum(devs, axis=0) + between) / cell_count
    return (center, jnp.sqrt(spread + epsilon)), low, high


def act_with_rows(values, rows, gain, shift):
    moments, low, high = group_moments(values, rows)
    full = jnp.concatenate(
        [low[:, None].astype(jnp.float32), values, high[:, None].astype(jnp.float32)], axis=1
    )
    act = norm_silu(full, moments, gain, shift)
    me = lax.axis_index("patch")
    row = lax.broadcasted_iota(jnp.int32, (1, full.shape[1], 1, 1), 1)
    pad = ((row == 0) & (me == 0)) | ((row == full.shape[1] - 1) & (me == lax.axis_size("patch") - 1))
    return jnp.where(pad, 0.0, act).astype(jnp.bfloat16)


def scatter_kernel(count, x_ref, o_ref, send_sem, recv_sem):
    seg = lax.axis_index("segment")
    me = lax.axis_index("patch")
    last = count - 1
    mesh_ids = pl.DeviceIdType.MESH
    barrier = pltpu.get_barrier_semaphore()

    @pl.when(seg == last)
    def _():
        for target in range(last):
            pl.semaphore_signal(barrier, 1, device_id=(target, me), device_id_type=mesh_ids)
        pl.semaphore_wait(barrier, last)
        copies = []
        for target in range(last):
            copy = pltpu.make_async_remote_copy(
                src_ref=x_ref.at[target],
                dst_ref=o_ref,
                send_sem=send_sem.at[target],
                recv_sem=recv_sem.at[0],
                device_id=(target, me),
                device_id_type=mesh_ids,
            )
            copy.start()
            copies.append(copy)
        o_ref[...] = x_ref[last]
        for copy in copies:
            copy.wait_send()

    @pl.when(seg != last)
    def _():
        pl.semaphore_signal(barrier, 1, device_id=(last, me), device_id_type=mesh_ids)
        pl.semaphore_wait(barrier, 1)
        pltpu.make_async_remote_copy(
            src_ref=x_ref.at[0],
            dst_ref=o_ref,
            send_sem=send_sem.at[0],
            recv_sem=recv_sem.at[0],
            device_id=(last, me),
            device_id_type=mesh_ids,
        ).wait_recv()


def scatter_from_last(pieces):
    count = lax.axis_size("segment")
    vmem = pl.BlockSpec(memory_space=pltpu.VMEM)
    return pl.pallas_call(
        lambda *refs: scatter_kernel(count, *refs),
        out_shape=jax.ShapeDtypeStruct(pieces.shape[1:], pieces.dtype),
        in_specs=[vmem],
        out_specs=vmem,
        scratch_shapes=[pltpu.SemaphoreType.DMA((count,)), pltpu.SemaphoreType.DMA((1,))],
        compiler_params=pltpu.CompilerParams(collective_id=2, has_side_effects=True),
        name="scatter_latent_columns",
    )(pieces)


def norm_silu(values, moments, gain, shift):
    center, root_spread = moments
    batch_size, height, chan_count, col_count = values.shape
    grouped = values.reshape(batch_size, height, GROUPS, chan_count // GROUPS, col_count)
    normed = (
        (grouped - center[:, None, :, None, None]) / root_spread[:, None, :, None, None]
    ).reshape(values.shape)
    normed = normed * gain[None, None, :, None] + shift[None, None, :, None]
    return jax.nn.silu(normed)


def conv_kernel(x_ref, w_ref, o_ref):
    batch, rows = o_ref.shape[0], o_ref.shape[1]
    for b in range(batch):
        for r in range(rows):
            acc = None
            for tap in range(9):
                part = jnp.dot(
                    w_ref[tap], x_ref[tap % 3, b, r + tap // 3], preferred_element_type=jnp.float32
                )
                acc = part if acc is None else acc + part
            o_ref[b, r] = acc


def fused_kernel(flags_ref, vals_ref, lo_ref, hi_ref, stat_ref, par_ref, w_ref, *rest):
    if len(rest) == 3:
        res_ref, o_ref, act_ref = rest
    else:
        res_ref = None
        o_ref, act_ref = rest
    rows, chans, cols = vals_ref.shape
    mean = stat_ref[0]
    std = stat_ref[1]
    gain = par_ref[0]
    shift = par_ref[1]
    col = lax.broadcasted_iota(jnp.int32, (chans, cols), 1)

    def put(slot, values, keep):
        normed = (values.astype(jnp.float32) - mean) / std * gain + shift
        act = normed / (1.0 + jnp.exp(-normed))
        act = jnp.where(keep, act, 0.0).astype(jnp.bfloat16).astype(jnp.float32)
        act_ref[slot, 1] = act.astype(jnp.bfloat16)
        left = jnp.where(col == 0, 0.0, pltpu.roll(act, 1, 1))
        act_ref[slot, 0] = left.astype(jnp.bfloat16)
        right = jnp.where(col == cols - 1, 0.0, pltpu.roll(act, cols - 1, 1))
        act_ref[slot, 2] = right.astype(jnp.bfloat16)

    put(0, lo_ref[...], flags_ref[0] > 0)
    for r in range(rows):
        put(r + 1, vals_ref[r], True)
    put(rows + 1, hi_ref[...], flags_ref[1] > 0)
    for r in range(rows):
        acc = None
        for tap in range(9):
            part = jnp.dot(
                w_ref[tap], act_ref[r + tap // 3, tap % 3], preferred_element_type=jnp.float32
            )
            acc = part if acc is None else acc + part
        if res_ref is not None:
            acc = res_ref[r].astype(jnp.float32) + acc
        o_ref[r] = acc.astype(o_ref.dtype)


def norm_conv(values, moments, low, high, params, norm_no, weights, block, residual=None):
    batch, rows, chans, cols = values.shape
    outs = weights.shape[-2]
    center, root_spread = moments
    per_group = chans // GROUPS
    stats_c = jnp.repeat(jnp.stack([center, root_spread], axis=1), per_group, axis=2)[..., None]
    me = lax.axis_index("patch")
    flags = jnp.stack([me > 0, me < lax.axis_size("patch") - 1]).astype(jnp.int32)
    flops = 2 * 9 * batch * rows * cols * chans * outs
    row_spec = pl.BlockSpec((None, chans, cols), lambda b: (b, 0, 0))
    block_spec = pl.BlockSpec((None, rows, chans, cols), lambda b: (b, 0, 0, 0))
    operands = [flags, values, low, high, stats_c, params, weights]
    in_specs = [
        pl.BlockSpec(memory_space=pltpu.SMEM),
        block_spec,
        row_spec,
        row_spec,
        pl.BlockSpec((None, 2, chans, 1), lambda b: (b, 0, 0, 0)),
        pl.BlockSpec((None, None, 2, chans, cols), lambda b: (block, norm_no, 0, 0, 0)),
        pl.BlockSpec((None, None) + weights.shape[2:], lambda b: (0, block, 0, 0, 0)),
    ]
    out_dtype = jnp.float32
    if residual is not None:
        operands.append(residual)
        in_specs.append(block_spec)
        out_dtype = residual.dtype
    return pl.pallas_call(
        fused_kernel,
        grid=(batch,),
        out_shape=jax.ShapeDtypeStruct((batch, rows, outs, cols), out_dtype),
        in_specs=in_specs,
        out_specs=pl.BlockSpec((None, rows, outs, cols), lambda b: (b, 0, 0, 0)),
        scratch_shapes=[pltpu.VMEM((rows + 2, 3, chans, cols), jnp.bfloat16)],
        cost_estimate=pl.CostEstimate(
            flops=flops,
            transcendentals=batch * (rows + 2) * chans * cols,
            bytes_accessed=values.size * values.dtype.itemsize + 9 * chans * outs * 2 + batch * rows * outs * cols * 4,
        ),
        name="norm_conv3x3_rows",
    )(*operands)


def conv_valid(rows_in, kernel):
    padded = jnp.pad(rows_in, ((0, 0), (0, 0), (0, 0), (1, 1)))
    height = rows_in.shape[1] - 2
    col_count = rows_in.shape[3]
    accum = jnp.zeros((rows_in.shape[0], height, kernel.shape[1], col_count), jnp.float32)
    for tap_no in range(9):
        row_off, col_off = (tap_no // 3, tap_no % 3)
        window = padded[:, row_off : row_off + height, :, col_off : col_off + col_count]
        accum = accum + jnp.einsum(
            "oi,bhiw->bhow", kernel[tap_no], window, preferred_element_type=jnp.float32
        )
    return accum


def resnet_unit(hidden, conv1_w, conv2_w, block, params):
    moments, low, high = group_moments(hidden.astype(jnp.float32), hidden)
    middle = norm_conv(hidden, moments, low, high, params, 0, conv1_w, block)
    moments, low, high = group_moments(middle, middle)
    return norm_conv(middle, moments, low, high, params, 1, conv2_w, block, residual=hidden)


def head_noise(source, head_w, head_gain, head_shift):
    head_input = act_with_rows(source.astype(jnp.float32), source, head_gain, head_shift)
    return jnp.transpose(conv_taps_after(head_input, head_w), (0, 2, 1, 3))


def conv_stacked(rows_in, kernel):
    padded = jnp.pad(rows_in, ((0, 0), (0, 0), (0, 0), (1, 1)))
    height = rows_in.shape[1] - 2
    col_count = rows_in.shape[3]
    windows = jnp.concatenate(
        [
            padded[:, tap // 3 : tap // 3 + height, :, tap % 3 : tap % 3 + col_count]
            for tap in range(9)
        ],
        axis=2,
    )
    flat = jnp.transpose(kernel, (1, 0, 2)).reshape(kernel.shape[1], -1)
    return jnp.einsum("ok,bhkw->bhow", flat, windows, preferred_element_type=jnp.float32)


def conv_taps_after(rows_in, kernel):
    batch, rows_halo, chans, cols = rows_in.shape
    height = rows_halo - 2
    outs = kernel.shape[1]
    stacked = kernel.reshape(9 * outs, chans)
    partial = jnp.einsum("kc,bhcw->bhkw", stacked, rows_in, preferred_element_type=jnp.float32)
    partial = jnp.pad(partial, ((0, 0), (0, 0), (0, 0), (1, 1)))
    accum = jnp.zeros((batch, height, outs, cols), jnp.float32)
    for tap in range(9):
        row_off, col_off = (tap // 3, tap % 3)
        accum = accum + partial[
            :, row_off : row_off + height, tap * outs : (tap + 1) * outs, col_off : col_off + cols
        ]
    return accum


def with_rows(values):
    return with_halo(values, (("patch", 1),), 1)


def per_device(
    features,
    latent,
    plan_pos,
    blocks_used,
    conv1_w,
    conv2_w,
    norm_gain,
    norm_shift,
    in_w,
    head_w,
    head_gain,
    head_shift,
):
    segment_count = lax.axis_size("segment")
    segment_pos = lax.axis_index("segment")
    last = segment_count - 1
    current = jnp.transpose(features[0], (0, 2, 1, 3))
    params = jnp.broadcast_to(
        jnp.stack([norm_gain[0], norm_shift[0]], axis=2)[..., None],
        norm_gain.shape[1:3] + (2, norm_gain.shape[3], features.shape[4]),
    )
    for step_no in range(STEPS):
        arrived = from_behind(current, "segment", 1)
        noise_local = lax.cond(
            segment_pos == last,
            lambda source: head_noise(source, head_w, head_gain, head_shift),
            lambda source: jnp.zeros(latent.shape, jnp.float32),
            current,
        )
        position = plan_pos + step_no
        sigma_now = sigma_at(position)
        sigma_next = sigma_at(position + 1)
        latent = latent + (sigma_next - sigma_now)[:, None, None, None] * noise_local
        scaled = (latent / jnp.sqrt(sigma_next * sigma_next + 1.0)[:, None, None, None]).astype(
            jnp.bfloat16
        )
        scaled_rows = jnp.transpose(scaled, (0, 2, 1, 3))
        peers = lax.axis_size("patch")
        origin = last * peers
        height = scaled_rows.shape[1]
        body = lax.ppermute(
            scaled_rows, ("segment", "patch"), [(origin + p, p) for p in range(peers)]
        )
        above = lax.ppermute(
            scaled_rows[:, height - 1 :],
            ("segment", "patch"),
            [(origin + p, p + 1) for p in range(peers - 1)],
        )
        below = lax.ppermute(
            scaled_rows[:, :1], ("segment", "patch"), [(origin + p, p - 1) for p in range(1, peers)]
        )
        entry_rows = conv_stacked(
            jnp.concatenate([above, body, below], axis=1), in_w
        ).astype(jnp.bfloat16)
        source = jnp.where(segment_pos == 0, entry_rows, arrived)
        after_one = resnet_unit(source, conv1_w, conv2_w, 0, params)
        current = lax.cond(
            blocks_used[0] >= 2,
            lambda hidden: resnet_unit(hidden, conv1_w, conv2_w, 1, params),
            lambda hidden: hidden,
            after_one,
        )
    batch_size, lat_count, height, col_count = latent.shape
    col_share = col_count // segment_count
    latent, current = lax.optimization_barrier((latent, current))
    pieces = latent.reshape(batch_size, lat_count, height, segment_count, col_share)
    pieces = jnp.transpose(pieces, (3, 0, 1, 2, 4)).reshape(segment_count, -1, 128)
    latent_part = scatter_from_last(pieces).reshape(batch_size, lat_count, height, col_share)
    return (latent_part, jnp.transpose(current, (0, 2, 1, 3))[None])


def solution(mesh):
    placed = (
        P("segment", None, None, "patch", None),
        P(None, None, "patch", None),
        P(),
        P("segment"),
        P("segment", None, None, None, None),
        P("segment", None, None, None, None),
        P("segment", None, None, None),
        P("segment", None, None, None),
        P(),
        P(),
        P(),
        P(),
    )
    return jax.shard_map(
        per_device,
        mesh=mesh,
        in_specs=placed,
        out_specs=(P(None, None, "patch", "segment"), P("segment", None, None, "patch", None)),
        check_vma=False,
    )
```

```python
import jax
import jax.numpy as jnp
from jax import lax
from jax.sharding import PartitionSpec as P
from jax.experimental import pallas as pl
from jax.experimental.pallas import tpu as pltpu

GROUPS = 32
STEPS = 2
SCHED = 12


epsilon = 1e-05
sigma_top = 3.0
sigma_low = 0.1
rho_power = 7.0


def with_halo(block, sides, width):
    for axis, dim in sides:
        count = lax.axis_size(axis)
        forward = [(i, i + 1) for i in range(count - 1)]
        backward = [(target, source) for source, target in forward]
        low = lax.ppermute(
            lax.slice_in_dim(block, block.shape[dim] - width, None, axis=dim), axis, forward
        )
        high = lax.ppermute(lax.slice_in_dim(block, 0, width, axis=dim), axis, backward)
        block = jnp.concatenate([low, block, high], axis=dim)
    return block


def from_behind(shard, axis, by):
    devices = lax.axis_size(axis)
    pairs = [(i, i + by) for i in range(devices) if 0 <= i + by < devices]
    return lax.ppermute(shard, axis, pairs)


def broadcast(shard, axis, root):
    mine = lax.axis_index(axis) == root
    return lax.psum(jnp.where(mine, shard, jnp.zeros_like(shard)), axis)


def sigma_at(position):
    fraction = position.astype(jnp.float32) / (SCHED - 1)
    top_root = sigma_top ** (1.0 / rho_power)
    low_root = sigma_low ** (1.0 / rho_power)
    return (top_root + fraction * (low_root - top_root)) ** rho_power


def exchange_kernel(
    peers, x_ref, top_ref, bot_ref, o_ref, lo_ref, hi_ref, send_sem, recv_sem, row_send, row_recv
):
    me = lax.axis_index("patch")
    seg = lax.axis_index("segment")
    mesh_ids = pl.DeviceIdType.MESH
    barrier = pltpu.get_barrier_semaphore()
    for dist in range(1, peers):
        pl.semaphore_signal(
            barrier, 1, device_id=(seg, lax.rem(me + dist, peers)), device_id_type=mesh_ids
        )
    pl.semaphore_wait(barrier, peers - 1)
    down = pltpu.make_async_remote_copy(
        src_ref=bot_ref,
        dst_ref=lo_ref,
        send_sem=row_send.at[0],
        recv_sem=row_recv.at[0],
        device_id=(seg, jnp.minimum(me + 1, peers - 1)),
        device_id_type=mesh_ids,
    )
    up = pltpu.make_async_remote_copy(
        src_ref=top_ref,
        dst_ref=hi_ref,
        send_sem=row_send.at[1],
        recv_sem=row_recv.at[1],
        device_id=(seg, jnp.maximum(me - 1, 0)),
        device_id_type=mesh_ids,
    )

    @pl.when(me < peers - 1)
    def _():
        down.start()

    @pl.when(me > 0)
    def _():
        up.start()

    copies = []
    for dist in range(1, peers):
        copy = pltpu.make_async_remote_copy(
            src_ref=x_ref,
            dst_ref=o_ref.at[me],
            send_sem=send_sem.at[dist],
            recv_sem=recv_sem.at[dist],
            device_id=(seg, lax.rem(me + dist, peers)),
            device_id_type=mesh_ids,
        )
        copy.start()
        copies.append(copy)
    o_ref[me] = x_ref[...]

    @pl.when(me == 0)
    def _():
        lo_ref[...] = jnp.zeros(lo_ref.shape, lo_ref.dtype)

    @pl.when(me == peers - 1)
    def _():
        hi_ref[...] = jnp.zeros(hi_ref.shape, hi_ref.dtype)

    for copy in copies:
        copy.wait()

    @pl.when(me < peers - 1)
    def _():
        down.wait_send()
        up.wait_recv()

    @pl.when(me > 0)
    def _():
        up.wait_send()
        down.wait_recv()


def exchange_patch(packed, top, bottom):
    peers = lax.axis_size("patch")
    vmem = pl.BlockSpec(memory_space=pltpu.VMEM)
    return pl.pallas_call(
        lambda *refs: exchange_kernel(peers, *refs),
        out_shape=(
            jax.ShapeDtypeStruct((peers,) + packed.shape, packed.dtype),
            jax.ShapeDtypeStruct(top.shape, top.dtype),
            jax.ShapeDtypeStruct(top.shape, top.dtype),
        ),
        in_specs=[vmem] * 3,
        out_specs=(vmem, vmem, vmem),
        scratch_shapes=[
            pltpu.SemaphoreType.DMA((peers,)),
            pltpu.SemaphoreType.DMA((peers,)),
            pltpu.SemaphoreType.DMA((2,)),
            pltpu.SemaphoreType.DMA((2,)),
        ],
        compiler_params=pltpu.CompilerParams(
            collective_id=0 if top.dtype == jnp.bfloat16 else 1, has_side_effects=True
        ),
        name="exchange_stats_rows",
    )(packed, top, bottom)


def group_moments(values, rows):
    batch_size, height, chan_count, col_count = values.shape
    grouped = values.reshape(batch_size, height, GROUPS, chan_count // GROUPS, col_count)
    local_count = chan_count // GROUPS * height * col_count
    peers = lax.axis_size("patch")
    local_sum = jnp.sum(grouped, axis=(1, 3, 4))
    local_center = local_sum / local_count
    local_dev = jnp.sum(
        jnp.square(grouped - local_center[:, None, :, None, None]), axis=(1, 3, 4)
    )
    flat = jnp.concatenate([local_sum.reshape(-1), local_dev.reshape(-1)])
    width = 128 * ((flat.shape[0] + 127) // 128)
    packed = jnp.pad(flat, (0, width - flat.shape[0]))[None]
    every, low, high = exchange_patch(packed, rows[:, 0], rows[:, height - 1])
    every = every.reshape(peers, width)
    half = batch_size * GROUPS
    sums = every[:, :half].reshape(peers, batch_size, GROUPS)
    devs = every[:, half : 2 * half].reshape(peers, batch_size, GROUPS)
    cell_count = local_count * peers
    center = jnp.sum(sums, axis=0) / cell_count
    between = jnp.sum(jnp.square(sums / local_count - center[None]), axis=0) * local_count
    spread = (jnp.sum(devs, axis=0) + between) / cell_count
    return (center, jnp.sqrt(spread + epsilon)), low, high


def act_with_rows(values, rows, gain, shift):
    moments, low, high = group_moments(values, rows)
    full = jnp.concatenate(
        [low[:, None].astype(jnp.float32), values, high[:, None].astype(jnp.float32)], axis=1
    )
    act = norm_silu(full, moments, gain, shift)
    me = lax.axis_index("patch")
    row = lax.broadcasted_iota(jnp.int32, (1, full.shape[1], 1, 1), 1)
    pad = ((row == 0) & (me == 0)) | ((row == full.shape[1] - 1) & (me == lax.axis_size("patch") - 1))
    return jnp.where(pad, 0.0, act).astype(jnp.bfloat16)


def scatter_kernel(count, x_ref, o_ref, send_sem, recv_sem):
    seg = lax.axis_index("segment")
    me = lax.axis_index("patch")
    last = count - 1
    mesh_ids = pl.DeviceIdType.MESH
    barrier = pltpu.get_barrier_semaphore()

    @pl.when(seg == last)
    def _():
        for target in range(last):
            pl.semaphore_signal(barrier, 1, device_id=(target, me), device_id_type=mesh_ids)
        pl.semaphore_wait(barrier, last)
        copies = []
        for target in range(last):
            copy = pltpu.make_async_remote_copy(
                src_ref=x_ref.at[target],
                dst_ref=o_ref,
                send_sem=send_sem.at[target],
                recv_sem=recv_sem.at[0],
                device_id=(target, me),
                device_id_type=mesh_ids,
            )
            copy.start()
            copies.append(copy)
        o_ref[...] = x_ref[last]
        for copy in copies:
            copy.wait_send()

    @pl.when(seg != last)
    def _():
        pl.semaphore_signal(barrier, 1, device_id=(last, me), device_id_type=mesh_ids)
        pl.semaphore_wait(barrier, 1)
        pltpu.make_async_remote_copy(
            src_ref=x_ref.at[0],
            dst_ref=o_ref,
            send_sem=send_sem.at[0],
            recv_sem=recv_sem.at[0],
            device_id=(last, me),
            device_id_type=mesh_ids,
        ).wait_recv()


def scatter_from_last(pieces):
    count = lax.axis_size("segment")
    vmem = pl.BlockSpec(memory_space=pltpu.VMEM)
    return pl.pallas_call(
        lambda *refs: scatter_kernel(count, *refs),
        out_shape=jax.ShapeDtypeStruct(pieces.shape[1:], pieces.dtype),
        in_specs=[vmem],
        out_specs=vmem,
        scratch_shapes=[pltpu.SemaphoreType.DMA((count,)), pltpu.SemaphoreType.DMA((1,))],
        compiler_params=pltpu.CompilerParams(collective_id=2, has_side_effects=True),
        name="scatter_latent_columns",
    )(pieces)


def norm_silu(values, moments, gain, shift):
    center, root_spread = moments
    batch_size, height, chan_count, col_count = values.shape
    grouped = values.reshape(batch_size, height, GROUPS, chan_count // GROUPS, col_count)
    normed = (
        (grouped - center[:, None, :, None, None]) / root_spread[:, None, :, None, None]
    ).reshape(values.shape)
    normed = normed * gain[None, None, :, None] + shift[None, None, :, None]
    return jax.nn.silu(normed)


def conv_kernel(x_ref, w_ref, o_ref):
    batch, rows = o_ref.shape[0], o_ref.shape[1]
    for b in range(batch):
        for r in range(rows):
            acc = None
            for tap in range(9):
                part = jnp.dot(
                    w_ref[tap], x_ref[tap % 3, b, r + tap // 3], preferred_element_type=jnp.float32
                )
                acc = part if acc is None else acc + part
            o_ref[b, r] = acc


def fused_kernel(flags_ref, vals_ref, lo_ref, hi_ref, stat_ref, par_ref, w_ref, *rest):
    if len(rest) == 3:
        res_ref, o_ref, act_ref = rest
    else:
        res_ref = None
        o_ref, act_ref = rest
    rows, chans, cols = vals_ref.shape
    mean = stat_ref[0]
    std = stat_ref[1]
    gain = par_ref[0]
    shift = par_ref[1]
    col = lax.broadcasted_iota(jnp.int32, (chans, cols), 1)

    def put(slot, values, keep):
        normed = (values.astype(jnp.float32) - mean) / std * gain + shift
        act = normed / (1.0 + jnp.exp(-normed))
        act = jnp.where(keep, act, 0.0).astype(jnp.bfloat16).astype(jnp.float32)
        act_ref[slot, 1] = act.astype(jnp.bfloat16)
        left = jnp.where(col == 0, 0.0, pltpu.roll(act, 1, 1))
        act_ref[slot, 0] = left.astype(jnp.bfloat16)
        right = jnp.where(col == cols - 1, 0.0, pltpu.roll(act, cols - 1, 1))
        act_ref[slot, 2] = right.astype(jnp.bfloat16)

    put(0, lo_ref[...], flags_ref[0] > 0)
    for r in range(rows):
        put(r + 1, vals_ref[r], True)
    put(rows + 1, hi_ref[...], flags_ref[1] > 0)
    for r in range(rows):
        acc = None
        for tap in range(9):
            part = jnp.dot(
                w_ref[tap], act_ref[r + tap // 3, tap % 3], preferred_element_type=jnp.float32
            )
            acc = part if acc is None else acc + part
        if res_ref is not None:
            acc = res_ref[r].astype(jnp.float32) + acc
        o_ref[r] = acc.astype(o_ref.dtype)


def norm_conv(values, moments, low, high, params, norm_no, weights, block, residual=None):
    batch, rows, chans, cols = values.shape
    outs = weights.shape[-2]
    center, root_spread = moments
    per_group = chans // GROUPS
    stats_c = jnp.broadcast_to(
        jnp.repeat(jnp.stack([center, root_spread], axis=1), per_group, axis=2)[..., None],
        (batch, 2, chans, cols),
    )
    me = lax.axis_index("patch")
    flags = jnp.stack([me > 0, me < lax.axis_size("patch") - 1]).astype(jnp.int32)
    flops = 2 * 9 * batch * rows * cols * chans * outs
    row_spec = pl.BlockSpec((None, chans, cols), lambda b: (b, 0, 0))
    block_spec = pl.BlockSpec((None, rows, chans, cols), lambda b: (b, 0, 0, 0))
    operands = [flags, values, low, high, stats_c, params, weights]
    in_specs = [
        pl.BlockSpec(memory_space=pltpu.SMEM),
        block_spec,
        row_spec,
        row_spec,
        pl.BlockSpec((None, 2, chans, cols), lambda b: (b, 0, 0, 0)),
        pl.BlockSpec((None, None, 2, chans, cols), lambda b: (block, norm_no, 0, 0, 0)),
        pl.BlockSpec((None, None) + weights.shape[2:], lambda b: (0, block, 0, 0, 0)),
    ]
    out_dtype = jnp.float32
    if residual is not None:
        operands.append(residual)
        in_specs.append(block_spec)
        out_dtype = residual.dtype
    return pl.pallas_call(
        fused_kernel,
        grid=(batch,),
        out_shape=jax.ShapeDtypeStruct((batch, rows, outs, cols), out_dtype),
        in_specs=in_specs,
        out_specs=pl.BlockSpec((None, rows, outs, cols), lambda b: (b, 0, 0, 0)),
        scratch_shapes=[pltpu.VMEM((rows + 2, 3, chans, cols), jnp.bfloat16)],
        cost_estimate=pl.CostEstimate(
            flops=flops,
            transcendentals=batch * (rows + 2) * chans * cols,
            bytes_accessed=values.size * values.dtype.itemsize + 9 * chans * outs * 2 + batch * rows * outs * cols * 4,
        ),
        name="norm_conv3x3_rows",
    )(*operands)


def conv_valid(rows_in, kernel):
    padded = jnp.pad(rows_in, ((0, 0), (0, 0), (0, 0), (1, 1)))
    height = rows_in.shape[1] - 2
    col_count = rows_in.shape[3]
    accum = jnp.zeros((rows_in.shape[0], height, kernel.shape[1], col_count), jnp.float32)
    for tap_no in range(9):
        row_off, col_off = (tap_no // 3, tap_no % 3)
        window = padded[:, row_off : row_off + height, :, col_off : col_off + col_count]
        accum = accum + jnp.einsum(
            "oi,bhiw->bhow", kernel[tap_no], window, preferred_element_type=jnp.float32
        )
    return accum


def resnet_unit(hidden, conv1_w, conv2_w, block, params):
    moments, low, high = group_moments(hidden.astype(jnp.float32), hidden)
    middle = norm_conv(hidden, moments, low, high, params, 0, conv1_w, block)
    moments, low, high = group_moments(middle, middle)
    return norm_conv(middle, moments, low, high, params, 1, conv2_w, block, residual=hidden)


def head_noise(source, head_w, head_gain, head_shift):
    head_input = act_with_rows(source.astype(jnp.float32), source, head_gain, head_shift)
    return jnp.transpose(conv_taps_after(head_input, head_w), (0, 2, 1, 3))


def conv_stacked(rows_in, kernel):
    padded = jnp.pad(rows_in, ((0, 0), (0, 0), (0, 0), (1, 1)))
    height = rows_in.shape[1] - 2
    col_count = rows_in.shape[3]
    windows = jnp.concatenate(
        [
            padded[:, tap // 3 : tap // 3 + height, :, tap % 3 : tap % 3 + col_count]
            for tap in range(9)
        ],
        axis=2,
    )
    flat = jnp.transpose(kernel, (1, 0, 2)).reshape(kernel.shape[1], -1)
    return jnp.einsum("ok,bhkw->bhow", flat, windows, preferred_element_type=jnp.float32)


def conv_taps_after(rows_in, kernel):
    batch, rows_halo, chans, cols = rows_in.shape
    height = rows_halo - 2
    outs = kernel.shape[1]
    stacked = kernel.reshape(9 * outs, chans)
    partial = jnp.einsum("kc,bhcw->bhkw", stacked, rows_in, preferred_element_type=jnp.float32)
    partial = jnp.pad(partial, ((0, 0), (0, 0), (0, 0), (1, 1)))
    accum = jnp.zeros((batch, height, outs, cols), jnp.float32)
    for tap in range(9):
        row_off, col_off = (tap // 3, tap % 3)
        accum = accum + partial[
            :, row_off : row_off + height, tap * outs : (tap + 1) * outs, col_off : col_off + cols
        ]
    return accum


def with_rows(values):
    return with_halo(values, (("patch", 1),), 1)


def per_device(
    features,
    latent,
    plan_pos,
    blocks_used,
    conv1_w,
    conv2_w,
    norm_gain,
    norm_shift,
    in_w,
    head_w,
    head_gain,
    head_shift,
):
    segment_count = lax.axis_size("segment")
    segment_pos = lax.axis_index("segment")
    last = segment_count - 1
    current = jnp.transpose(features[0], (0, 2, 1, 3))
    params = jnp.broadcast_to(
        jnp.stack([norm_gain[0], norm_shift[0]], axis=2)[..., None],
        norm_gain.shape[1:3] + (2, norm_gain.shape[3], features.shape[4]),
    )
    for step_no in range(STEPS):
        arrived = from_behind(current, "segment", 1)
        noise_local = lax.cond(
            segment_pos == last,
            lambda source: head_noise(source, head_w, head_gain, head_shift),
            lambda source: jnp.zeros(latent.shape, jnp.float32),
            current,
        )
        position = plan_pos + step_no
        sigma_now = sigma_at(position)
        sigma_next = sigma_at(position + 1)
        latent = latent + (sigma_next - sigma_now)[:, None, None, None] * noise_local
        scaled = (latent / jnp.sqrt(sigma_next * sigma_next + 1.0)[:, None, None, None]).astype(
            jnp.bfloat16
        )
        scaled_rows = jnp.transpose(scaled, (0, 2, 1, 3))
        peers = lax.axis_size("patch")
        origin = last * peers
        height = scaled_rows.shape[1]
        body = lax.ppermute(
            scaled_rows, ("segment", "patch"), [(origin + p, p) for p in range(peers)]
        )
        above = lax.ppermute(
            scaled_rows[:, height - 1 :],
            ("segment", "patch"),
            [(origin + p, p + 1) for p in range(peers - 1)],
        )
        below = lax.ppermute(
            scaled_rows[:, :1], ("segment", "patch"), [(origin + p, p - 1) for p in range(1, peers)]
        )
        entry_rows = conv_stacked(
            jnp.concatenate([above, body, below], axis=1), in_w
        ).astype(jnp.bfloat16)
        source = jnp.where(segment_pos == 0, entry_rows, arrived)
        after_one = resnet_unit(source, conv1_w, conv2_w, 0, params)
        current = lax.cond(
            blocks_used[0] >= 2,
            lambda hidden: resnet_unit(hidden, conv1_w, conv2_w, 1, params),
            lambda hidden: hidden,
            after_one,
        )
    batch_size, lat_count, height, col_count = latent.shape
    col_share = col_count // segment_count
    latent, current = lax.optimization_barrier((latent, current))
    pieces = latent.reshape(batch_size, lat_count, height, segment_count, col_share)
    pieces = jnp.transpose(pieces, (3, 0, 1, 2, 4)).reshape(segment_count, -1, 128)
    latent_part = scatter_from_last(pieces).reshape(batch_size, lat_count, height, col_share)
    return (latent_part, jnp.transpose(current, (0, 2, 1, 3))[None])


def solution(mesh):
    placed = (
        P("segment", None, None, "patch", None),
        P(None, None, "patch", None),
        P(),
        P("segment"),
        P("segment", None, None, None, None),
        P("segment", None, None, None, None),
        P("segment", None, None, None),
        P("segment", None, None, None),
        P(),
        P(),
        P(),
        P(),
    )
    return jax.shard_map(
        per_device,
        mesh=mesh,
        in_specs=placed,
        out_specs=(P(None, None, "patch", "segment"), P("segment", None, None, "patch", None)),
        check_vma=False,
    )
```

```python
import jax
import jax.numpy as jnp
from jax import lax
from jax.sharding import PartitionSpec as P
from jax.experimental import pallas as pl
from jax.experimental.pallas import tpu as pltpu

GROUPS = 32
STEPS = 2
SCHED = 12


epsilon = 1e-05
sigma_top = 3.0
sigma_low = 0.1
rho_power = 7.0


def with_halo(block, sides, width):
    for axis, dim in sides:
        count = lax.axis_size(axis)
        forward = [(i, i + 1) for i in range(count - 1)]
        backward = [(target, source) for source, target in forward]
        low = lax.ppermute(
            lax.slice_in_dim(block, block.shape[dim] - width, None, axis=dim), axis, forward
        )
        high = lax.ppermute(lax.slice_in_dim(block, 0, width, axis=dim), axis, backward)
        block = jnp.concatenate([low, block, high], axis=dim)
    return block


def from_behind(shard, axis, by):
    devices = lax.axis_size(axis)
    pairs = [(i, i + by) for i in range(devices) if 0 <= i + by < devices]
    return lax.ppermute(shard, axis, pairs)


def broadcast(shard, axis, root):
    mine = lax.axis_index(axis) == root
    return lax.psum(jnp.where(mine, shard, jnp.zeros_like(shard)), axis)


def sigma_at(position):
    fraction = position.astype(jnp.float32) / (SCHED - 1)
    top_root = sigma_top ** (1.0 / rho_power)
    low_root = sigma_low ** (1.0 / rho_power)
    return (top_root + fraction * (low_root - top_root)) ** rho_power


def exchange_kernel(
    peers, x_ref, top_ref, bot_ref, o_ref, lo_ref, hi_ref, send_sem, recv_sem, row_send, row_recv
):
    me = lax.axis_index("patch")
    seg = lax.axis_index("segment")
    mesh_ids = pl.DeviceIdType.MESH
    barrier = pltpu.get_barrier_semaphore()
    for dist in range(1, peers):
        pl.semaphore_signal(
            barrier, 1, device_id=(seg, lax.rem(me + dist, peers)), device_id_type=mesh_ids
        )
    pl.semaphore_wait(barrier, peers - 1)
    down = pltpu.make_async_remote_copy(
        src_ref=bot_ref,
        dst_ref=lo_ref,
        send_sem=row_send.at[0],
        recv_sem=row_recv.at[0],
        device_id=(seg, jnp.minimum(me + 1, peers - 1)),
        device_id_type=mesh_ids,
    )
    up = pltpu.make_async_remote_copy(
        src_ref=top_ref,
        dst_ref=hi_ref,
        send_sem=row_send.at[1],
        recv_sem=row_recv.at[1],
        device_id=(seg, jnp.maximum(me - 1, 0)),
        device_id_type=mesh_ids,
    )

    @pl.when(me < peers - 1)
    def _():
        down.start()

    @pl.when(me > 0)
    def _():
        up.start()

    copies = []
    for dist in range(1, peers):
        copy = pltpu.make_async_remote_copy(
            src_ref=x_ref,
            dst_ref=o_ref.at[me],
            send_sem=send_sem.at[dist],
            recv_sem=recv_sem.at[dist],
            device_id=(seg, lax.rem(me + dist, peers)),
            device_id_type=mesh_ids,
        )
        copy.start()
        copies.append(copy)
    o_ref[me] = x_ref[...]

    @pl.when(me == 0)
    def _():
        lo_ref[...] = jnp.zeros(lo_ref.shape, lo_ref.dtype)

    @pl.when(me == peers - 1)
    def _():
        hi_ref[...] = jnp.zeros(hi_ref.shape, hi_ref.dtype)

    for copy in copies:
        copy.wait()

    @pl.when(me < peers - 1)
    def _():
        down.wait_send()
        up.wait_recv()

    @pl.when(me > 0)
    def _():
        up.wait_send()
        down.wait_recv()


def exchange_patch(packed, top, bottom):
    peers = lax.axis_size("patch")
    vmem = pl.BlockSpec(memory_space=pltpu.VMEM)
    return pl.pallas_call(
        lambda *refs: exchange_kernel(peers, *refs),
        out_shape=(
            jax.ShapeDtypeStruct((peers,) + packed.shape, packed.dtype),
            jax.ShapeDtypeStruct(top.shape, top.dtype),
            jax.ShapeDtypeStruct(top.shape, top.dtype),
        ),
        in_specs=[vmem] * 3,
        out_specs=(vmem, vmem, vmem),
        scratch_shapes=[
            pltpu.SemaphoreType.DMA((peers,)),
            pltpu.SemaphoreType.DMA((peers,)),
            pltpu.SemaphoreType.DMA((2,)),
            pltpu.SemaphoreType.DMA((2,)),
        ],
        compiler_params=pltpu.CompilerParams(
            collective_id=0 if top.dtype == jnp.bfloat16 else 1, has_side_effects=True
        ),
        name="exchange_stats_rows",
    )(packed, top, bottom)


def group_moments(values, rows):
    batch_size, height, chan_count, col_count = values.shape
    grouped = values.reshape(batch_size, height, GROUPS, chan_count // GROUPS, col_count)
    local_count = chan_count // GROUPS * height * col_count
    peers = lax.axis_size("patch")
    local_sum = jnp.sum(grouped, axis=(1, 3, 4))
    local_center = local_sum / local_count
    local_dev = jnp.sum(
        jnp.square(grouped - local_center[:, None, :, None, None]), axis=(1, 3, 4)
    )
    flat = jnp.concatenate([local_sum.reshape(-1), local_dev.reshape(-1)])
    width = 128 * ((flat.shape[0] + 127) // 128)
    packed = jnp.pad(flat, (0, width - flat.shape[0]))[None]
    every, low, high = exchange_patch(packed, rows[:, 0], rows[:, height - 1])
    every = every.reshape(peers, width)
    half = batch_size * GROUPS
    sums = every[:, :half].reshape(peers, batch_size, GROUPS)
    devs = every[:, half : 2 * half].reshape(peers, batch_size, GROUPS)
    cell_count = local_count * peers
    center = jnp.sum(sums, axis=0) / cell_count
    between = jnp.sum(jnp.square(sums / local_count - center[None]), axis=0) * local_count
    spread = (jnp.sum(devs, axis=0) + between) / cell_count
    return (center, jnp.sqrt(spread + epsilon)), low, high


def act_with_rows(values, rows, gain, shift):
    moments, low, high = group_moments(values, rows)
    full = jnp.concatenate(
        [low[:, None].astype(jnp.float32), values, high[:, None].astype(jnp.float32)], axis=1
    )
    act = norm_silu(full, moments, gain, shift)
    me = lax.axis_index("patch")
    row = lax.broadcasted_iota(jnp.int32, (1, full.shape[1], 1, 1), 1)
    pad = ((row == 0) & (me == 0)) | ((row == full.shape[1] - 1) & (me == lax.axis_size("patch") - 1))
    return jnp.where(pad, 0.0, act).astype(jnp.bfloat16)


def scatter_kernel(count, x_ref, o_ref, send_sem, recv_sem):
    seg = lax.axis_index("segment")
    me = lax.axis_index("patch")
    last = count - 1
    mesh_ids = pl.DeviceIdType.MESH
    barrier = pltpu.get_barrier_semaphore()

    @pl.when(seg == last)
    def _():
        for target in range(last):
            pl.semaphore_signal(barrier, 1, device_id=(target, me), device_id_type=mesh_ids)
        pl.semaphore_wait(barrier, last)
        copies = []
        for target in range(last):
            copy = pltpu.make_async_remote_copy(
                src_ref=x_ref.at[target],
                dst_ref=o_ref,
                send_sem=send_sem.at[target],
                recv_sem=recv_sem.at[0],
                device_id=(target, me),
                device_id_type=mesh_ids,
            )
            copy.start()
            copies.append(copy)
        o_ref[...] = x_ref[last]
        for copy in copies:
            copy.wait_send()

    @pl.when(seg != last)
    def _():
        pl.semaphore_signal(barrier, 1, device_id=(last, me), device_id_type=mesh_ids)
        pl.semaphore_wait(barrier, 1)
        pltpu.make_async_remote_copy(
            src_ref=x_ref.at[0],
            dst_ref=o_ref,
            send_sem=send_sem.at[0],
            recv_sem=recv_sem.at[0],
            device_id=(last, me),
            device_id_type=mesh_ids,
        ).wait_recv()


def scatter_from_last(pieces):
    count = lax.axis_size("segment")
    vmem = pl.BlockSpec(memory_space=pltpu.VMEM)
    return pl.pallas_call(
        lambda *refs: scatter_kernel(count, *refs),
        out_shape=jax.ShapeDtypeStruct(pieces.shape[1:], pieces.dtype),
        in_specs=[vmem],
        out_specs=vmem,
        scratch_shapes=[pltpu.SemaphoreType.DMA((count,)), pltpu.SemaphoreType.DMA((1,))],
        compiler_params=pltpu.CompilerParams(collective_id=2, has_side_effects=True),
        name="scatter_latent_columns",
    )(pieces)


def norm_silu(values, moments, gain, shift):
    center, root_spread = moments
    batch_size, height, chan_count, col_count = values.shape
    grouped = values.reshape(batch_size, height, GROUPS, chan_count // GROUPS, col_count)
    normed = (
        (grouped - center[:, None, :, None, None]) / root_spread[:, None, :, None, None]
    ).reshape(values.shape)
    normed = normed * gain[None, None, :, None] + shift[None, None, :, None]
    return jax.nn.silu(normed)


def conv_kernel(x_ref, w_ref, o_ref):
    batch, rows = o_ref.shape[0], o_ref.shape[1]
    for b in range(batch):
        for r in range(rows):
            acc = None
            for tap in range(9):
                part = jnp.dot(
                    w_ref[tap], x_ref[tap % 3, b, r + tap // 3], preferred_element_type=jnp.float32
                )
                acc = part if acc is None else acc + part
            o_ref[b, r] = acc


def fused_kernel(flags_ref, vals_ref, lo_ref, hi_ref, stat_ref, par_ref, w_ref, *rest):
    if len(rest) == 3:
        res_ref, o_ref, act_ref = rest
    else:
        res_ref = None
        o_ref, act_ref = rest
    rows, chans, cols = vals_ref.shape
    mean = stat_ref[0]
    std = stat_ref[1]
    gain = par_ref[0]
    shift = par_ref[1]
    col = lax.broadcasted_iota(jnp.int32, (chans, cols), 1)

    def put(slot, values, keep):
        normed = (values.astype(jnp.float32) - mean) / std * gain + shift
        act = normed / (1.0 + jnp.exp(-normed))
        act = jnp.where(keep, act, 0.0).astype(jnp.bfloat16).astype(jnp.float32)
        act_ref[slot, 1] = act.astype(jnp.bfloat16)
        left = jnp.where(col == 0, 0.0, pltpu.roll(act, 1, 1))
        act_ref[slot, 0] = left.astype(jnp.bfloat16)
        right = jnp.where(col == cols - 1, 0.0, pltpu.roll(act, cols - 1, 1))
        act_ref[slot, 2] = right.astype(jnp.bfloat16)

    put(0, lo_ref[...], flags_ref[0] > 0)
    for r in range(rows):
        put(r + 1, vals_ref[r], True)
    put(rows + 1, hi_ref[...], flags_ref[1] > 0)
    for r in range(rows):
        acc = None
        for tap in range(9):
            part = jnp.dot(
                w_ref[tap], act_ref[r + tap // 3, tap % 3], preferred_element_type=jnp.float32
            )
            acc = part if acc is None else acc + part
        if res_ref is not None:
            acc = res_ref[r].astype(jnp.float32) + acc
        o_ref[r] = acc.astype(o_ref.dtype)


EDGE_FLAGS = [None]


def norm_conv(values, moments, low, high, params, norm_no, weights, block, residual=None):
    batch, rows, chans, cols = values.shape
    outs = weights.shape[-2]
    center, root_spread = moments
    per_group = chans // GROUPS
    stats_c = jnp.repeat(jnp.stack([center, root_spread], axis=1), per_group, axis=2)[..., None]
    flags = EDGE_FLAGS[0]
    flops = 2 * 9 * batch * rows * cols * chans * outs
    row_spec = pl.BlockSpec((None, chans, cols), lambda b: (b, 0, 0))
    block_spec = pl.BlockSpec((None, rows, chans, cols), lambda b: (b, 0, 0, 0))
    operands = [flags, values, low, high, stats_c, params, weights]
    in_specs = [
        pl.BlockSpec(memory_space=pltpu.SMEM),
        block_spec,
        row_spec,
        row_spec,
        pl.BlockSpec((None, 2, chans, 1), lambda b: (b, 0, 0, 0)),
        pl.BlockSpec((None, None, 2, chans, cols), lambda b: (block, norm_no, 0, 0, 0)),
        pl.BlockSpec((None, None) + weights.shape[2:], lambda b: (0, block, 0, 0, 0)),
    ]
    out_dtype = jnp.float32
    if residual is not None:
        operands.append(residual)
        in_specs.append(block_spec)
        out_dtype = residual.dtype
    return pl.pallas_call(
        fused_kernel,
        grid=(batch,),
        out_shape=jax.ShapeDtypeStruct((batch, rows, outs, cols), out_dtype),
        in_specs=in_specs,
        out_specs=pl.BlockSpec((None, rows, outs, cols), lambda b: (b, 0, 0, 0)),
        scratch_shapes=[pltpu.VMEM((rows + 2, 3, chans, cols), jnp.bfloat16)],
        cost_estimate=pl.CostEstimate(
            flops=flops,
            transcendentals=batch * (rows + 2) * chans * cols,
            bytes_accessed=values.size * values.dtype.itemsize + 9 * chans * outs * 2 + batch * rows * outs * cols * 4,
        ),
        name="norm_conv3x3_rows",
    )(*operands)


def conv_valid(rows_in, kernel):
    padded = jnp.pad(rows_in, ((0, 0), (0, 0), (0, 0), (1, 1)))
    height = rows_in.shape[1] - 2
    col_count = rows_in.shape[3]
    accum = jnp.zeros((rows_in.shape[0], height, kernel.shape[1], col_count), jnp.float32)
    for tap_no in range(9):
        row_off, col_off = (tap_no // 3, tap_no % 3)
        window = padded[:, row_off : row_off + height, :, col_off : col_off + col_count]
        accum = accum + jnp.einsum(
            "oi,bhiw->bhow", kernel[tap_no], window, preferred_element_type=jnp.float32
        )
    return accum


def resnet_unit(hidden, conv1_w, conv2_w, block, params):
    moments, low, high = group_moments(hidden.astype(jnp.float32), hidden)
    middle = norm_conv(hidden, moments, low, high, params, 0, conv1_w, block)
    moments, low, high = group_moments(middle, middle)
    return norm_conv(middle, moments, low, high, params, 1, conv2_w, block, residual=hidden)


def head_noise(source, head_w, head_gain, head_shift):
    head_input = act_with_rows(source.astype(jnp.float32), source, head_gain, head_shift)
    return jnp.transpose(conv_taps_after(head_input, head_w), (0, 2, 1, 3))


def conv_stacked(rows_in, kernel):
    padded = jnp.pad(rows_in, ((0, 0), (0, 0), (0, 0), (1, 1)))
    height = rows_in.shape[1] - 2
    col_count = rows_in.shape[3]
    windows = jnp.concatenate(
        [
            padded[:, tap // 3 : tap // 3 + height, :, tap % 3 : tap % 3 + col_count]
            for tap in range(9)
        ],
        axis=2,
    )
    flat = jnp.transpose(kernel, (1, 0, 2)).reshape(kernel.shape[1], -1)
    return jnp.einsum("ok,bhkw->bhow", flat, windows, preferred_element_type=jnp.float32)


def conv_taps_after(rows_in, kernel):
    batch, rows_halo, chans, cols = rows_in.shape
    height = rows_halo - 2
    outs = kernel.shape[1]
    stacked = kernel.reshape(9 * outs, chans)
    partial = jnp.einsum("kc,bhcw->bhkw", stacked, rows_in, preferred_element_type=jnp.float32)
    partial = jnp.pad(partial, ((0, 0), (0, 0), (0, 0), (1, 1)))
    accum = jnp.zeros((batch, height, outs, cols), jnp.float32)
    for tap in range(9):
        row_off, col_off = (tap // 3, tap % 3)
        accum = accum + partial[
            :, row_off : row_off + height, tap * outs : (tap + 1) * outs, col_off : col_off + cols
        ]
    return accum


def with_rows(values):
    return with_halo(values, (("patch", 1),), 1)


def per_device(
    features,
    latent,
    plan_pos,
    blocks_used,
    conv1_w,
    conv2_w,
    norm_gain,
    norm_shift,
    in_w,
    head_w,
    head_gain,
    head_shift,
):
    segment_count = lax.axis_size("segment")
    segment_pos = lax.axis_index("segment")
    last = segment_count - 1
    current = jnp.transpose(features[0], (0, 2, 1, 3))
    patch_pos = lax.axis_index("patch")
    EDGE_FLAGS[0] = jnp.stack([patch_pos > 0, patch_pos < lax.axis_size("patch") - 1]).astype(
        jnp.int32
    )
    params = jnp.broadcast_to(
        jnp.stack([norm_gain[0], norm_shift[0]], axis=2)[..., None],
        norm_gain.shape[1:3] + (2, norm_gain.shape[3], features.shape[4]),
    )
    for step_no in range(STEPS):
        arrived = from_behind(current, "segment", 1)
        noise_local = lax.cond(
            segment_pos == last,
            lambda source: head_noise(source, head_w, head_gain, head_shift),
            lambda source: jnp.zeros(latent.shape, jnp.float32),
            current,
        )
        position = plan_pos + step_no
        sigma_now = sigma_at(position)
        sigma_next = sigma_at(position + 1)
        latent = latent + (sigma_next - sigma_now)[:, None, None, None] * noise_local
        scaled = (latent / jnp.sqrt(sigma_next * sigma_next + 1.0)[:, None, None, None]).astype(
            jnp.bfloat16
        )
        scaled_rows = jnp.transpose(scaled, (0, 2, 1, 3))
        peers = lax.axis_size("patch")
        origin = last * peers
        height = scaled_rows.shape[1]
        body = lax.ppermute(
            scaled_rows, ("segment", "patch"), [(origin + p, p) for p in range(peers)]
        )
        above = lax.ppermute(
            scaled_rows[:, height - 1 :],
            ("segment", "patch"),
            [(origin + p, p + 1) for p in range(peers - 1)],
        )
        below = lax.ppermute(
            scaled_rows[:, :1], ("segment", "patch"), [(origin + p, p - 1) for p in range(1, peers)]
        )
        entry_rows = conv_stacked(
            jnp.concatenate([above, body, below], axis=1), in_w
        ).astype(jnp.bfloat16)
        source = jnp.where(segment_pos == 0, entry_rows, arrived)
        after_one = resnet_unit(source, conv1_w, conv2_w, 0, params)
        current = lax.cond(
            blocks_used[0] >= 2,
            lambda hidden: resnet_unit(hidden, conv1_w, conv2_w, 1, params),
            lambda hidden: hidden,
            after_one,
        )
    batch_size, lat_count, height, col_count = latent.shape
    col_share = col_count // segment_count
    latent, current = lax.optimization_barrier((latent, current))
    pieces = latent.reshape(batch_size, lat_count, height, segment_count, col_share)
    pieces = jnp.transpose(pieces, (3, 0, 1, 2, 4)).reshape(segment_count, -1, 128)
    latent_part = scatter_from_last(pieces).reshape(batch_size, lat_count, height, col_share)
    return (latent_part, jnp.transpose(current, (0, 2, 1, 3))[None])


def solution(mesh):
    placed = (
        P("segment", None, None, "patch", None),
        P(None, None, "patch", None),
        P(),
        P("segment"),
        P("segment", None, None, None, None),
        P("segment", None, None, None, None),
        P("segment", None, None, None),
        P("segment", None, None, None),
        P(),
        P(),
        P(),
        P(),
    )
    return jax.shard_map(
        per_device,
        mesh=mesh,
        in_specs=placed,
        out_specs=(P(None, None, "patch", "segment"), P("segment", None, None, "patch", None)),
        check_vma=False,
    )
```

```python
import jax
import jax.numpy as jnp
from jax import lax
from jax.sharding import PartitionSpec as P
from jax.experimental import pallas as pl
from jax.experimental.pallas import tpu as pltpu

GROUPS = 32
STEPS = 2
SCHED = 12


epsilon = 1e-05
sigma_top = 3.0
sigma_low = 0.1
rho_power = 7.0


def with_halo(block, sides, width):
    for axis, dim in sides:
        count = lax.axis_size(axis)
        forward = [(i, i + 1) for i in range(count - 1)]
        backward = [(target, source) for source, target in forward]
        low = lax.ppermute(
            lax.slice_in_dim(block, block.shape[dim] - width, None, axis=dim), axis, forward
        )
        high = lax.ppermute(lax.slice_in_dim(block, 0, width, axis=dim), axis, backward)
        block = jnp.concatenate([low, block, high], axis=dim)
    return block


def from_behind(shard, axis, by):
    devices = lax.axis_size(axis)
    pairs = [(i, i + by) for i in range(devices) if 0 <= i + by < devices]
    return lax.ppermute(shard, axis, pairs)


def broadcast(shard, axis, root):
    mine = lax.axis_index(axis) == root
    return lax.psum(jnp.where(mine, shard, jnp.zeros_like(shard)), axis)


def sigma_at(position):
    fraction = position.astype(jnp.float32) / (SCHED - 1)
    top_root = sigma_top ** (1.0 / rho_power)
    low_root = sigma_low ** (1.0 / rho_power)
    return (top_root + fraction * (low_root - top_root)) ** rho_power


def exchange_kernel(
    peers, x_ref, top_ref, bot_ref, o_ref, lo_ref, hi_ref, send_sem, recv_sem, row_send, row_recv
):
    me = lax.axis_index("patch")
    seg = lax.axis_index("segment")
    mesh_ids = pl.DeviceIdType.MESH
    barrier = pltpu.get_barrier_semaphore()
    for dist in range(1, peers):
        pl.semaphore_signal(
            barrier, 1, device_id=(seg, lax.rem(me + dist, peers)), device_id_type=mesh_ids
        )
    pl.semaphore_wait(barrier, peers - 1)
    down = pltpu.make_async_remote_copy(
        src_ref=bot_ref,
        dst_ref=lo_ref,
        send_sem=row_send.at[0],
        recv_sem=row_recv.at[0],
        device_id=(seg, jnp.minimum(me + 1, peers - 1)),
        device_id_type=mesh_ids,
    )
    up = pltpu.make_async_remote_copy(
        src_ref=top_ref,
        dst_ref=hi_ref,
        send_sem=row_send.at[1],
        recv_sem=row_recv.at[1],
        device_id=(seg, jnp.maximum(me - 1, 0)),
        device_id_type=mesh_ids,
    )

    @pl.when(me < peers - 1)
    def _():
        down.start()

    @pl.when(me > 0)
    def _():
        up.start()

    copies = []
    for dist in range(1, peers):
        copy = pltpu.make_async_remote_copy(
            src_ref=x_ref,
            dst_ref=o_ref.at[me],
            send_sem=send_sem.at[dist],
            recv_sem=recv_sem.at[dist],
            device_id=(seg, lax.rem(me + dist, peers)),
            device_id_type=mesh_ids,
        )
        copy.start()
        copies.append(copy)
    o_ref[me] = x_ref[...]

    @pl.when(me == 0)
    def _():
        lo_ref[...] = jnp.zeros(lo_ref.shape, lo_ref.dtype)

    @pl.when(me == peers - 1)
    def _():
        hi_ref[...] = jnp.zeros(hi_ref.shape, hi_ref.dtype)

    for copy in copies:
        copy.wait()

    @pl.when(me < peers - 1)
    def _():
        down.wait_send()
        up.wait_recv()

    @pl.when(me > 0)
    def _():
        up.wait_send()
        down.wait_recv()


def exchange_patch(packed, top, bottom):
    peers = lax.axis_size("patch")
    vmem = pl.BlockSpec(memory_space=pltpu.VMEM)
    return pl.pallas_call(
        lambda *refs: exchange_kernel(peers, *refs),
        out_shape=(
            jax.ShapeDtypeStruct((peers,) + packed.shape, packed.dtype),
            jax.ShapeDtypeStruct(top.shape, top.dtype),
            jax.ShapeDtypeStruct(top.shape, top.dtype),
        ),
        in_specs=[vmem] * 3,
        out_specs=(vmem, vmem, vmem),
        scratch_shapes=[
            pltpu.SemaphoreType.DMA((peers,)),
            pltpu.SemaphoreType.DMA((peers,)),
            pltpu.SemaphoreType.DMA((2,)),
            pltpu.SemaphoreType.DMA((2,)),
        ],
        compiler_params=pltpu.CompilerParams(
            collective_id=0 if top.dtype == jnp.bfloat16 else 1, has_side_effects=True
        ),
        name="exchange_stats_rows",
    )(packed, top, bottom)


def group_moments(values, rows):
    batch_size, height, chan_count, col_count = values.shape
    grouped = values.reshape(batch_size, height, GROUPS, chan_count // GROUPS, col_count)
    local_count = chan_count // GROUPS * height * col_count
    peers = lax.axis_size("patch")
    local_sum = jnp.sum(grouped, axis=(1, 3, 4))
    local_center = local_sum / local_count
    local_dev = jnp.sum(
        jnp.square(grouped - local_center[:, None, :, None, None]), axis=(1, 3, 4)
    )
    flat = jnp.concatenate([local_sum.reshape(-1), local_dev.reshape(-1)])
    width = 128 * ((flat.shape[0] + 127) // 128)
    packed = jnp.pad(flat, (0, width - flat.shape[0]))[None]
    every, low, high = exchange_patch(packed, rows[:, 0], rows[:, height - 1])
    every = every.reshape(peers, width)
    half = batch_size * GROUPS
    sums = every[:, :half].reshape(peers, batch_size, GROUPS)
    devs = every[:, half : 2 * half].reshape(peers, batch_size, GROUPS)
    cell_count = local_count * peers
    center = jnp.sum(sums, axis=0) / cell_count
    between = jnp.sum(jnp.square(sums / local_count - center[None]), axis=0) * local_count
    spread = (jnp.sum(devs, axis=0) + between) / cell_count
    return (center, jnp.sqrt(spread + epsilon)), low, high


def act_with_rows(values, rows, gain, shift):
    moments, low, high = group_moments(values, rows)
    full = jnp.concatenate(
        [low[:, None].astype(jnp.float32), values, high[:, None].astype(jnp.float32)], axis=1
    )
    act = norm_silu(full, moments, gain, shift)
    me = lax.axis_index("patch")
    row = lax.broadcasted_iota(jnp.int32, (1, full.shape[1], 1, 1), 1)
    pad = ((row == 0) & (me == 0)) | ((row == full.shape[1] - 1) & (me == lax.axis_size("patch") - 1))
    return jnp.where(pad, 0.0, act).astype(jnp.bfloat16)


def scatter_kernel(count, x_ref, o_ref, send_sem, recv_sem):
    seg = lax.axis_index("segment")
    me = lax.axis_index("patch")
    last = count - 1
    mesh_ids = pl.DeviceIdType.MESH
    barrier = pltpu.get_barrier_semaphore()

    @pl.when(seg == last)
    def _():
        for target in range(last):
            pl.semaphore_signal(barrier, 1, device_id=(target, me), device_id_type=mesh_ids)
        pl.semaphore_wait(barrier, last)
        copies = []
        for target in range(last):
            copy = pltpu.make_async_remote_copy(
                src_ref=x_ref.at[target],
                dst_ref=o_ref,
                send_sem=send_sem.at[target],
                recv_sem=recv_sem.at[0],
                device_id=(target, me),
                device_id_type=mesh_ids,
            )
            copy.start()
            copies.append(copy)
        o_ref[...] = x_ref[last]
        for copy in copies:
            copy.wait_send()

    @pl.when(seg != last)
    def _():
        pl.semaphore_signal(barrier, 1, device_id=(last, me), device_id_type=mesh_ids)
        pl.semaphore_wait(barrier, 1)
        pltpu.make_async_remote_copy(
            src_ref=x_ref.at[0],
            dst_ref=o_ref,
            send_sem=send_sem.at[0],
            recv_sem=recv_sem.at[0],
            device_id=(last, me),
            device_id_type=mesh_ids,
        ).wait_recv()


def scatter_from_last(pieces):
    count = lax.axis_size("segment")
    vmem = pl.BlockSpec(memory_space=pltpu.VMEM)
    return pl.pallas_call(
        lambda *refs: scatter_kernel(count, *refs),
        out_shape=jax.ShapeDtypeStruct(pieces.shape[1:], pieces.dtype),
        in_specs=[vmem],
        out_specs=vmem,
        scratch_shapes=[pltpu.SemaphoreType.DMA((count,)), pltpu.SemaphoreType.DMA((1,))],
        compiler_params=pltpu.CompilerParams(collective_id=2, has_side_effects=True),
        name="scatter_latent_columns",
    )(pieces)


def norm_silu(values, moments, gain, shift):
    center, root_spread = moments
    batch_size, height, chan_count, col_count = values.shape
    grouped = values.reshape(batch_size, height, GROUPS, chan_count // GROUPS, col_count)
    normed = (
        (grouped - center[:, None, :, None, None]) / root_spread[:, None, :, None, None]
    ).reshape(values.shape)
    normed = normed * gain[None, None, :, None] + shift[None, None, :, None]
    return jax.nn.silu(normed)


def conv_kernel(x_ref, w_ref, o_ref):
    batch, rows = o_ref.shape[0], o_ref.shape[1]
    for b in range(batch):
        for r in range(rows):
            acc = None
            for tap in range(9):
                part = jnp.dot(
                    w_ref[tap], x_ref[tap % 3, b, r + tap // 3], preferred_element_type=jnp.float32
                )
                acc = part if acc is None else acc + part
            o_ref[b, r] = acc


def fused_kernel(flags_ref, vals_ref, lo_ref, hi_ref, stat_ref, par_ref, w_ref, *rest):
    if len(rest) == 3:
        res_ref, o_ref, act_ref = rest
    else:
        res_ref = None
        o_ref, act_ref = rest
    rows, chans, cols = vals_ref.shape
    mean = stat_ref[0]
    std = stat_ref[1]
    gain = par_ref[0]
    shift = par_ref[1]
    col = lax.broadcasted_iota(jnp.int32, (chans, cols), 1)

    def put(slot, values, keep):
        normed = (values.astype(jnp.float32) - mean) / std * gain + shift
        act = normed / (1.0 + jnp.exp(-normed))
        act = jnp.where(keep, act, 0.0).astype(jnp.bfloat16).astype(jnp.float32)
        act_ref[slot, 1] = act.astype(jnp.bfloat16)
        left = jnp.where(col == 0, 0.0, pltpu.roll(act, 1, 1))
        act_ref[slot, 0] = left.astype(jnp.bfloat16)
        right = jnp.where(col == cols - 1, 0.0, pltpu.roll(act, cols - 1, 1))
        act_ref[slot, 2] = right.astype(jnp.bfloat16)

    put(0, lo_ref[...], flags_ref[0] > 0)
    for r in range(rows):
        put(r + 1, vals_ref[r], True)
    put(rows + 1, hi_ref[...], flags_ref[1] > 0)
    for r in range(rows):
        acc = None
        for tap in range(9):
            part = jnp.dot(
                w_ref[tap], act_ref[r + tap // 3, tap % 3], preferred_element_type=jnp.float32
            )
            acc = part if acc is None else acc + part
        if res_ref is not None:
            acc = res_ref[r].astype(jnp.float32) + acc
        o_ref[r] = acc.astype(o_ref.dtype)


def norm_conv(values, moments, low, high, params, norm_no, weights, block, residual=None):
    batch, rows, chans, cols = values.shape
    outs = weights.shape[-2]
    center, root_spread = moments
    per_group = chans // GROUPS
    stats_c = jnp.repeat(jnp.stack([center, root_spread], axis=1), per_group, axis=2)[..., None]
    me = lax.axis_index("patch")
    flags = jnp.stack([me > 0, me < lax.axis_size("patch") - 1]).astype(jnp.int32)
    flops = 2 * 9 * batch * rows * cols * chans * outs
    row_spec = pl.BlockSpec((None, chans, cols), lambda b: (b, 0, 0))
    block_spec = pl.BlockSpec((None, rows, chans, cols), lambda b: (b, 0, 0, 0))
    operands = [flags, values, low, high, stats_c, params, weights]
    in_specs = [
        pl.BlockSpec(memory_space=pltpu.SMEM),
        block_spec,
        row_spec,
        row_spec,
        pl.BlockSpec((None, 2, chans, 1), lambda b: (b, 0, 0, 0)),
        pl.BlockSpec((None, None, 2, chans, cols), lambda b: (block, norm_no, 0, 0, 0)),
        pl.BlockSpec((None, None) + weights.shape[2:], lambda b: (0, block, 0, 0, 0)),
    ]
    out_dtype = jnp.float32
    if residual is not None:
        operands.append(residual)
        in_specs.append(block_spec)
        out_dtype = residual.dtype
    return pl.pallas_call(
        fused_kernel,
        grid=(batch,),
        out_shape=jax.ShapeDtypeStruct((batch, rows, outs, cols), out_dtype),
        in_specs=in_specs,
        out_specs=pl.BlockSpec((None, rows, outs, cols), lambda b: (b, 0, 0, 0)),
        scratch_shapes=[pltpu.VMEM((rows + 2, 3, chans, cols), jnp.bfloat16)],
        cost_estimate=pl.CostEstimate(
            flops=flops,
            transcendentals=batch * (rows + 2) * chans * cols,
            bytes_accessed=values.size * values.dtype.itemsize + 9 * chans * outs * 2 + batch * rows * outs * cols * 4,
        ),
        name="norm_conv3x3_rows",
    )(*operands)


def conv_valid(rows_in, kernel):
    padded = jnp.pad(rows_in, ((0, 0), (0, 0), (0, 0), (1, 1)))
    height = rows_in.shape[1] - 2
    col_count = rows_in.shape[3]
    accum = jnp.zeros((rows_in.shape[0], height, kernel.shape[1], col_count), jnp.float32)
    for tap_no in range(9):
        row_off, col_off = (tap_no // 3, tap_no % 3)
        window = padded[:, row_off : row_off + height, :, col_off : col_off + col_count]
        accum = accum + jnp.einsum(
            "oi,bhiw->bhow", kernel[tap_no], window, preferred_element_type=jnp.float32
        )
    return accum


def resnet_unit(hidden, conv1_w, conv2_w, block, params):
    moments, low, high = group_moments(hidden.astype(jnp.float32), hidden)
    middle = norm_conv(hidden, moments, low, high, params, 0, conv1_w, block)
    moments, low, high = group_moments(middle, middle)
    return norm_conv(middle, moments, low, high, params, 1, conv2_w, block, residual=hidden)


def head_noise(source, head_w, head_params):
    moments, low, high = group_moments(source.astype(jnp.float32), source)
    noise = norm_conv(source, moments, low, high, head_params, 0, head_w[None, None], 0)
    return jnp.transpose(noise, (0, 2, 1, 3))


def conv_stacked(rows_in, kernel):
    padded = jnp.pad(rows_in, ((0, 0), (0, 0), (0, 0), (1, 1)))
    height = rows_in.shape[1] - 2
    col_count = rows_in.shape[3]
    windows = jnp.concatenate(
        [
            padded[:, tap // 3 : tap // 3 + height, :, tap % 3 : tap % 3 + col_count]
            for tap in range(9)
        ],
        axis=2,
    )
    flat = jnp.transpose(kernel, (1, 0, 2)).reshape(kernel.shape[1], -1)
    return jnp.einsum("ok,bhkw->bhow", flat, windows, preferred_element_type=jnp.float32)


def conv_taps_after(rows_in, kernel):
    batch, rows_halo, chans, cols = rows_in.shape
    height = rows_halo - 2
    outs = kernel.shape[1]
    stacked = kernel.reshape(9 * outs, chans)
    partial = jnp.einsum("kc,bhcw->bhkw", stacked, rows_in, preferred_element_type=jnp.float32)
    partial = jnp.pad(partial, ((0, 0), (0, 0), (0, 0), (1, 1)))
    accum = jnp.zeros((batch, height, outs, cols), jnp.float32)
    for tap in range(9):
        row_off, col_off = (tap // 3, tap % 3)
        accum = accum + partial[
            :, row_off : row_off + height, tap * outs : (tap + 1) * outs, col_off : col_off + cols
        ]
    return accum


def with_rows(values):
    return with_halo(values, (("patch", 1),), 1)


def per_device(
    features,
    latent,
    plan_pos,
    blocks_used,
    conv1_w,
    conv2_w,
    norm_gain,
    norm_shift,
    in_w,
    head_w,
    head_gain,
    head_shift,
):
    segment_count = lax.axis_size("segment")
    segment_pos = lax.axis_index("segment")
    last = segment_count - 1
    current = jnp.transpose(features[0], (0, 2, 1, 3))
    head_params = jnp.broadcast_to(
        jnp.stack([head_gain, head_shift])[None, None, :, :, None],
        (1, 1, 2, head_gain.shape[0], features.shape[4]),
    )
    params = jnp.broadcast_to(
        jnp.stack([norm_gain[0], norm_shift[0]], axis=2)[..., None],
        norm_gain.shape[1:3] + (2, norm_gain.shape[3], features.shape[4]),
    )
    for step_no in range(STEPS):
        arrived = from_behind(current, "segment", 1)
        noise_local = lax.cond(
            segment_pos == last,
            lambda source: head_noise(source, head_w, head_params),
            lambda source: jnp.zeros(latent.shape, jnp.float32),
            current,
        )
        position = plan_pos + step_no
        sigma_now = sigma_at(position)
        sigma_next = sigma_at(position + 1)
        latent = latent + (sigma_next - sigma_now)[:, None, None, None] * noise_local
        scaled = (latent / jnp.sqrt(sigma_next * sigma_next + 1.0)[:, None, None, None]).astype(
            jnp.bfloat16
        )
        scaled_rows = jnp.transpose(scaled, (0, 2, 1, 3))
        peers = lax.axis_size("patch")
        origin = last * peers
        height = scaled_rows.shape[1]
        body = lax.ppermute(
            scaled_rows, ("segment", "patch"), [(origin + p, p) for p in range(peers)]
        )
        above = lax.ppermute(
            scaled_rows[:, height - 1 :],
            ("segment", "patch"),
            [(origin + p, p + 1) for p in range(peers - 1)],
        )
        below = lax.ppermute(
            scaled_rows[:, :1], ("segment", "patch"), [(origin + p, p - 1) for p in range(1, peers)]
        )
        entry_rows = conv_stacked(
            jnp.concatenate([above, body, below], axis=1), in_w
        ).astype(jnp.bfloat16)
        source = jnp.where(segment_pos == 0, entry_rows, arrived)
        after_one = resnet_unit(source, conv1_w, conv2_w, 0, params)
        current = lax.cond(
            blocks_used[0] >= 2,
            lambda hidden: resnet_unit(hidden, conv1_w, conv2_w, 1, params),
            lambda hidden: hidden,
            after_one,
        )
    batch_size, lat_count, height, col_count = latent.shape
    col_share = col_count // segment_count
    latent, current = lax.optimization_barrier((latent, current))
    pieces = latent.reshape(batch_size, lat_count, height, segment_count, col_share)
    pieces = jnp.transpose(pieces, (3, 0, 1, 2, 4)).reshape(segment_count, -1, 128)
    latent_part = scatter_from_last(pieces).reshape(batch_size, lat_count, height, col_share)
    return (latent_part, jnp.transpose(current, (0, 2, 1, 3))[None])


def solution(mesh):
    placed = (
        P("segment", None, None, "patch", None),
        P(None, None, "patch", None),
        P(),
        P("segment"),
        P("segment", None, None, None, None),
        P("segment", None, None, None, None),
        P("segment", None, None, None),
        P("segment", None, None, None),
        P(),
        P(),
        P(),
        P(),
    )
    return jax.shard_map(
        per_device,
        mesh=mesh,
        in_specs=placed,
        out_specs=(P(None, None, "patch", "segment"), P("segment", None, None, "patch", None)),
        check_vma=False,
    )
```
